32 devices in a mesh: wave: 8 (over z, y), lev: 4 (over x, core).
Axes of the slice: x: 2, y: 2, z: 4, core: 2. Of those that a mesh axis runs over, the one named last changes fastest.
Arguments:
- fine_state: float32 [8, 3, 2, 24, 49], P('lev', None, None, 'wave'), may hold values from -6 to 6
- fold_pairs: int32 [24], replicated, may hold values from 0 to 23, each once
- legendre: bfloat16 [24, 96, 49], P('wave', 'lev'), may hold values from -0.875 to 0.875
- gauss_weights: float32 [96], P('lev'), may hold values from 0.5 to 3
- grid_coef: float32 [8, 2560], replicated, may hold values from -4 to 4
- modes_from: float32 [8, 8], replicated
- modes_to: float32 [8, 8], replicated, as said below
- mode_rates: float32 [8], replicated, may hold values from 0.2 to 20
Outputs:
- corrected: float32 [8, 2, 2, 24, 49], P('lev', None, None, 'wave')
- fine_tend: float32 [8, 3, 2, 24, 49], P('lev', None, None, 'wave')
The draws below stay inside these ranges and needn't reach their ends.
Inputs may be any that keep to these rules, and one draw needn't show every extreme that they name: Slot p holds zonal wavenumbers fold_pairs[p] and 47 - fold_pairs[p]; every value occurs once. modes_to is the inverse of modes_from.
All inputs are finite; a program needn't handle non-finite values.
Results may differ from the reference program's by a relative error of at most 0.02.
Values may be sent and summed in bfloat16 or wider, within the bound.
No kernel may reach another device: no remote copies, remote signals or barrier semaphores. Data moves between devices by JAX's collectives and lax.ppermute only.
A program may use at most 64 MiB of HBM per device.

```python
import math
import jax
import jax.numpy as jnp
from jax import lax

NLON = 2560
LEV = 8
NODES = 3
WAVES = 48
LAT = 96
ROWS = 49
PAIRS = 24
NC = 24


def vertical_pair(key):
    base_key = jax.random.fold_in(key, 71)
    noise_draw = jax.random.normal(base_key, (LEV, LEV), jnp.float32)
    eigen_basis = jnp.eye(LEV, dtype=jnp.float32) + 0.5 * noise_draw / math.sqrt(LEV)
    return (eigen_basis, jnp.linalg.inv(eigen_basis))


def draw_modes_from(key, part):
    return vertical_pair(key)[0]


def draw_modes_to(key, part):
    return vertical_pair(key)[1]


def block_scale(key, shape, cuts, least, high):
    def one(dim, parts):
        heights = jax.random.uniform(jax.random.fold_in(jax.random.fold_in(key, 6), dim), (parts,), jnp.float32, least / len(cuts), high / len(cuts))
        return jnp.repeat(jnp.exp(heights), shape[dim] // parts).reshape((-1,) + (1,) * (len(shape) - dim - 1))

    gain = one(*cuts[0])
    for cut in cuts[1:]:
        gain = gain * one(*cut)
    return gain


def scatter_about(own_key, extent, scale, limit, shards=(), held_as=jnp.bfloat16):
    level = block_scale(own_key, extent, shards, -0.22, 0.18) if shards else 1.0
    drawn = jax.random.normal(own_key, extent, jnp.float32) * scale * level
    return jnp.minimum(jnp.maximum(drawn, -limit), limit).astype(held_as)


def setup_inputs(seed: int = 0) -> dict:
    key_of = jax.random.split(jax.random.key(seed), 9)
    return {
        "fine_state": scatter_about(key_of[0], (LEV, NODES, 2, PAIRS, ROWS), 1.0, 6.0, ((0, 4), (3, 8)), jnp.float32),
        "fold_pairs": jax.random.permutation(key_of[1], PAIRS).astype(jnp.int32),
        "legendre": scatter_about(key_of[2], (PAIRS, LAT, ROWS), ROWS ** -0.5, 0.875, ((0, 8), (1, 4))),
        "gauss_weights": jnp.clip(jnp.exp(math.log(3.0) - 1.7917595 * jax.random.uniform(key_of[3], (LAT,), jnp.float32) ** block_scale(key_of[3], (LAT,), ((0, 4),), -0.2, 0.2)), 0.5, 3.0),
        "grid_coef": jnp.clip(jax.random.uniform(key_of[4], (LEV, NLON), jnp.float32, -4.0, 4.0), -4.0, 4.0),
        "modes_from": draw_modes_from(jax.random.fold_in(key_of[8], 71), 0),
        "modes_to": draw_modes_to(jax.random.fold_in(key_of[8], 71), 0),
        "mode_rates": jnp.clip(jnp.exp(jax.random.uniform(key_of[7], (LEV,), jnp.float32, math.log(0.2), math.log(20.0))), 0.2, 20.0),
    }


STEP_HALF = 0.5
quad_weights = ((5.0 / 24.0, 1.0 / 3.0, -1.0 / 24.0), (-1.0 / 24.0, 1.0 / 3.0, 5.0 / 24.0))
HIGHEST = lax.Precision.HIGHEST

def fourier_table(waves, points, amplitude):
    steps = jnp.arange(points, dtype=jnp.int32)
    turns = waves[:, :, None] * steps[None, None, :] % points
    angles = turns.astype(jnp.float32) * (2.0 * math.pi / points)
    return jnp.stack([jnp.cos(angles) * amplitude, -jnp.sin(angles) * amplitude]).astype(jnp.bfloat16)

def fine_rows(small_wave, fine_width):
    row_ids = jnp.arange(fine_width + 1, dtype=jnp.int32)[None, :]
    return row_ids < fine_width - small_wave[:, None]

def coarse_rows(small_wave, coarse):
    row_ids = jnp.arange(coarse, dtype=jnp.int32)[None, :]
    coarse_keep = row_ids < coarse - small_wave[:, None]
    degree = (small_wave[:, None] + row_ids).astype(jnp.float32)
    return (coarse_keep, degree)

def pair_blocks(values, which_axis):
    leading = jnp.moveaxis(values, which_axis, 0)
    block_size = math.gcd(leading.shape[0], 16)
    return leading.reshape((leading.shape[0] // block_size, block_size) + leading.shape[1:])

def unblock(values, which_axis):
    flattened = values.reshape((values.shape[0] * values.shape[1],) + values.shape[2:])
    return jnp.moveaxis(flattened, 0, which_axis)

def legendre_inverse(spectral, legendre_table, row_mask):

    def block_step(items):
        spec_block, table_block, mask_block = items
        split_spec = spec_block.astype(jnp.float32)[:, :, :, :, None, :] * mask_block.astype(jnp.float32)[:, None, None, None, :, :]
        return jnp.einsum('pabcmr,plr->pabcml', split_spec, table_block.astype(jnp.float32), precision=HIGHEST).astype(jnp.bfloat16)
    mapped = lax.map(block_step, (pair_blocks(spectral, 3), pair_blocks(legendre_table, 0), pair_blocks(row_mask, 0)))
    return unblock(mapped, 3)

def legendre_forward(returned, legendre_table, row_mask):

    def block_step(items):
        back_block, table_block, mask_block = items
        members = jnp.einsum('pabcml,plr->pabcmr', back_block.astype(jnp.float32), table_block.astype(jnp.float32), precision=HIGHEST)
        return jnp.sum(members * mask_block.astype(jnp.float32)[:, None, None, None, :, :], axis=4)
    mapped = lax.map(block_step, (pair_blocks(returned, 3), pair_blocks(legendre_table, 0), pair_blocks(row_mask, 0)))
    return unblock(mapped, 3)

def grid_step(fourier, wave_table, coef, weights, factor):
    grid_field = jnp.einsum('abcpmz,cpmk->abzk', fourier.astype(jnp.float32), wave_table.astype(jnp.float32), precision=HIGHEST)
    product = (coef[:, None, None, :] * grid_field * grid_field).astype(jnp.bfloat16)
    returned = jnp.einsum('abzk,cpmk->abcpmz', product.astype(jnp.float32), wave_table.astype(jnp.float32), precision=HIGHEST)
    return (returned * (weights * factor)).astype(jnp.bfloat16)

def mix(matrix, values):
    return jnp.einsum('ql,lbcpr->qbcpr', matrix, values, precision=HIGHEST)

def reference(fine_state, fold_pairs, legendre, gauss_weights, grid_coef, modes_from, modes_to, mode_rates):
    first_member = fine_rows(fold_pairs, WAVES)
    member_mask = jnp.stack([first_member, jnp.logical_not(first_member)], 1).astype(jnp.bfloat16)
    coarse_keep, degree = coarse_rows(fold_pairs, NC)
    keep_mask = coarse_keep[:, None, :].astype(jnp.bfloat16)
    keep_float = coarse_keep.astype(jnp.float32)
    fine_table = fourier_table(jnp.stack([fold_pairs, WAVES - 1 - fold_pairs], 1), NLON, WAVES ** (-0.5))
    coarse_table = fourier_table(fold_pairs[:, None], NLON // 2, NC ** (-0.5))
    coarse_leg = legendre[:, :, :NC]
    coarse_coef = grid_coef[:, ::2]
    fine_fourier = legendre_inverse(fine_state.astype(jnp.bfloat16), legendre, member_mask)
    fine_back = grid_step(fine_fourier, fine_table, grid_coef, gauss_weights, 2.0 * WAVES / NLON)
    fine_tend = legendre_forward(fine_back, legendre, member_mask)

    def coarse_eval(modes):
        levels = (mix(modes_from, modes) * keep_float).astype(jnp.bfloat16)
        coarse_fourier = legendre_inverse(levels, coarse_leg, keep_mask)
        coarse_back = grid_step(coarse_fourier, coarse_table, coarse_coef, gauss_weights, 2.0 * NC / (NLON // 2))
        return mix(modes_to, legendre_forward(coarse_back, coarse_leg, keep_mask))
    old_state = mix(modes_to, fine_state[..., :NC] * keep_float)
    old_tend = mix(modes_to, fine_tend[..., :NC] * keep_float)
    old_coarse = coarse_eval(old_state[:, 1:2])
    stiffness = mode_rates[:, None, None, None] * (degree * (degree + 1.0) / (NC * (NC + 1.0)))[None, None]
    source = old_tend - stiffness[:, None] * old_state
    integral_mid = quad_weights[0][0] * source[:, 0] + quad_weights[0][1] * source[:, 1] + quad_weights[0][2] * source[:, 2]
    integral_end = quad_weights[1][0] * source[:, 0] + quad_weights[1][1] * source[:, 1] + quad_weights[1][2] * source[:, 2]
    divisor = 1.0 + STEP_HALF * stiffness
    next_mid = (old_state[:, 0] + STEP_HALF * stiffness * old_state[:, 1] + integral_mid) / divisor
    coarse_fresh = coarse_eval(next_mid[:, None])
    next_end = (next_mid + STEP_HALF * (coarse_fresh[:, 0] - old_coarse[:, 0]) + STEP_HALF * stiffness * old_state[:, 2] + integral_end) / divisor
    change = jnp.stack([next_mid - old_state[:, 1], next_end - old_state[:, 2]], 1)
    lifted = mix(modes_from, change)
    corrected = fine_state[:, 1:] + jnp.pad(lifted, ((0, 0), (0, 0), (0, 0), (0, 0), (0, ROWS - NC)))
    return (corrected, fine_tend)
```

```python
import functools
import math

import jax
import jax.numpy as jnp
import numpy as np
from jax import lax
from jax.experimental import pallas as pl
from jax.experimental.pallas import tpu as pltpu
from jax.sharding import PartitionSpec as P

STEP_HALF = 0.5
quad_weights = ((5.0 / 24.0, 1.0 / 3.0, -1.0 / 24.0), (-1.0 / 24.0, 1.0 / 3.0, 5.0 / 24.0))
HIGHEST = lax.Precision.HIGHEST


def fourier_table(waves, points, amplitude):
    steps = jnp.arange(points, dtype=jnp.int32)
    turns = waves[:, :, None] * steps[None, None, :] % points
    angles = turns.astype(jnp.float32) * (2.0 * math.pi / points)
    return jnp.stack([jnp.cos(angles) * amplitude, -jnp.sin(angles) * amplitude]).astype(
        jnp.bfloat16
    )


def fine_rows(small_wave, fine_width):
    row_ids = jnp.arange(fine_width + 1, dtype=jnp.int32)[None, :]
    return row_ids < fine_width - small_wave[:, None]


def coarse_rows(small_wave, coarse):
    row_ids = jnp.arange(coarse, dtype=jnp.int32)[None, :]
    coarse_keep = row_ids < coarse - small_wave[:, None]
    degree = (small_wave[:, None] + row_ids).astype(jnp.float32)
    return (coarse_keep, degree)


def legendre_inverse(spectral, legendre_table, row_mask):
    split_spec = spectral[:, :, :, :, None, :] * row_mask[None, None, None]
    return jnp.einsum(
        "abcpmr,plr->abcpml", split_spec, legendre_table, preferred_element_type=jnp.float32
    ).astype(jnp.bfloat16)


def legendre_forward(returned, legendre_table, row_mask):
    members = jnp.einsum(
        "abcpml,plr->abcpmr", returned, legendre_table, preferred_element_type=jnp.float32
    )
    return jnp.sum(members * row_mask.astype(jnp.float32)[None, None, None], axis=4)


def grid_step(fourier, wave_table, coef, weights, factor):
    grid_field = jnp.einsum(
        "abcpmz,cpmk->abzk", fourier, wave_table, preferred_element_type=jnp.float32
    )
    product = (coef[:, None, None, :] * grid_field * grid_field).astype(jnp.bfloat16)
    returned = jnp.einsum(
        "abzk,cpmk->abcpmz", product, wave_table, preferred_element_type=jnp.float32
    )
    return (returned * (weights * factor)).astype(jnp.bfloat16)


def mix(matrix, values):
    return jnp.einsum("ql,lbcpr->qbcpr", matrix, values, precision=HIGHEST)


def split_plan(
    fine_state, fold_pairs, legendre, gauss_weights, grid_coef, modes_from, modes_to, mode_rates
):
    n_wave = lax.axis_size("wave")
    wave_idx = lax.axis_index("wave")
    lev_idx = lax.axis_index("lev")
    lev_dev = fine_state.shape[0]
    pairs_dev = fine_state.shape[3]
    fine_width = fine_state.shape[4] - 1
    coarse = fine_width // 2
    longitudes = grid_coef.shape[1]
    band_size = legendre.shape[1] // n_wave
    small_wave = lax.dynamic_slice_in_dim(fold_pairs, wave_idx * pairs_dev, pairs_dev)
    first_member = fine_rows(small_wave, fine_width)
    member_mask = jnp.stack([first_member, jnp.logical_not(first_member)], 1).astype(jnp.bfloat16)
    coarse_keep, degree = coarse_rows(small_wave, coarse)
    keep_mask = coarse_keep[:, None, :].astype(jnp.bfloat16)
    keep_float = coarse_keep.astype(jnp.float32)
    fine_table = fourier_table(
        jnp.stack([fold_pairs, fine_width - 1 - fold_pairs], 1), longitudes, fine_width ** (-0.5)
    )
    coarse_table = fourier_table(fold_pairs[:, None], longitudes // 2, coarse ** (-0.5))
    coarse_leg = legendre[:, :, :coarse]
    coarse_coef = grid_coef[:, ::2]
    band_gauss = lax.dynamic_slice_in_dim(gauss_weights, wave_idx * band_size, band_size)
    local_to = lax.dynamic_slice_in_dim(modes_to, lev_idx * lev_dev, lev_dev, 1)
    local_from = lax.dynamic_slice_in_dim(modes_from, lev_idx * lev_dev, lev_dev, 1)
    mode_decay = lax.dynamic_slice_in_dim(mode_rates, lev_idx * lev_dev, lev_dev)

    def project(partial_sum):
        return mix(modes_to, partial_sum)

    def coarse_start(modes):
        gathered = lax.all_gather(modes, "lev", axis=0, tiled=True)
        levels = (mix(modes_from, gathered) * keep_float).astype(jnp.bfloat16)
        return legendre_inverse(levels, coarse_leg, keep_mask)

    def coarse_grid_step(fourier):
        return grid_step(
            fourier, coarse_table, coarse_coef, band_gauss, 2.0 * coarse / (longitudes // 2)
        )

    def coarse_finish(returned):
        partial_sum = legendre_forward(returned, coarse_leg, keep_mask)
        return lax.psum_scatter(
            project(partial_sum).astype(jnp.bfloat16), "lev", scatter_dimension=0, tiled=True
        ).astype(jnp.float32)

    def coarse_eval(modes):
        fourier = lax.all_to_all(
            coarse_start(modes), "wave", split_axis=5, concat_axis=3, tiled=True
        )
        returned = lax.all_to_all(
            coarse_grid_step(fourier), "wave", split_axis=3, concat_axis=5, tiled=True
        )
        return coarse_finish(returned)

    restricted = fine_state[..., :coarse] * keep_float
    fine_spec = lax.all_gather(fine_state.astype(jnp.bfloat16), "lev", axis=0, tiled=True)
    fine_fourier = legendre_inverse(fine_spec, legendre, member_mask)
    fine_fourier = lax.all_to_all(fine_fourier, "wave", split_axis=5, concat_axis=3, tiled=True)
    fine_back = lax.all_to_all(
        grid_step(fine_fourier, fine_table, grid_coef, band_gauss, 2.0 * fine_width / longitudes),
        "wave",
        split_axis=3,
        concat_axis=5,
        tiled=True,
    )
    fine_tend = lax.psum_scatter(
        legendre_forward(fine_back, legendre, member_mask).astype(jnp.bfloat16),
        "lev",
        scatter_dimension=0,
        tiled=True,
    ).astype(jnp.float32)
    restricted_tend = fine_tend[..., :coarse] * keep_float
    stacked = jnp.concatenate([restricted, restricted_tend], 1)
    both_modes = lax.psum_scatter(
        mix(local_to, stacked).astype(jnp.bfloat16), "lev", scatter_dimension=0, tiled=True
    ).astype(jnp.float32)
    nodes = fine_state.shape[1]
    old_state = both_modes[:, :nodes]
    old_tend = both_modes[:, nodes:]
    old_coarse = coarse_eval(old_state[:, 1:2])
    stiffness = (
        mode_decay[:, None, None, None]
        * (degree * (degree + 1.0) / (coarse * (coarse + 1.0)))[None, None]
    )
    source = old_tend - stiffness[:, None] * old_state
    integral_mid = (
        quad_weights[0][0] * source[:, 0]
        + quad_weights[0][1] * source[:, 1]
        + quad_weights[0][2] * source[:, 2]
    )
    integral_end = (
        quad_weights[1][0] * source[:, 0]
        + quad_weights[1][1] * source[:, 1]
        + quad_weights[1][2] * source[:, 2]
    )
    divisor = 1.0 + STEP_HALF * stiffness
    next_mid = (old_state[:, 0] + STEP_HALF * stiffness * old_state[:, 1] + integral_mid) / divisor
    coarse_fresh = coarse_eval(next_mid[:, None])
    next_end = (
        next_mid
        + STEP_HALF * (coarse_fresh[:, 0] - old_coarse[:, 0])
        + STEP_HALF * stiffness * old_state[:, 2]
        + integral_end
    ) / divisor
    change = jnp.stack([next_mid - old_state[:, 1], next_end - old_state[:, 2]], 1)
    lifted = lax.psum_scatter(
        mix(local_from, change).astype(jnp.bfloat16), "lev", scatter_dimension=0, tiled=True
    ).astype(jnp.float32)
    corrected = fine_state[:, 1:] + jnp.pad(
        lifted, ((0, 0), (0, 0), (0, 0), (0, 0), (0, fine_width + 1 - coarse))
    )
    return (corrected, fine_tend)


LANES = 128
REPLICATED_BYTES = 16 * 2**20


def round_up(value, unit):
    return -(-value // unit) * unit


def interpolation(points, targets, degree):
    offset = (
        2.0 * np.pi * (np.arange(targets)[:, None] / targets - np.arange(points)[None, :] / points)
    )
    order = np.arange(1, degree + 1)
    return (1.0 + 2.0 * np.cos(offset[:, :, None] * order).sum(-1)) / points


def wave_rows(waves, points, amplitude):
    turns = np.arange(waves)[:, None] * np.arange(points)[None, :] % points
    angles = turns * (2.0 * np.pi / points)
    return np.concatenate([np.cos(angles), -np.sin(angles)]) * amplitude


def rows_of(column_waves, valid, waves):
    hot = (column_waves[:, None] == jnp.arange(waves)[None, :]) & valid[:, None]
    zero = jnp.zeros_like(hot)
    return jnp.concatenate(
        [jnp.concatenate([hot, zero], 1), jnp.concatenate([zero, hot], 1)]
    ).astype(jnp.bfloat16)


def matmul(a, b):
    return jnp.dot(a, b, preferred_element_type=jnp.float32)


def matmul_nt(a, b):
    return lax.dot_general(a, b, (((1,), (1,)), ((), ())), preferred_element_type=jnp.float32)


def matmul_exact(a, b):
    return jnp.dot(a, b, preferred_element_type=jnp.float32, precision=lax.Precision.HIGHEST)


def sweep_kernel(
    size,
    place_ref,
    fold_ref,
    own_ref,
    other_ref,
    wave_ref,
    quad_ref,
    coarse_wave_ref,
    coarse_quad_ref,
    mix_to_ref,
    mix_from_ref,
    mix_back_ref,
    lift_ref,
    rate_ref,
    tend_ref,
    lifted_ref,
    leg_s,
    state_s,
    fourier_s,
    back_s,
    tend_s,
    coarse_s,
    coarse_back_s,
    change_s,
):
    (n_wave, n_pair, lev_dev, nodes, slots, fine_width, coarse, lats) = size
    n_lev = 2 * n_pair
    levels = n_lev * lev_dev
    dev_rows = lev_dev * nodes * 2
    rows = levels * nodes * 2
    all_lats = n_lev * lats
    wide = leg_s.shape[2]
    fine_columns = n_wave * slots * 2
    coarse_columns = n_wave * slots
    lane = lax.broadcasted_iota(jnp.int32, (1, wide), 1)
    head = slots * coarse
    rest = fine_width + 1 - coarse
    lane_slot = jnp.full((1, wide), -1, jnp.int32)
    lane_row = jnp.zeros((1, wide), jnp.int32)
    for s in range(slots):
        inside = (lane >= s * coarse) & (lane < (s + 1) * coarse)
        lane_slot = jnp.where(inside, s, lane_slot)
        lane_row = jnp.where(inside, lane - s * coarse, lane_row)
        begin = head + s * rest
        inside = (lane >= begin) & (lane < begin + rest)
        lane_slot = jnp.where(inside, s, lane_slot)
        lane_row = jnp.where(inside, lane - begin + coarse, lane_row)

    def lane_wave(w):
        value = jnp.zeros((1, wide), jnp.int32)
        for s in range(slots):
            value = jnp.where(lane_slot == s, fold_ref[w * slots + s], value)
        return value

    member_masks, slot_masks, keeps, stiffs = [], [], [], []
    for w in range(n_wave):
        small = lane_wave(w)
        first = lane_row < fine_width - small
        masks = []
        for s in range(slots):
            own_slot = lane_slot == s
            masks.append((own_slot & first).astype(jnp.float32))
            masks.append((own_slot & jnp.logical_not(first)).astype(jnp.float32))
        member_masks.append(masks)
        in_coarse = (lane < head) & (lane_row < coarse - small)
        keep = in_coarse[:, :LANES].astype(jnp.float32)
        keeps.append(keep)
        slot_masks.append([keep * (lane_slot[:, :LANES] == s).astype(jnp.float32) for s in range(slots)])
        degree = (small + lane_row)[:, :LANES].astype(jnp.float32)
        stiffs.append(rate_ref[...] * (degree * (degree + 1.0) / (coarse * (coarse + 1.0))))

    weights_lane = slots * (fine_width + 1)
    for w in range(n_wave):
        for x in range(n_pair):
            for o, ref in enumerate((own_ref, other_ref)):
                d = 2 * x + o
                block = ref[w * n_pair + x].astype(jnp.float32)
                leg_s[w, d * lats : (d + 1) * lats, :] = block[:lats]
                state_s[w, d * dev_rows : (d + 1) * dev_rows, :] = block[lats : lats + dev_rows]
        if all_lats < leg_s.shape[1]:
            leg_s[w, all_lats:, :] = jnp.zeros((leg_s.shape[1] - all_lats, wide), jnp.float32)

    def legendre(w):
        return leg_s[w].astype(jnp.bfloat16)

    def weighted(w):
        table = leg_s[w]
        column = table[:, weights_lane : weights_lane + 1] + table[:, weights_lane + 1 : weights_lane + 2]
        return (table * column).astype(jnp.bfloat16)

    for w in range(n_wave):
        state = state_s[w]
        left = jnp.concatenate([state * mask for mask in member_masks[w]], 0).astype(jnp.bfloat16)
        out = matmul_nt(left, legendre(w))
        for j in range(2 * slots):
            fourier_s[pl.ds(w * 2 * slots + j, rows, stride=fine_columns), :] = out[j * rows : (j + 1) * rows]

    both = 2 * fine_columns
    for a in range(levels):
        pieces = [
            fourier_s[(a * nodes + b) * both : (a * nodes + b + 1) * both, :].astype(jnp.bfloat16)
            for b in range(nodes)
        ]
        grid = matmul(wave_ref[...], jnp.concatenate(pieces, 1))
        product = (grid * grid).astype(jnp.bfloat16)
        back = matmul(quad_ref[a], product)
        for b in range(nodes):
            back_s[(a * nodes + b) * both : (a * nodes + b + 1) * both, :] = back[:, b * LANES : (b + 1) * LANES]

    stacked = []
    for w in range(n_wave):
        left = jnp.concatenate(
            [
                back_s[pl.ds(w * 2 * slots + j, rows, stride=fine_columns), :].astype(jnp.bfloat16)
                for j in range(2 * slots)
            ],
            0,
        )
        out = matmul(left, weighted(w))
        total = member_masks[w][0] * out[:rows]
        for j in range(1, 2 * slots):
            total = total + member_masks[w][j] * out[j * rows : (j + 1) * rows]
        tend_s[w] = total
        stacked.append(state_s[w][:, :LANES] * keeps[w])
        stacked.append(total[:, :LANES] * keeps[w])
    place = place_ref[0]
    begin = pl.multiple_of(place_ref[1] * (2 * dev_rows), 8)
    tend_ref[...] = tend_s[place, pl.ds(begin, dev_rows), :]

    modes = matmul_exact(mix_to_ref[...], jnp.concatenate(stacked, 1))
    per_node = levels * 2
    evals, later, old_of, mid_of = [], [], [], []
    for w in range(n_wave):
        old, source = [], []
        stiff = stiffs[w]
        for b in range(nodes):
            part = modes[b * per_node : (b + 1) * per_node]
            old.append(part[:, 2 * w * LANES : (2 * w + 1) * LANES])
            source.append(part[:, (2 * w + 1) * LANES : (2 * w + 2) * LANES] - stiff * old[-1])
        divisor = 1.0 + STEP_HALF * stiff
        mid = sum(quad_weights[0][b] * source[b] for b in range(nodes))
        mid = (mid + old[0] + STEP_HALF * stiff * old[1]) / divisor
        end = sum(quad_weights[1][b] * source[b] for b in range(nodes))
        end = end + mid + STEP_HALF * stiff * old[2]
        evals.append(old[1])
        evals.append(mid)
        later.append((end, divisor))
        old_of.append(old)
        mid_of.append(mid)

    level_values = matmul_exact(mix_from_ref[...], jnp.concatenate(evals, 1))
    for w in range(n_wave):
        left = jnp.concatenate(
            [
                level_values[:, (2 * w + e) * LANES : (2 * w + e + 1) * LANES] * slot_masks[w][s]
                for s in range(slots)
                for e in range(2)
            ],
            0,
        ).astype(jnp.bfloat16)
        out = matmul_nt(left, legendre(w)[:, :LANES])
        for s in range(slots):
            for e in range(2):
                at = (s * 2 + e) * per_node
                coarse_s[e, pl.ds(w * slots + s, per_node, stride=coarse_columns), :] = out[at : at + per_node]

    both_c = 2 * coarse_columns
    for a in range(levels):
        pieces = [coarse_s[e, a * both_c : (a + 1) * both_c, :].astype(jnp.bfloat16) for e in range(2)]
        grid = matmul(coarse_wave_ref[...], jnp.concatenate(pieces, 1))
        product = (grid * grid).astype(jnp.bfloat16)
        back = matmul(coarse_quad_ref[a], product)
        for e in range(2):
            coarse_back_s[e, a * both_c : (a + 1) * both_c, :] = back[:, e * LANES : (e + 1) * LANES]

    tends = []
    for w in range(n_wave):
        left = jnp.concatenate(
            [
                coarse_back_s[e, pl.ds(w * slots + s, per_node, stride=coarse_columns), :].astype(jnp.bfloat16)
                for s in range(slots)
                for e in range(2)
            ],
            0,
        )
        out = matmul(left, weighted(w)[:, :LANES])
        for e in range(2):
            total = None
            for s in range(slots):
                at = (s * 2 + e) * per_node
                term = slot_masks[w][s] * out[at : at + per_node]
                total = term if total is None else total + term
            tends.append(total)
    coarse_modes = matmul_exact(mix_back_ref[...], jnp.concatenate(tends, 1))
    for w in range(n_wave):
        before = coarse_modes[:, 2 * w * LANES : (2 * w + 1) * LANES]
        fresh = coarse_modes[:, (2 * w + 1) * LANES : (2 * w + 2) * LANES]
        end, divisor = later[w]
        end = (end + STEP_HALF * (fresh - before)) / divisor
        change_s[w, :per_node, :] = mid_of[w] - old_of[w][1]
        change_s[w, per_node:, :] = end - old_of[w][2]
    lifted_ref[...] = matmul_exact(lift_ref[...], change_s[place])


def replicated_plan(
    fine_state, fold_pairs, legendre, gauss_weights, grid_coef, modes_from, modes_to, mode_rates
):
    n_wave = lax.axis_size("wave")
    n_lev = lax.axis_size("lev")
    wave_idx = lax.axis_index("wave")
    lev_idx = lax.axis_index("lev")
    n_pair = n_lev // 2
    core = lev_idx % 2
    lev_dev, nodes, _, slots, fine_rows_count = fine_state.shape
    fine_width = fine_rows_count - 1
    coarse = fine_width // 2
    lats = legendre.shape[1]
    levels = lev_dev * n_lev
    longitudes = grid_coef.shape[1]
    head, rest = slots * coarse, slots * (fine_rows_count - coarse)
    dev_rows = lev_dev * nodes * 2
    wide = round_up(head + rest + 2, LANES)
    block_rows = round_up(lats + dev_rows, 8)
    bf = jnp.bfloat16

    def lanes_first(values):
        flat = values.shape[:-2]
        return [
            values[..., :coarse].reshape(flat + (head,)),
            values[..., coarse:].reshape(flat + (rest,)),
        ]

    weight_high = gauss_weights.astype(bf)
    weight_low = (gauss_weights - weight_high.astype(jnp.float32)).astype(bf)
    table = jnp.concatenate(
        lanes_first(jnp.swapaxes(legendre, 0, 1)) + [weight_high[:, None], weight_low[:, None]], 1
    )
    state = jnp.concatenate(lanes_first(fine_state.astype(bf).reshape(dev_rows, slots, fine_rows_count)), 1)
    block = jnp.concatenate(
        [
            jnp.pad(table, ((0, 0), (0, wide - table.shape[1]))),
            jnp.pad(state, ((0, block_rows - lats - dev_rows), (0, wide - state.shape[1]))),
        ]
    )
    chips = n_wave * n_pair
    groups = [[2 * i + c for i in range(chips)] for c in range(2)]
    own = lax.all_to_all(
        jnp.broadcast_to(block[None], (chips,) + block.shape),
        ("wave", "lev"),
        0,
        0,
        tiled=True,
        axis_index_groups=groups,
    )
    other = lax.ppermute(own, ("wave", "lev"), [(i, i ^ 1) for i in range(2 * chips)])

    points = round_up(4 * (fine_width - 1) + 1, 32)
    coarse_points = round_up(4 * (coarse - 1) + 1, 32)
    fine_amp, coarse_amp = fine_width**-0.5, coarse**-0.5
    small = fold_pairs.reshape(n_wave * slots)
    column_waves = jnp.stack([small, fine_width - 1 - small], 1).reshape(-1)
    hot = rows_of(column_waves, column_waves >= 0, fine_width)
    coarse_hot = rows_of(small, small >= 0, coarse)

    def by_level(values):
        paired = values.reshape(n_pair, 2, lev_dev, -1)
        return jnp.where(core == 1, paired[:, ::-1], paired).reshape(values.shape)

    coef = by_level(grid_coef)

    def tables(waves, amplitude, count, degree, stride, one_hot, factor):
        sampled = jnp.asarray(wave_rows(waves, count, amplitude).T, bf)
        basis = np.zeros((2 * waves, longitudes))
        basis[:, ::stride] = wave_rows(waves, longitudes // stride, amplitude * factor)
        spread = interpolation(count, longitudes, degree)
        scaled = (coef[:, None, :] * jnp.asarray(basis, jnp.float32)[None]).astype(bf)
        quad = jnp.einsum(
            "amk,kj->amj", scaled, jnp.asarray(spread, bf), preferred_element_type=jnp.float32
        ).astype(bf)
        synth = jnp.einsum("jm,cm->jc", sampled, one_hot, preferred_element_type=jnp.float32).astype(bf)
        quad = jnp.einsum("cm,amj->acj", one_hot, quad, preferred_element_type=jnp.float32).astype(bf)
        return synth, quad

    wave_table, quad_table = tables(
        fine_width, fine_amp, points, 2 * (fine_width - 1), 1, hot, 2.0 * fine_width / longitudes
    )
    coarse_wave, coarse_quad = tables(
        coarse, coarse_amp, coarse_points, 2 * (coarse - 1), 2, coarse_hot, 2.0 * coarse / (longitudes // 2)
    )

    to_rows = by_level(modes_to.T).T
    from_rows = by_level(modes_from)
    eye_c, eye_b = jnp.eye(2, dtype=jnp.float32), jnp.eye(nodes, dtype=jnp.float32)
    mix_to = jnp.einsum("qa,bd,ce->bqcade", to_rows, eye_b, eye_c).transpose(0, 1, 2, 3, 4, 5)
    mix_to = mix_to.reshape(nodes * levels * 2, levels * nodes * 2)
    mix_from = jnp.einsum("aq,ce->acqe", from_rows, eye_c).reshape(levels * 2, levels * 2)
    mix_back = jnp.einsum("qa,ce->qcae", to_rows, eye_c).reshape(levels * 2, levels * 2)
    own_from = lax.dynamic_slice_in_dim(modes_from, lev_idx * lev_dev, lev_dev, 0)
    lift = jnp.einsum("aq,bd,ce->abcdqe", own_from, jnp.eye(nodes - 1, dtype=jnp.float32), eye_c)
    lift = lift.reshape(lev_dev * (nodes - 1) * 2, (nodes - 1) * levels * 2)
    rates = jnp.broadcast_to(jnp.repeat(mode_rates, 2)[:, None], (levels * 2, LANES))
    place = jnp.stack([wave_idx, lev_idx // 2]).astype(jnp.int32)

    size = (n_wave, n_pair, lev_dev, nodes, slots, fine_width, coarse, lats)
    vmem = pl.BlockSpec(memory_space=pltpu.VMEM)
    smem = pl.BlockSpec(memory_space=pltpu.SMEM)
    rows = levels * nodes * 2
    lat_rows = round_up(n_lev * lats, LANES)
    f32 = jnp.float32
    tend, lifted = pl.pallas_call(
        functools.partial(sweep_kernel, size),
        out_shape=(
            jax.ShapeDtypeStruct((dev_rows, wide), f32),
            jax.ShapeDtypeStruct((lev_dev * (nodes - 1) * 2, LANES), f32),
        ),
        in_specs=[smem, smem] + [vmem] * 11,
        out_specs=(vmem, vmem),
        scratch_shapes=[
            pltpu.VMEM((n_wave, lat_rows, wide), f32),
            pltpu.VMEM((n_wave, rows, wide), f32),
            pltpu.VMEM((rows * n_wave * slots * 2, lat_rows), f32),
            pltpu.VMEM((rows * n_wave * slots * 2, lat_rows), f32),
            pltpu.VMEM((n_wave, rows, wide), f32),
            pltpu.VMEM((2, levels * 2 * n_wave * slots, lat_rows), f32),
            pltpu.VMEM((2, levels * 2 * n_wave * slots, lat_rows), f32),
            pltpu.VMEM((n_wave, (nodes - 1) * levels * 2, LANES), f32),
        ],
        name="sweep",
    )(
        place,
        fold_pairs,
        own,
        other,
        wave_table,
        quad_table,
        coarse_wave,
        coarse_quad,
        mix_to,
        mix_from,
        mix_back,
        lift,
        rates,
    )

    def slots_last(values, width):
        return values.reshape(values.shape[0], slots, width)

    fine_tend = jnp.concatenate(
        [
            slots_last(tend[:, :head], coarse),
            slots_last(tend[:, head : head + rest], fine_rows_count - coarse),
        ],
        2,
    ).reshape(fine_state.shape)
    raised = lifted[:, :head].reshape(lev_dev, nodes - 1, 2, slots, coarse)
    corrected = fine_state[:, 1:] + jnp.pad(
        raised, ((0, 0), (0, 0), (0, 0), (0, 0), (0, fine_rows_count - coarse))
    )
    return (corrected, fine_tend)


def fits_replicated(fine_state, legendre):
    n_wave, n_lev = lax.axis_size("wave"), lax.axis_size("lev")
    slots, fine_rows_count = fine_state.shape[3:]
    gathered = 4 * n_wave * n_lev * (legendre.size + fine_state.size)
    return (
        n_lev % 2 == 0
        and slots * (fine_rows_count // 2) <= LANES
        and n_lev * legendre.shape[1] <= LANES
        and fine_state.shape[1] == len(quad_weights[0])
        and gathered * 8 <= REPLICATED_BYTES
    )


def per_device(fine_state, fold_pairs, legendre, *rest):
    plan = replicated_plan if fits_replicated(fine_state, legendre) else split_plan
    return plan(fine_state, fold_pairs, legendre, *rest)


def solution(mesh):
    placed = (
        P("lev", None, None, "wave", None),
        P(),
        P("wave", "lev", None),
        P("lev"),
        P(),
        P(),
        P(),
        P(),
    )
    return jax.shard_map(
        per_device,
        mesh=mesh,
        in_specs=placed,
        out_specs=(P("lev", None, None, "wave", None), P("lev", None, None, "wave", None)),
        check_vma=False,
    )
```

```python
import functools
import math

import jax
import jax.numpy as jnp
import numpy as np
from jax import lax
from jax.experimental import pallas as pl
from jax.experimental.pallas import tpu as pltpu
from jax.sharding import PartitionSpec as P

STEP_HALF = 0.5
quad_weights = ((5.0 / 24.0, 1.0 / 3.0, -1.0 / 24.0), (-1.0 / 24.0, 1.0 / 3.0, 5.0 / 24.0))
HIGHEST = lax.Precision.HIGHEST


def fourier_table(waves, points, amplitude):
    steps = jnp.arange(points, dtype=jnp.int32)
    turns = waves[:, :, None] * steps[None, None, :] % points
    angles = turns.astype(jnp.float32) * (2.0 * math.pi / points)
    return jnp.stack([jnp.cos(angles) * amplitude, -jnp.sin(angles) * amplitude]).astype(
        jnp.bfloat16
    )


def fine_rows(small_wave, fine_width):
    row_ids = jnp.arange(fine_width + 1, dtype=jnp.int32)[None, :]
    return row_ids < fine_width - small_wave[:, None]


def coarse_rows(small_wave, coarse):
    row_ids = jnp.arange(coarse, dtype=jnp.int32)[None, :]
    coarse_keep = row_ids < coarse - small_wave[:, None]
    degree = (small_wave[:, None] + row_ids).astype(jnp.float32)
    return (coarse_keep, degree)


def legendre_inverse(spectral, legendre_table, row_mask):
    split_spec = spectral[:, :, :, :, None, :] * row_mask[None, None, None]
    return jnp.einsum(
        "abcpmr,plr->abcpml", split_spec, legendre_table, preferred_element_type=jnp.float32
    ).astype(jnp.bfloat16)


def legendre_forward(returned, legendre_table, row_mask):
    members = jnp.einsum(
        "abcpml,plr->abcpmr", returned, legendre_table, preferred_element_type=jnp.float32
    )
    return jnp.sum(members * row_mask.astype(jnp.float32)[None, None, None], axis=4)


def grid_step(fourier, wave_table, coef, weights, factor):
    grid_field = jnp.einsum(
        "abcpmz,cpmk->abzk", fourier, wave_table, preferred_element_type=jnp.float32
    )
    product = (coef[:, None, None, :] * grid_field * grid_field).astype(jnp.bfloat16)
    returned = jnp.einsum(
        "abzk,cpmk->abcpmz", product, wave_table, preferred_element_type=jnp.float32
    )
    return (returned * (weights * factor)).astype(jnp.bfloat16)


def mix(matrix, values):
    return jnp.einsum("ql,lbcpr->qbcpr", matrix, values, precision=HIGHEST)


def split_plan(
    fine_state, fold_pairs, legendre, gauss_weights, grid_coef, modes_from, modes_to, mode_rates
):
    n_wave = lax.axis_size("wave")
    wave_idx = lax.axis_index("wave")
    lev_idx = lax.axis_index("lev")
    lev_dev = fine_state.shape[0]
    pairs_dev = fine_state.shape[3]
    fine_width = fine_state.shape[4] - 1
    coarse = fine_width // 2
    longitudes = grid_coef.shape[1]
    band_size = legendre.shape[1] // n_wave
    small_wave = lax.dynamic_slice_in_dim(fold_pairs, wave_idx * pairs_dev, pairs_dev)
    first_member = fine_rows(small_wave, fine_width)
    member_mask = jnp.stack([first_member, jnp.logical_not(first_member)], 1).astype(jnp.bfloat16)
    coarse_keep, degree = coarse_rows(small_wave, coarse)
    keep_mask = coarse_keep[:, None, :].astype(jnp.bfloat16)
    keep_float = coarse_keep.astype(jnp.float32)
    fine_table = fourier_table(
        jnp.stack([fold_pairs, fine_width - 1 - fold_pairs], 1), longitudes, fine_width ** (-0.5)
    )
    coarse_table = fourier_table(fold_pairs[:, None], longitudes // 2, coarse ** (-0.5))
    coarse_leg = legendre[:, :, :coarse]
    coarse_coef = grid_coef[:, ::2]
    band_gauss = lax.dynamic_slice_in_dim(gauss_weights, wave_idx * band_size, band_size)
    local_to = lax.dynamic_slice_in_dim(modes_to, lev_idx * lev_dev, lev_dev, 1)
    local_from = lax.dynamic_slice_in_dim(modes_from, lev_idx * lev_dev, lev_dev, 1)
    mode_decay = lax.dynamic_slice_in_dim(mode_rates, lev_idx * lev_dev, lev_dev)

    def project(partial_sum):
        return mix(modes_to, partial_sum)

    def coarse_start(modes):
        gathered = lax.all_gather(modes, "lev", axis=0, tiled=True)
        levels = (mix(modes_from, gathered) * keep_float).astype(jnp.bfloat16)
        return legendre_inverse(levels, coarse_leg, keep_mask)

    def coarse_grid_step(fourier):
        return grid_step(
            fourier, coarse_table, coarse_coef, band_gauss, 2.0 * coarse / (longitudes // 2)
        )

    def coarse_finish(returned):
        partial_sum = legendre_forward(returned, coarse_leg, keep_mask)
        return lax.psum_scatter(
            project(partial_sum).astype(jnp.bfloat16), "lev", scatter_dimension=0, tiled=True
        ).astype(jnp.float32)

    def coarse_eval(modes):
        fourier = lax.all_to_all(
            coarse_start(modes), "wave", split_axis=5, concat_axis=3, tiled=True
        )
        returned = lax.all_to_all(
            coarse_grid_step(fourier), "wave", split_axis=3, concat_axis=5, tiled=True
        )
        return coarse_finish(returned)

    restricted = fine_state[..., :coarse] * keep_float
    fine_spec = lax.all_gather(fine_state.astype(jnp.bfloat16), "lev", axis=0, tiled=True)
    fine_fourier = legendre_inverse(fine_spec, legendre, member_mask)
    fine_fourier = lax.all_to_all(fine_fourier, "wave", split_axis=5, concat_axis=3, tiled=True)
    fine_back = lax.all_to_all(
        grid_step(fine_fourier, fine_table, grid_coef, band_gauss, 2.0 * fine_width / longitudes),
        "wave",
        split_axis=3,
        concat_axis=5,
        tiled=True,
    )
    fine_tend = lax.psum_scatter(
        legendre_forward(fine_back, legendre, member_mask).astype(jnp.bfloat16),
        "lev",
        scatter_dimension=0,
        tiled=True,
    ).astype(jnp.float32)
    restricted_tend = fine_tend[..., :coarse] * keep_float
    stacked = jnp.concatenate([restricted, restricted_tend], 1)
    both_modes = lax.psum_scatter(
        mix(local_to, stacked).astype(jnp.bfloat16), "lev", scatter_dimension=0, tiled=True
    ).astype(jnp.float32)
    nodes = fine_state.shape[1]
    old_state = both_modes[:, :nodes]
    old_tend = both_modes[:, nodes:]
    old_coarse = coarse_eval(old_state[:, 1:2])
    stiffness = (
        mode_decay[:, None, None, None]
        * (degree * (degree + 1.0) / (coarse * (coarse + 1.0)))[None, None]
    )
    source = old_tend - stiffness[:, None] * old_state
    integral_mid = (
        quad_weights[0][0] * source[:, 0]
        + quad_weights[0][1] * source[:, 1]
        + quad_weights[0][2] * source[:, 2]
    )
    integral_end = (
        quad_weights[1][0] * source[:, 0]
        + quad_weights[1][1] * source[:, 1]
        + quad_weights[1][2] * source[:, 2]
    )
    divisor = 1.0 + STEP_HALF * stiffness
    next_mid = (old_state[:, 0] + STEP_HALF * stiffness * old_state[:, 1] + integral_mid) / divisor
    coarse_fresh = coarse_eval(next_mid[:, None])
    next_end = (
        next_mid
        + STEP_HALF * (coarse_fresh[:, 0] - old_coarse[:, 0])
        + STEP_HALF * stiffness * old_state[:, 2]
        + integral_end
    ) / divisor
    change = jnp.stack([next_mid - old_state[:, 1], next_end - old_state[:, 2]], 1)
    lifted = lax.psum_scatter(
        mix(local_from, change).astype(jnp.bfloat16), "lev", scatter_dimension=0, tiled=True
    ).astype(jnp.float32)
    corrected = fine_state[:, 1:] + jnp.pad(
        lifted, ((0, 0), (0, 0), (0, 0), (0, 0), (0, fine_width + 1 - coarse))
    )
    return (corrected, fine_tend)


LANES = 128
SUBLANES = 8
REPLICATED_BYTES = 16 * 2**20


def round_up(value, unit):
    return -(-value // unit) * unit


def interpolation(points, targets, degree):
    offset = (
        2.0 * np.pi * (np.arange(targets)[:, None] / targets - np.arange(points)[None, :] / points)
    )
    order = np.arange(1, degree + 1)
    return (1.0 + 2.0 * np.cos(offset[:, :, None] * order).sum(-1)) / points


def wave_rows(waves, points, amplitude):
    turns = np.arange(waves)[:, None] * np.arange(points)[None, :] % points
    angles = turns * (2.0 * np.pi / points)
    return np.concatenate([np.cos(angles), -np.sin(angles)]) * amplitude


def matmul(a, b):
    return jnp.dot(a, b, preferred_element_type=jnp.float32)


def matmul_nt(a, b):
    return lax.dot_general(a, b, (((1,), (1,)), ((), ())), preferred_element_type=jnp.float32)


def matmul_exact(a, b):
    return jnp.dot(a, b, preferred_element_type=jnp.float32, precision=lax.Precision.HIGHEST)


def high_low(values):
    high = values.astype(jnp.bfloat16)
    return high, (values - high.astype(jnp.float32)).astype(jnp.bfloat16)


def matmul_split(left, right):
    high, low = high_low(right)
    return matmul(left, jnp.concatenate([high, low, high], 0))


class Sizes:
    def __init__(self, fine_state, legendre):
        self.n_wave, self.n_lev = lax.axis_size("wave"), lax.axis_size("lev")
        self.lev_dev, self.nodes, _, self.slots, self.fine_rows = fine_state.shape
        self.lats = legendre.shape[1]
        self.n_pair = self.n_lev // 2
        self.fine_width = self.fine_rows - 1
        self.coarse = self.fine_width // 2
        self.levels = self.n_lev * self.lev_dev
        self.dev_rows = self.lev_dev * self.nodes * 2
        self.rows = self.levels * self.nodes * 2
        self.per_node = self.levels * 2
        self.head = self.slots * self.coarse
        self.rest = self.fine_rows - self.coarse
        self.used = self.slots * self.fine_rows
        self.state_rows = round_up(self.dev_rows, SUBLANES)
        self.groups = (self.lats + self.state_rows) // SUBLANES
        self.unit = LANES // self.groups
        self.block_rows = self.lats + SUBLANES + self.state_rows
        self.chips = self.n_wave * self.n_pair
        self.fine_columns = self.n_wave * self.slots * 2
        self.coarse_columns = self.n_wave * self.slots
        self.points = round_up(4 * (self.fine_width - 1) + 1, 32)
        self.coarse_points = round_up(4 * (self.coarse - 1) + 1, 32)


def pack_kernel(z, state_ref, leg_ref, gauss_ref, out_ref, rows_s):
    bf, f32 = jnp.bfloat16, jnp.float32
    row = lax.broadcasted_iota(jnp.int32, (z.fine_rows, LANES), 0)
    lane = lax.broadcasted_iota(jnp.int32, (z.fine_rows, LANES), 1)
    for n in range(z.dev_rows):
        a, b, c = n // (z.nodes * 2), n // 2 % z.nodes, n % 2
        values = state_ref[a, b, c]
        for s in range(z.slots):
            rows_s[s, n : n + 1, :] = values[s : s + 1]
    if z.state_rows > z.dev_rows:
        for s in range(z.slots):
            rows_s[s, z.dev_rows :, :] = jnp.zeros((z.state_rows - z.dev_rows, z.fine_rows), f32)
    table = jnp.zeros((z.lats, LANES), f32)
    state = jnp.zeros((z.state_rows, LANES), f32)
    extra = jnp.zeros((SUBLANES, LANES), f32)
    for s in range(z.slots):
        target = jnp.where(row < z.coarse, s * z.coarse + row, z.head + s * z.rest + row - z.coarse)
        leg = leg_ref[s].astype(f32)
        spec = rows_s[s]
        place = (target == lane).astype(bf)
        table = table + matmul(leg.astype(bf), place)
        state = state + matmul(spec.astype(bf), place)
        if z.head + (s + 1) * z.rest > LANES:
            for q in range(z.groups):
                at = q * SUBLANES
                part = leg[at : at + SUBLANES] if at < z.lats else spec[at - z.lats : at - z.lats + SUBLANES]
                place = ((target >= LANES) & (target - LANES + q * z.unit == lane)).astype(bf)
                extra = extra + matmul(part.astype(bf), place)
    wide_row = lax.broadcasted_iota(jnp.int32, (SUBLANES, z.lats), 0)
    wide_lane = lax.broadcasted_iota(jnp.int32, (SUBLANES, z.lats), 1)
    out_lane = lax.broadcasted_iota(jnp.int32, (SUBLANES, LANES), 1)
    for q in range(z.lats // SUBLANES):
        chosen = jnp.where(wide_lane == wide_row + q * SUBLANES, gauss_ref[...], 0.0)
        column = jnp.sum(chosen, axis=1, keepdims=True)
        high = column.astype(bf).astype(f32)
        at = q * z.unit + z.used - LANES
        extra = extra + jnp.where(out_lane == at, high, 0.0)
        extra = extra + jnp.where(out_lane == at + 1, column - high, 0.0)
    block = jnp.concatenate([table, extra, state], 0).astype(bf)
    for i in range(z.chips):
        out_ref[i] = block


def mix_matrix(pick_left, matrix, pick_right, mask, cut):
    values = matmul_exact(matmul_exact(pick_left, matrix), pick_right) * mask
    high, low = high_low(values)
    lane = lax.broadcasted_iota(jnp.int32, values.shape, 1)
    return jnp.where(lane < cut, high.astype(jnp.float32), low.astype(jnp.float32)).astype(jnp.bfloat16)


def tables_kernel(
    z,
    rate_ref,
    fold_smem,
    fold_ref,
    coef_ref,
    to_ref,
    from_ref,
    basis_ref,
    spread_ref,
    coarse_spread_ref,
    sampled_ref,
    coarse_sampled_ref,
    to_left_ref,
    to_right_ref,
    to_mask_ref,
    from_left_ref,
    from_right_ref,
    from_mask_ref,
    back_left_ref,
    back_right_ref,
    lift_left_ref,
    lift_right_ref,
    lift_mask_ref,
    wave_ref,
    quad_ref,
    coarse_wave_ref,
    coarse_quad_ref,
    mix_to_ref,
    mix_from_ref,
    mix_back_ref,
    lift_ref,
    member_ref,
    slot_ref,
    keep_ref,
    stiff_ref,
):
    bf, f32 = jnp.bfloat16, jnp.float32
    lev = lax.axis_index("lev")
    core = lax.rem(lev, 2)
    waves, coarse = z.fine_width, z.coarse
    half = z.fine_columns

    def wave_column(count, per_slot):
        row = lax.broadcasted_iota(jnp.int32, (count, z.coarse_columns), 0)
        lane = lax.broadcasted_iota(jnp.int32, (count, z.coarse_columns), 1)
        inside = (row >= lane * per_slot) & (row < (lane + 1) * per_slot)
        small = jnp.sum(jnp.where(inside, fold_ref[...].astype(f32), 0.0), axis=1, keepdims=True)
        if per_slot == 1:
            return small
        first = lax.broadcasted_iota(jnp.int32, (count, 1), 0) & 1
        return jnp.where(first == 0, small, waves - 1 - small)

    def one_hot(count, per_slot, width):
        column = wave_column(count, per_slot)
        lane = lax.broadcasted_iota(jnp.int32, (count, 2 * width), 1).astype(f32)
        top = (lane == column).astype(f32)
        bottom = (lane == column + width).astype(f32)
        return jnp.concatenate([top, bottom], 0).astype(bf)

    hot = one_hot(half, 2, waves)
    coarse_hot = one_hot(z.coarse_columns, 1, coarse)
    wave_ref[...] = matmul_nt(sampled_ref[...], hot).astype(bf)
    coarse_wave_ref[...] = matmul_nt(coarse_sampled_ref[...], coarse_hot).astype(bf)
    for x in range(z.n_pair):
        for o in range(2):
            for al in range(z.lev_dev):
                a = (2 * x + o) * z.lev_dev + al
                level = (2 * x + (core if o == 0 else 1 - core)) * z.lev_dev + al
                scaled = coef_ref[pl.ds(level, 1), :] * basis_ref[...].astype(f32)
                low = jnp.concatenate([scaled[:coarse], scaled[waves : waves + coarse]], 0)
                quad = matmul(scaled.astype(bf), spread_ref[...]).astype(bf)
                quad_ref[a] = matmul(hot, quad).astype(bf)
                quad = matmul(low.astype(bf), coarse_spread_ref[...]).astype(bf)
                coarse_quad_ref[a] = matmul(coarse_hot, quad).astype(bf)

    def mix(left, matrix_ref, right, mask_ref):
        return mix_matrix(left, matrix_ref[...], right, mask_ref[...], right.shape[1] // 3 * 2)

    mix_to_ref[...] = mix(to_left_ref[...], to_ref, to_right_ref[core], to_mask_ref)
    mix_from_ref[...] = mix(from_left_ref[core], from_ref, from_right_ref[...], from_mask_ref)
    mix_back_ref[...] = mix(back_left_ref[...], to_ref, back_right_ref[core], from_mask_ref)
    lift_ref[...] = mix(lift_left_ref[lev], from_ref, lift_right_ref[...], lift_mask_ref)

    wide = 2 * LANES
    lane = lax.broadcasted_iota(jnp.int32, (1, wide), 1)
    lane_slot = jnp.full((1, wide), -1, jnp.int32)
    lane_row = jnp.zeros((1, wide), jnp.int32)
    for s in range(z.slots):
        for begin, width, first in ((s * coarse, coarse, 0), (z.head + s * z.rest, z.rest, coarse)):
            inside = (lane >= begin) & (lane < begin + width)
            lane_slot = jnp.where(inside, s, lane_slot)
            lane_row = jnp.where(inside, lane - begin + first, lane_row)
    rate_row = lax.broadcasted_iota(jnp.int32, (z.per_node, LANES), 0)
    rates = jnp.zeros((z.per_node, LANES), f32)
    for q in range(z.levels):
        rates = jnp.where((rate_row >= 2 * q) & (rate_row < 2 * q + 2), rate_ref[q], rates)
    for w in range(z.n_wave):
        small = jnp.zeros((1, wide), jnp.int32)
        for s in range(z.slots):
            small = jnp.where(lane_slot == s, fold_smem[w * z.slots + s], small)
        first = lane_row < waves - small
        keep = (lane < z.head) & (lane_row < coarse - small)
        keep_ref[w : w + 1, :] = keep[:, :LANES].astype(f32)
        for s in range(z.slots):
            own = lane_slot == s
            at = (w * z.slots + s) * 2
            member_ref[at : at + 1, :] = (own & first).astype(f32)
            member_ref[at + 1 : at + 2, :] = (own & jnp.logical_not(first)).astype(f32)
            slot_ref[w * z.slots + s : w * z.slots + s + 1, :] = (own & keep)[:, :LANES].astype(f32)
        degree = (small + lane_row)[:, :LANES].astype(f32)
        stiff_ref[w] = rates * (degree * (degree + 1.0) / (coarse * (coarse + 1.0)))


def sweep_kernel(
    z,
    own_ref,
    other_ref,
    state_ref,
    wave_ref,
    quad_ref,
    coarse_wave_ref,
    coarse_quad_ref,
    mix_to_ref,
    mix_from_ref,
    mix_back_ref,
    lift_ref,
    member_ref,
    slot_ref,
    keep_ref,
    stiff_ref,
    corrected_ref,
    tend_ref,
    leg_s,
    state_s,
    fourier_s,
    back_s,
    tend_s,
    coarse_s,
    coarse_back_s,
    change_s,
):
    bf, f32 = jnp.bfloat16, jnp.float32
    slots, rows, lats, per_node = z.slots, z.rows, z.lats, z.per_node
    wide = 2 * LANES
    all_lats = z.n_lev * lats

    def member(w, j):
        at = w * slots * 2 + j
        return member_ref[at : at + 1, :]

    def slot(w, s):
        return slot_ref[w * slots + s : w * slots + s + 1, :]

    def keep(w):
        return keep_ref[w : w + 1, :]

    for w in range(z.n_wave):
        for x in range(z.n_pair):
            for o, ref in enumerate((own_ref, other_ref)):
                d = 2 * x + o
                block = ref[w * z.n_pair + x].astype(f32)
                extra = block[lats : lats + SUBLANES]
                leg_s[w, d * lats : (d + 1) * lats, :LANES] = block[:lats]
                state_at = d * z.dev_rows
                begin = lats + SUBLANES
                state_s[w, state_at : state_at + z.dev_rows, :LANES] = block[begin : begin + z.dev_rows]
                for q in range(z.groups):
                    moved = extra if q == 0 else pltpu.roll(extra, LANES - q * z.unit, 1)
                    at = q * SUBLANES
                    if at < lats:
                        leg_s[w, d * lats + at : d * lats + at + SUBLANES, LANES:] = moved
                    else:
                        at = at - lats
                        count = min(SUBLANES, z.dev_rows - at)
                        state_s[w, state_at + at : state_at + at + count, LANES:] = moved[:count]
        if all_lats < leg_s.shape[1]:
            leg_s[w, all_lats:, :] = jnp.zeros((leg_s.shape[1] - all_lats, wide), f32)

    def legendre(w):
        return leg_s[w].astype(bf)

    def weighted(w):
        table = leg_s[w]
        column = table[:, z.used : z.used + 1] + table[:, z.used + 1 : z.used + 2]
        return (table * column).astype(bf)

    for w in range(z.n_wave):
        state = state_s[w]
        left = jnp.concatenate([state * member(w, j) for j in range(2 * slots)], 0).astype(bf)
        out = matmul_nt(left, legendre(w))
        for j in range(2 * slots):
            fourier_s[pl.ds(w * 2 * slots + j, rows, stride=z.fine_columns), :] = out[j * rows : (j + 1) * rows]

    both = 2 * z.fine_columns
    for a in range(z.levels):
        pieces = [
            fourier_s[(a * z.nodes + b) * both : (a * z.nodes + b + 1) * both, :].astype(bf)
            for b in range(z.nodes)
        ]
        grid = matmul(wave_ref[...], jnp.concatenate(pieces, 1))
        product = (grid * grid).astype(bf)
        back = matmul(quad_ref[a], product)
        for b in range(z.nodes):
            back_s[(a * z.nodes + b) * both : (a * z.nodes + b + 1) * both, :] = back[:, b * LANES : (b + 1) * LANES]

    stacked = []
    for w in range(z.n_wave):
        left = jnp.concatenate(
            [
                back_s[pl.ds(w * 2 * slots + j, rows, stride=z.fine_columns), :].astype(bf)
                for j in range(2 * slots)
            ],
            0,
        )
        out = matmul(left, weighted(w))
        total = member(w, 0) * out[:rows]
        for j in range(1, 2 * slots):
            total = total + member(w, j) * out[j * rows : (j + 1) * rows]
        tend_s[w, :rows, :] = total
        stacked.append(state_s[w][:, :LANES] * keep(w))
        stacked.append(total[:, :LANES] * keep(w))

    modes = matmul_split(mix_to_ref[...], jnp.concatenate(stacked, 1))
    evals, later, old_of, mid_of = [], [], [], []
    for w in range(z.n_wave):
        old, source = [], []
        stiff = stiff_ref[w]
        for b in range(z.nodes):
            part = modes[b * per_node : (b + 1) * per_node]
            old.append(part[:, 2 * w * LANES : (2 * w + 1) * LANES])
            source.append(part[:, (2 * w + 1) * LANES : (2 * w + 2) * LANES] - stiff * old[-1])
        divisor = 1.0 + STEP_HALF * stiff
        mid = sum(quad_weights[0][b] * source[b] for b in range(z.nodes))
        mid = (mid + old[0] + STEP_HALF * stiff * old[1]) / divisor
        end = sum(quad_weights[1][b] * source[b] for b in range(z.nodes))
        end = end + mid + STEP_HALF * stiff * old[2]
        evals.append(old[1])
        evals.append(mid)
        later.append((end, divisor))
        old_of.append(old)
        mid_of.append(mid)

    level_values = matmul_split(mix_from_ref[...], jnp.concatenate(evals, 1))
    for w in range(z.n_wave):
        left = jnp.concatenate(
            [
                level_values[:, (2 * w + e) * LANES : (2 * w + e + 1) * LANES] * slot(w, s)
                for s in range(slots)
                for e in range(2)
            ],
            0,
        ).astype(bf)
        out = matmul_nt(left, legendre(w)[:, :LANES])
        for s in range(slots):
            for e in range(2):
                at = (s * 2 + e) * per_node
                coarse_s[e, pl.ds(w * slots + s, per_node, stride=z.coarse_columns), :] = out[at : at + per_node]

    both_c = 2 * z.coarse_columns
    for a in range(z.levels):
        pieces = [coarse_s[e, a * both_c : (a + 1) * both_c, :].astype(bf) for e in range(2)]
        grid = matmul(coarse_wave_ref[...], jnp.concatenate(pieces, 1))
        product = (grid * grid).astype(bf)
        back = matmul(coarse_quad_ref[a], product)
        for e in range(2):
            coarse_back_s[e, a * both_c : (a + 1) * both_c, :] = back[:, e * LANES : (e + 1) * LANES]

    tends = []
    for w in range(z.n_wave):
        left = jnp.concatenate(
            [
                coarse_back_s[e, pl.ds(w * slots + s, per_node, stride=z.coarse_columns), :].astype(bf)
                for s in range(slots)
                for e in range(2)
            ],
            0,
        )
        out = matmul(left, weighted(w)[:, :LANES])
        for e in range(2):
            total = None
            for s in range(slots):
                at = (s * 2 + e) * per_node
                term = slot(w, s) * out[at : at + per_node]
                total = term if total is None else total + term
            tends.append(total)
    coarse_modes = matmul_split(mix_back_ref[...], jnp.concatenate(tends, 1))
    for w in range(z.n_wave):
        before = coarse_modes[:, 2 * w * LANES : (2 * w + 1) * LANES]
        fresh = coarse_modes[:, (2 * w + 1) * LANES : (2 * w + 2) * LANES]
        end, divisor = later[w]
        end = (end + STEP_HALF * (fresh - before)) / divisor
        change_s[w, :per_node, :] = mid_of[w] - old_of[w][1]
        change_s[w, per_node:, :] = end - old_of[w][2]

    place = lax.axis_index("wave")
    begin = pl.multiple_of(lax.div(lax.axis_index("lev"), 2) * (2 * z.dev_rows), SUBLANES)
    mine = tend_s[place, pl.ds(begin, z.state_rows), :]
    raised = matmul_split(lift_ref[...], change_s[place])
    lane = lax.broadcasted_iota(jnp.int32, (z.state_rows, wide), 1)
    for s in range(slots):
        low = mine if s == 0 else pltpu.roll(mine, wide - s * z.coarse, 1)
        high = pltpu.roll(mine, wide - (z.head + s * z.rest - z.coarse), 1)
        values = jnp.where(lane < z.coarse, low, high)
        for n in range(z.dev_rows):
            a, b, c = n // (z.nodes * 2), n // 2 % z.nodes, n % 2
            tend_ref[a, b, c, s : s + 1, :] = values[n : n + 1, : z.fine_rows]
        low = raised if s == 0 else pltpu.roll(raised, LANES - s * z.coarse, 1)
        low = jnp.where(lane[: low.shape[0], :LANES] < z.coarse, low, 0.0)
        for n in range(low.shape[0]):
            a, b, c = n // (2 * (z.nodes - 1)), n // 2 % (z.nodes - 1), n % 2
            corrected_ref[a, b, c, s : s + 1, :] = (
                state_ref[a, b + 1, c, s : s + 1, :] + low[n : n + 1, : z.fine_rows]
            )


def mix_constants(z):
    level, node, part = np.arange(z.levels), np.arange(z.nodes), np.arange(2)

    def pick(index):
        return (np.asarray(index)[:, None] == level[None, :]).astype(np.float32)

    def grid(*axes):
        return [m.reshape(-1) for m in np.meshgrid(*axes, indexing="ij")]

    def ordered(index, core):
        lev, inner = index // z.lev_dev, index % z.lev_dev
        return (lev ^ core) * z.lev_dev + inner

    def thrice(matrix):
        return np.concatenate([matrix] * 3, -1)

    rb, rq, rc = grid(node, level, part)
    ca, cb, cc = grid(level, node, part)
    sa, sc = grid(level, part)
    to_mask = (rb[:, None] == cb[None]) & (rc[:, None] == cc[None])
    same_part = sc[:, None] == sc[None]
    la, lb, lc = grid(np.arange(z.lev_dev), np.arange(z.nodes - 1), part)
    kb, kq, kc = grid(np.arange(z.nodes - 1), level, part)
    lift_mask = (lb[:, None] == kb[None]) & (lc[:, None] == kc[None])
    by_core = range(2)
    constants = (
        pick(rq),
        np.stack([thrice(pick(ordered(ca, k)).T) for k in by_core]),
        thrice(to_mask),
        np.stack([pick(ordered(sa, k)) for k in by_core]),
        thrice(pick(sa).T),
        thrice(same_part),
        pick(sa),
        np.stack([thrice(pick(ordered(sa, k)).T) for k in by_core]),
        np.stack([pick(k * z.lev_dev + la) for k in range(z.n_lev)]),
        thrice(pick(kq).T),
        thrice(lift_mask),
    )
    return [jnp.asarray(c, jnp.float32) for c in constants]


def replicated_plan(
    fine_state, fold_pairs, legendre, gauss_weights, grid_coef, modes_from, modes_to, mode_rates
):
    z = Sizes(fine_state, legendre)
    bf, f32 = jnp.bfloat16, jnp.float32
    longitudes = grid_coef.shape[1]
    vmem = pl.BlockSpec(memory_space=pltpu.VMEM)
    smem = pl.BlockSpec(memory_space=pltpu.SMEM)
    shape = jax.ShapeDtypeStruct
    block = pl.pallas_call(
        functools.partial(pack_kernel, z),
        out_shape=shape((z.chips, z.block_rows, LANES), bf),
        in_specs=[vmem] * 3,
        out_specs=vmem,
        scratch_shapes=[pltpu.VMEM((z.slots, z.state_rows, z.fine_rows), f32)],
        name="pack",
    )(fine_state, legendre, gauss_weights[None])
    groups = [[2 * i + c for i in range(z.chips)] for c in range(2)]
    own = lax.all_to_all(
        block, ("wave", "lev"), 0, 0, tiled=True, axis_index_groups=groups
    )
    other = lax.ppermute(own, ("wave", "lev"), [(i, i ^ 1) for i in range(2 * z.chips)])

    fine_amp, coarse_amp = z.fine_width**-0.5, z.coarse**-0.5
    basis = wave_rows(z.fine_width, longitudes, fine_amp)
    spread = interpolation(z.points, longitudes, 2 * (z.fine_width - 1))
    spread *= 2.0 * z.fine_width / longitudes
    coarse_spread = interpolation(z.coarse_points, longitudes, 2 * (z.coarse - 1))
    coarse_spread *= 2.0 * z.coarse / (longitudes // 2) * (coarse_amp / fine_amp)
    coarse_spread[1::2] = 0.0
    sampled = wave_rows(z.fine_width, z.points, fine_amp).T
    coarse_sampled = wave_rows(z.coarse, z.coarse_points, coarse_amp).T
    constants = [jnp.asarray(c, bf) for c in (basis, spread, coarse_spread, sampled, coarse_sampled)]
    mixes = mix_constants(z)
    wide = 2 * LANES
    n_lift = z.lev_dev * (z.nodes - 1) * 2
    tables = pl.pallas_call(
        functools.partial(tables_kernel, z),
        out_shape=(
            shape((z.points, 2 * z.fine_columns), bf),
            shape((z.levels, 2 * z.fine_columns, z.points), bf),
            shape((z.coarse_points, 2 * z.coarse_columns), bf),
            shape((z.levels, 2 * z.coarse_columns, z.coarse_points), bf),
            shape((z.rows, 3 * z.rows), bf),
            shape((z.per_node, 3 * z.per_node), bf),
            shape((z.per_node, 3 * z.per_node), bf),
            shape((n_lift, 3 * (z.nodes - 1) * z.per_node), bf),
            shape((z.fine_columns, wide), f32),
            shape((z.coarse_columns, LANES), f32),
            shape((z.n_wave, LANES), f32),
            shape((z.n_wave, z.per_node, LANES), f32),
        ),
        in_specs=[smem, smem] + [vmem] * (4 + len(constants) + len(mixes)),
        out_specs=(vmem,) * 12,
        cost_estimate=pl.CostEstimate(flops=10**9, bytes_accessed=4 * 10**6, transcendentals=0),
        name="tables",
    )(mode_rates, fold_pairs, fold_pairs[None], grid_coef, modes_to, modes_from, *constants, *mixes)

    lat_rows = round_up(z.n_lev * z.lats, LANES)
    corrected, fine_tend = pl.pallas_call(
        functools.partial(sweep_kernel, z),
        out_shape=(
            shape((z.lev_dev, z.nodes - 1, 2, z.slots, z.fine_rows), f32),
            shape(fine_state.shape, f32),
        ),
        in_specs=[vmem] * 15,
        out_specs=(vmem, vmem),
        scratch_shapes=[
            pltpu.VMEM((z.n_wave, lat_rows, wide), f32),
            pltpu.VMEM((z.n_wave, z.rows, wide), f32),
            pltpu.VMEM((z.rows * z.fine_columns, lat_rows), f32),
            pltpu.VMEM((z.rows * z.fine_columns, lat_rows), f32),
            pltpu.VMEM((z.n_wave, z.rows + SUBLANES, wide), f32),
            pltpu.VMEM((2, z.per_node * z.coarse_columns, lat_rows), f32),
            pltpu.VMEM((2, z.per_node * z.coarse_columns, lat_rows), f32),
            pltpu.VMEM((z.n_wave, (z.nodes - 1) * z.per_node, LANES), f32),
        ],
        name="sweep",
    )(own, other, fine_state, *tables)
    return (corrected, fine_tend)


def fits_replicated(fine_state, legendre):
    n_wave, n_lev = lax.axis_size("wave"), lax.axis_size("lev")
    if n_lev % 2 or fine_state.shape[1] != len(quad_weights[0]):
        return False
    z = Sizes(fine_state, legendre)
    gathered = 32 * n_wave * n_lev * (legendre.size + fine_state.size)
    return (
        z.head <= LANES
        and z.used > LANES
        and z.used + 2 - LANES <= z.unit
        and z.lats % SUBLANES == 0
        and n_lev * z.lats <= LANES
        and gathered <= REPLICATED_BYTES
    )


def per_device(fine_state, fold_pairs, legendre, *rest):
    plan = replicated_plan if fits_replicated(fine_state, legendre) else split_plan
    return plan(fine_state, fold_pairs, legendre, *rest)


def solution(mesh):
    placed = (
        P("lev", None, None, "wave", None),
        P(),
        P("wave", "lev", None),
        P("lev"),
        P(),
        P(),
        P(),
        P(),
    )
    return jax.shard_map(
        per_device,
        mesh=mesh,
        in_specs=placed,
        out_specs=(P("lev", None, None, "wave", None), P("lev", None, None, "wave", None)),
        check_vma=False,
    )
```

```python
import functools
import math

import jax
import jax.numpy as jnp
import numpy as np
from jax import lax
from jax.experimental import pallas as pl
from jax.experimental.pallas import tpu as pltpu
from jax.sharding import PartitionSpec as P

STEP_HALF = 0.5
quad_weights = ((5.0 / 24.0, 1.0 / 3.0, -1.0 / 24.0), (-1.0 / 24.0, 1.0 / 3.0, 5.0 / 24.0))
HIGHEST = lax.Precision.HIGHEST


def fourier_table(waves, points, amplitude):
    steps = jnp.arange(points, dtype=jnp.int32)
    turns = waves[:, :, None] * steps[None, None, :] % points
    angles = turns.astype(jnp.float32) * (2.0 * math.pi / points)
    return jnp.stack([jnp.cos(angles) * amplitude, -jnp.sin(angles) * amplitude]).astype(
        jnp.bfloat16
    )


def fine_rows(small_wave, fine_width):
    row_ids = jnp.arange(fine_width + 1, dtype=jnp.int32)[None, :]
    return row_ids < fine_width - small_wave[:, None]


def coarse_rows(small_wave, coarse):
    row_ids = jnp.arange(coarse, dtype=jnp.int32)[None, :]
    coarse_keep = row_ids < coarse - small_wave[:, None]
    degree = (small_wave[:, None] + row_ids).astype(jnp.float32)
    return (coarse_keep, degree)


def legendre_inverse(spectral, legendre_table, row_mask):
    split_spec = spectral[:, :, :, :, None, :] * row_mask[None, None, None]
    return jnp.einsum(
        "abcpmr,plr->abcpml", split_spec, legendre_table, preferred_element_type=jnp.float32
    ).astype(jnp.bfloat16)


def legendre_forward(returned, legendre_table, row_mask):
    members = jnp.einsum(
        "abcpml,plr->abcpmr", returned, legendre_table, preferred_element_type=jnp.float32
    )
    return jnp.sum(members * row_mask.astype(jnp.float32)[None, None, None], axis=4)


def grid_step(fourier, wave_table, coef, weights, factor):
    grid_field = jnp.einsum(
        "abcpmz,cpmk->abzk", fourier, wave_table, preferred_element_type=jnp.float32
    )
    product = (coef[:, None, None, :] * grid_field * grid_field).astype(jnp.bfloat16)
    returned = jnp.einsum(
        "abzk,cpmk->abcpmz", product, wave_table, preferred_element_type=jnp.float32
    )
    return (returned * (weights * factor)).astype(jnp.bfloat16)


def mix(matrix, values):
    return jnp.einsum("ql,lbcpr->qbcpr", matrix, values, precision=HIGHEST)


def split_plan(
    fine_state, fold_pairs, legendre, gauss_weights, grid_coef, modes_from, modes_to, mode_rates
):
    n_wave = lax.axis_size("wave")
    wave_idx = lax.axis_index("wave")
    lev_idx = lax.axis_index("lev")
    lev_dev = fine_state.shape[0]
    pairs_dev = fine_state.shape[3]
    fine_width = fine_state.shape[4] - 1
    coarse = fine_width // 2
    longitudes = grid_coef.shape[1]
    band_size = legendre.shape[1] // n_wave
    small_wave = lax.dynamic_slice_in_dim(fold_pairs, wave_idx * pairs_dev, pairs_dev)
    first_member = fine_rows(small_wave, fine_width)
    member_mask = jnp.stack([first_member, jnp.logical_not(first_member)], 1).astype(jnp.bfloat16)
    coarse_keep, degree = coarse_rows(small_wave, coarse)
    keep_mask = coarse_keep[:, None, :].astype(jnp.bfloat16)
    keep_float = coarse_keep.astype(jnp.float32)
    fine_table = fourier_table(
        jnp.stack([fold_pairs, fine_width - 1 - fold_pairs], 1), longitudes, fine_width ** (-0.5)
    )
    coarse_table = fourier_table(fold_pairs[:, None], longitudes // 2, coarse ** (-0.5))
    coarse_leg = legendre[:, :, :coarse]
    coarse_coef = grid_coef[:, ::2]
    band_gauss = lax.dynamic_slice_in_dim(gauss_weights, wave_idx * band_size, band_size)
    local_to = lax.dynamic_slice_in_dim(modes_to, lev_idx * lev_dev, lev_dev, 1)
    local_from = lax.dynamic_slice_in_dim(modes_from, lev_idx * lev_dev, lev_dev, 1)
    mode_decay = lax.dynamic_slice_in_dim(mode_rates, lev_idx * lev_dev, lev_dev)

    def project(partial_sum):
        return mix(modes_to, partial_sum)

    def coarse_start(modes):
        gathered = lax.all_gather(modes, "lev", axis=0, tiled=True)
        levels = (mix(modes_from, gathered) * keep_float).astype(jnp.bfloat16)
        return legendre_inverse(levels, coarse_leg, keep_mask)

    def coarse_grid_step(fourier):
        return grid_step(
            fourier, coarse_table, coarse_coef, band_gauss, 2.0 * coarse / (longitudes // 2)
        )

    def coarse_finish(returned):
        partial_sum = legendre_forward(returned, coarse_leg, keep_mask)
        return lax.psum_scatter(
            project(partial_sum).astype(jnp.bfloat16), "lev", scatter_dimension=0, tiled=True
        ).astype(jnp.float32)

    def coarse_eval(modes):
        fourier = lax.all_to_all(
            coarse_start(modes), "wave", split_axis=5, concat_axis=3, tiled=True
        )
        returned = lax.all_to_all(
            coarse_grid_step(fourier), "wave", split_axis=3, concat_axis=5, tiled=True
        )
        return coarse_finish(returned)

    restricted = fine_state[..., :coarse] * keep_float
    fine_spec = lax.all_gather(fine_state.astype(jnp.bfloat16), "lev", axis=0, tiled=True)
    fine_fourier = legendre_inverse(fine_spec, legendre, member_mask)
    fine_fourier = lax.all_to_all(fine_fourier, "wave", split_axis=5, concat_axis=3, tiled=True)
    fine_back = lax.all_to_all(
        grid_step(fine_fourier, fine_table, grid_coef, band_gauss, 2.0 * fine_width / longitudes),
        "wave",
        split_axis=3,
        concat_axis=5,
        tiled=True,
    )
    fine_tend = lax.psum_scatter(
        legendre_forward(fine_back, legendre, member_mask).astype(jnp.bfloat16),
        "lev",
        scatter_dimension=0,
        tiled=True,
    ).astype(jnp.float32)
    restricted_tend = fine_tend[..., :coarse] * keep_float
    stacked = jnp.concatenate([restricted, restricted_tend], 1)
    both_modes = lax.psum_scatter(
        mix(local_to, stacked).astype(jnp.bfloat16), "lev", scatter_dimension=0, tiled=True
    ).astype(jnp.float32)
    nodes = fine_state.shape[1]
    old_state = both_modes[:, :nodes]
    old_tend = both_modes[:, nodes:]
    old_coarse = coarse_eval(old_state[:, 1:2])
    stiffness = (
        mode_decay[:, None, None, None]
        * (degree * (degree + 1.0) / (coarse * (coarse + 1.0)))[None, None]
    )
    source = old_tend - stiffness[:, None] * old_state
    integral_mid = (
        quad_weights[0][0] * source[:, 0]
        + quad_weights[0][1] * source[:, 1]
        + quad_weights[0][2] * source[:, 2]
    )
    integral_end = (
        quad_weights[1][0] * source[:, 0]
        + quad_weights[1][1] * source[:, 1]
        + quad_weights[1][2] * source[:, 2]
    )
    divisor = 1.0 + STEP_HALF * stiffness
    next_mid = (old_state[:, 0] + STEP_HALF * stiffness * old_state[:, 1] + integral_mid) / divisor
    coarse_fresh = coarse_eval(next_mid[:, None])
    next_end = (
        next_mid
        + STEP_HALF * (coarse_fresh[:, 0] - old_coarse[:, 0])
        + STEP_HALF * stiffness * old_state[:, 2]
        + integral_end
    ) / divisor
    change = jnp.stack([next_mid - old_state[:, 1], next_end - old_state[:, 2]], 1)
    lifted = lax.psum_scatter(
        mix(local_from, change).astype(jnp.bfloat16), "lev", scatter_dimension=0, tiled=True
    ).astype(jnp.float32)
    corrected = fine_state[:, 1:] + jnp.pad(
        lifted, ((0, 0), (0, 0), (0, 0), (0, 0), (0, fine_width + 1 - coarse))
    )
    return (corrected, fine_tend)


LANES = 128
SUBLANES = 8
REPLICATED_BYTES = 16 * 2**20
VMEM_BYTES = 28 * 2**20


def round_up(value, unit):
    return -(-value // unit) * unit


def interpolation(points, targets, degree):
    offset = (
        2.0 * np.pi * (np.arange(targets)[:, None] / targets - np.arange(points)[None, :] / points)
    )
    order = np.arange(1, degree + 1)
    return (1.0 + 2.0 * np.cos(offset[:, :, None] * order).sum(-1)) / points


def wave_rows(waves, points, amplitude):
    turns = np.arange(waves)[:, None] * np.arange(points)[None, :] % points
    angles = turns * (2.0 * np.pi / points)
    return np.concatenate([np.cos(angles), -np.sin(angles)]) * amplitude


def matmul(a, b):
    return jnp.dot(a, b, preferred_element_type=jnp.float32)


def matmul_nt(a, b):
    return lax.dot_general(a, b, (((1,), (1,)), ((), ())), preferred_element_type=jnp.float32)


def matmul_exact(a, b):
    return jnp.dot(a, b, preferred_element_type=jnp.float32, precision=lax.Precision.HIGHEST)


def high_low(values):
    high = values.astype(jnp.bfloat16)
    return high, (values - high.astype(jnp.float32)).astype(jnp.bfloat16)


def matmul_split(left, right):
    high, low = high_low(right)
    return matmul(left, jnp.concatenate([high, low, high], 0))


class Sizes:
    def __init__(self, fine_state, legendre):
        self.n_wave, self.n_lev = lax.axis_size("wave"), lax.axis_size("lev")
        self.lev_dev, self.nodes, _, self.slots, self.fine_rows = fine_state.shape
        self.lats = legendre.shape[1]
        self.n_pair = self.n_lev // 2
        self.fine_width = self.fine_rows - 1
        self.coarse = self.fine_width // 2
        self.levels = self.n_lev * self.lev_dev
        self.dev_rows = self.lev_dev * self.nodes * 2
        self.rows = self.levels * self.nodes * 2
        self.per_node = self.levels * 2
        self.head = self.slots * self.coarse
        self.rest = self.fine_rows - self.coarse
        self.used = self.slots * self.fine_rows
        self.state_rows = round_up(self.dev_rows, SUBLANES)
        self.groups = (self.lats + self.state_rows) // SUBLANES
        self.unit = LANES // self.groups
        self.block_rows = self.lats + SUBLANES + self.state_rows
        self.chips = self.n_wave * self.n_pair
        self.fine_columns = self.n_wave * self.slots * 2
        self.coarse_columns = self.n_wave * self.slots
        self.points = round_up(4 * (self.fine_width - 1) + 1, 32)
        self.coarse_points = round_up(4 * (self.coarse - 1) + 1, 32)


def pack_kernel(z, state_ref, leg_ref, gauss_ref, out_ref, rows_s):
    bf, f32 = jnp.bfloat16, jnp.float32
    row = lax.broadcasted_iota(jnp.int32, (z.fine_rows, LANES), 0)
    lane = lax.broadcasted_iota(jnp.int32, (z.fine_rows, LANES), 1)
    for a in range(z.lev_dev):
        for b in range(z.nodes):
            n = (a * z.nodes + b) * 2
            for s in range(z.slots):
                rows_s[s, n : n + 2, :] = state_ref[a, b, s]
    if z.state_rows > z.dev_rows:
        for s in range(z.slots):
            rows_s[s, z.dev_rows :, :] = jnp.zeros((z.state_rows - z.dev_rows, z.fine_rows), f32)
    table = jnp.zeros((z.lats, LANES), f32)
    state = jnp.zeros((z.state_rows, LANES), f32)
    extra = jnp.zeros((SUBLANES, LANES), f32)
    for s in range(z.slots):
        target = jnp.where(row < z.coarse, s * z.coarse + row, z.head + s * z.rest + row - z.coarse)
        leg = leg_ref[s].astype(f32)
        spec = rows_s[s]
        place = (target == lane).astype(bf)
        table = table + matmul(leg.astype(bf), place)
        state = state + matmul(spec.astype(bf), place)
        if z.head + (s + 1) * z.rest > LANES:
            for q in range(z.groups):
                at = q * SUBLANES
                part = leg[at : at + SUBLANES] if at < z.lats else spec[at - z.lats : at - z.lats + SUBLANES]
                place = ((target >= LANES) & (target - LANES + q * z.unit == lane)).astype(bf)
                extra = extra + matmul(part.astype(bf), place)
    wide_row = lax.broadcasted_iota(jnp.int32, (SUBLANES, z.lats), 0)
    wide_lane = lax.broadcasted_iota(jnp.int32, (SUBLANES, z.lats), 1)
    out_lane = lax.broadcasted_iota(jnp.int32, (SUBLANES, LANES), 1)
    for q in range(z.lats // SUBLANES):
        chosen = jnp.where(wide_lane == wide_row + q * SUBLANES, gauss_ref[...], 0.0)
        column = jnp.sum(chosen, axis=1, keepdims=True)
        high = column.astype(bf).astype(f32)
        at = q * z.unit + z.used - LANES
        extra = extra + jnp.where(out_lane == at, high, 0.0)
        extra = extra + jnp.where(out_lane == at + 1, column - high, 0.0)
    block = jnp.concatenate([table, extra, state], 0).astype(bf)
    for i in range(z.chips):
        out_ref[i] = block


def mix_matrix(pick_left, matrix, pick_right, mask, cut):
    values = matmul_exact(matmul_exact(pick_left, matrix), pick_right) * mask
    high, low = high_low(values)
    lane = lax.broadcasted_iota(jnp.int32, values.shape, 1)
    return jnp.where(lane < cut, high.astype(jnp.float32), low.astype(jnp.float32)).astype(jnp.bfloat16)


def tables_kernel(
    z,
    rate_ref,
    fold_smem,
    fold_ref,
    coef_ref,
    to_ref,
    from_ref,
    basis_ref,
    spread_ref,
    coarse_spread_ref,
    sampled_ref,
    coarse_sampled_ref,
    to_left_ref,
    to_right_ref,
    to_mask_ref,
    from_left_ref,
    from_right_ref,
    from_mask_ref,
    back_left_ref,
    back_right_ref,
    lift_left_ref,
    lift_right_ref,
    lift_mask_ref,
    wave_ref,
    quad_ref,
    coarse_wave_ref,
    coarse_quad_ref,
    mix_to_ref,
    mix_from_ref,
    mix_back_ref,
    lift_ref,
    member_ref,
    slot_ref,
    keep_ref,
    stiff_ref,
    scaled_s,
    low_s,
):
    bf, f32 = jnp.bfloat16, jnp.float32
    lev = lax.axis_index("lev")
    core = lax.rem(lev, 2)
    waves, coarse = z.fine_width, z.coarse
    half = z.fine_columns

    def wave_column(count, per_slot):
        row = lax.broadcasted_iota(jnp.int32, (count, z.coarse_columns), 0)
        lane = lax.broadcasted_iota(jnp.int32, (count, z.coarse_columns), 1)
        inside = (row >= lane * per_slot) & (row < (lane + 1) * per_slot)
        small = jnp.sum(jnp.where(inside, fold_ref[...].astype(f32), 0.0), axis=1, keepdims=True)
        if per_slot == 1:
            return small
        first = lax.broadcasted_iota(jnp.int32, (count, 1), 0) & 1
        return jnp.where(first == 0, small, waves - 1 - small)

    def one_hot(count, per_slot, width):
        column = wave_column(count, per_slot)
        lane = lax.broadcasted_iota(jnp.int32, (count, 2 * width), 1).astype(f32)
        top = (lane == column).astype(f32)
        bottom = (lane == column + width).astype(f32)
        return jnp.concatenate([top, bottom], 0).astype(bf)

    hot = one_hot(half, 2, waves)
    coarse_hot = one_hot(z.coarse_columns, 1, coarse)
    wave_ref[...] = matmul_nt(sampled_ref[...], hot).astype(bf)
    coarse_wave_ref[...] = matmul_nt(coarse_sampled_ref[...], coarse_hot).astype(bf)
    tall, short = 2 * waves, 2 * coarse
    table = basis_ref[...].astype(f32)
    for x in range(z.n_pair):
        for o in range(2):
            for al in range(z.lev_dev):
                a = (2 * x + o) * z.lev_dev + al
                level = (2 * x + (core if o == 0 else 1 - core)) * z.lev_dev + al
                scaled = coef_ref[pl.ds(level, 1), :] * table
                scaled_s[a * tall : (a + 1) * tall, :] = scaled.astype(bf)
                low = jnp.concatenate([scaled[:coarse], scaled[waves : waves + coarse]], 0)
                low_s[a * short : (a + 1) * short, :] = low.astype(bf)
    quad = matmul(scaled_s[...], spread_ref[...]).astype(bf)
    coarse_quad = matmul(low_s[...], coarse_spread_ref[...]).astype(bf)
    for a in range(z.levels):
        quad_ref[a] = matmul(hot, quad[a * tall : (a + 1) * tall]).astype(bf)
        coarse_quad_ref[a] = matmul(coarse_hot, coarse_quad[a * short : (a + 1) * short]).astype(bf)

    def mix(left, matrix_ref, right, mask_ref):
        return mix_matrix(left, matrix_ref[...], right, mask_ref[...], right.shape[1] // 3 * 2)

    mix_to_ref[...] = mix(to_left_ref[...], to_ref, to_right_ref[core], to_mask_ref)
    mix_from_ref[...] = mix(from_left_ref[core], from_ref, from_right_ref[...], from_mask_ref)
    mix_back_ref[...] = mix(back_left_ref[...], to_ref, back_right_ref[core], from_mask_ref)
    lift_ref[...] = mix(lift_left_ref[lev], from_ref, lift_right_ref[...], lift_mask_ref)

    wide = 2 * LANES
    lane = lax.broadcasted_iota(jnp.int32, (1, wide), 1)
    lane_slot = jnp.full((1, wide), -1, jnp.int32)
    lane_row = jnp.zeros((1, wide), jnp.int32)
    for s in range(z.slots):
        for begin, width, first in ((s * coarse, coarse, 0), (z.head + s * z.rest, z.rest, coarse)):
            inside = (lane >= begin) & (lane < begin + width)
            lane_slot = jnp.where(inside, s, lane_slot)
            lane_row = jnp.where(inside, lane - begin + first, lane_row)
    rate_row = lax.broadcasted_iota(jnp.int32, (z.per_node, LANES), 0)
    rates = jnp.zeros((z.per_node, LANES), f32)
    for q in range(z.levels):
        rates = jnp.where((rate_row >= 2 * q) & (rate_row < 2 * q + 2), rate_ref[q], rates)
    for w in range(z.n_wave):
        small = jnp.zeros((1, wide), jnp.int32)
        for s in range(z.slots):
            small = jnp.where(lane_slot == s, fold_smem[w * z.slots + s], small)
        first = lane_row < waves - small
        keep = (lane < z.head) & (lane_row < coarse - small)
        keep_ref[w : w + 1, :] = keep[:, :LANES].astype(f32)
        for s in range(z.slots):
            own = lane_slot == s
            at = (w * z.slots + s) * 2
            member_ref[at : at + 1, :] = (own & first).astype(f32)
            member_ref[at + 1 : at + 2, :] = (own & jnp.logical_not(first)).astype(f32)
            slot_ref[w * z.slots + s : w * z.slots + s + 1, :] = (own & keep)[:, :LANES].astype(f32)
        degree = (small + lane_row)[:, :LANES].astype(f32)
        stiff_ref[w] = rates * (degree * (degree + 1.0) / (coarse * (coarse + 1.0)))


def sweep_kernel(
    z,
    own_ref,
    other_ref,
    state_ref,
    wave_ref,
    quad_ref,
    coarse_wave_ref,
    coarse_quad_ref,
    mix_to_ref,
    mix_from_ref,
    mix_back_ref,
    lift_ref,
    member_ref,
    slot_ref,
    keep_ref,
    stiff_ref,
    corrected_ref,
    tend_ref,
    leg_s,
    state_s,
    fourier_s,
    back_s,
    tend_s,
    coarse_s,
    coarse_back_s,
    change_s,
):
    bf, f32 = jnp.bfloat16, jnp.float32
    slots, rows, lats, per_node = z.slots, z.rows, z.lats, z.per_node
    wide = 2 * LANES
    all_lats = z.n_lev * lats

    def member(w, j):
        at = w * slots * 2 + j
        return member_ref[at : at + 1, :]

    def slot(w, s):
        return slot_ref[w * slots + s : w * slots + s + 1, :]

    def keep(w):
        return keep_ref[w : w + 1, :]

    for w in range(z.n_wave):
        for x in range(z.n_pair):
            for o, ref in enumerate((own_ref, other_ref)):
                d = 2 * x + o
                block = ref[w * z.n_pair + x].astype(f32)
                extra = block[lats : lats + SUBLANES]
                leg_s[w, d * lats : (d + 1) * lats, :LANES] = block[:lats]
                state_at = d * z.dev_rows
                begin = lats + SUBLANES
                state_s[w, state_at : state_at + z.dev_rows, :LANES] = block[begin : begin + z.dev_rows]
                for q in range(z.groups):
                    moved = extra if q == 0 else pltpu.roll(extra, LANES - q * z.unit, 1)
                    at = q * SUBLANES
                    if at < lats:
                        leg_s[w, d * lats + at : d * lats + at + SUBLANES, LANES:] = moved
                    else:
                        at = at - lats
                        count = min(SUBLANES, z.dev_rows - at)
                        state_s[w, state_at + at : state_at + at + count, LANES:] = moved[:count]
        if all_lats < leg_s.shape[1]:
            leg_s[w, all_lats:, :] = jnp.zeros((leg_s.shape[1] - all_lats, wide), f32)

    def legendre(w):
        return leg_s[w].astype(bf)

    def weighted(w):
        table = leg_s[w]
        column = table[:, z.used : z.used + 1] + table[:, z.used + 1 : z.used + 2]
        return (table * column).astype(bf)

    for w in range(z.n_wave):
        state = state_s[w]
        left = jnp.concatenate([state * member(w, j) for j in range(2 * slots)], 0).astype(bf)
        out = matmul_nt(left, legendre(w))
        for j in range(2 * slots):
            fourier_s[pl.ds(w * 2 * slots + j, rows, stride=z.fine_columns), :] = out[j * rows : (j + 1) * rows]

    both = 2 * z.fine_columns
    for a in range(z.levels):
        pieces = [
            fourier_s[(a * z.nodes + b) * both : (a * z.nodes + b + 1) * both, :].astype(bf)
            for b in range(z.nodes)
        ]
        grid = matmul(wave_ref[...], jnp.concatenate(pieces, 1))
        product = (grid * grid).astype(bf)
        back = matmul(quad_ref[a], product)
        for b in range(z.nodes):
            back_s[(a * z.nodes + b) * both : (a * z.nodes + b + 1) * both, :] = back[:, b * LANES : (b + 1) * LANES]

    stacked = []
    for w in range(z.n_wave):
        left = jnp.concatenate(
            [
                back_s[pl.ds(w * 2 * slots + j, rows, stride=z.fine_columns), :].astype(bf)
                for j in range(2 * slots)
            ],
            0,
        )
        out = matmul(left, weighted(w))
        total = member(w, 0) * out[:rows]
        for j in range(1, 2 * slots):
            total = total + member(w, j) * out[j * rows : (j + 1) * rows]
        tend_s[w, :rows, :] = total
        stacked.append(state_s[w][:, :LANES] * keep(w))
        stacked.append(total[:, :LANES] * keep(w))

    modes = matmul_split(mix_to_ref[...], jnp.concatenate(stacked, 1))
    evals, later, old_of, mid_of = [], [], [], []
    for w in range(z.n_wave):
        old, source = [], []
        stiff = stiff_ref[w]
        for b in range(z.nodes):
            part = modes[b * per_node : (b + 1) * per_node]
            old.append(part[:, 2 * w * LANES : (2 * w + 1) * LANES])
            source.append(part[:, (2 * w + 1) * LANES : (2 * w + 2) * LANES] - stiff * old[-1])
        divisor = 1.0 + STEP_HALF * stiff
        mid = sum(quad_weights[0][b] * source[b] for b in range(z.nodes))
        mid = (mid + old[0] + STEP_HALF * stiff * old[1]) / divisor
        end = sum(quad_weights[1][b] * source[b] for b in range(z.nodes))
        end = end + mid + STEP_HALF * stiff * old[2]
        evals.append(old[1])
        evals.append(mid)
        later.append((end, divisor))
        old_of.append(old)
        mid_of.append(mid)

    level_values = matmul_split(mix_from_ref[...], jnp.concatenate(evals, 1))
    for w in range(z.n_wave):
        left = jnp.concatenate(
            [
                level_values[:, (2 * w + e) * LANES : (2 * w + e + 1) * LANES] * slot(w, s)
                for s in range(slots)
                for e in range(2)
            ],
            0,
        ).astype(bf)
        out = matmul_nt(left, legendre(w)[:, :LANES])
        for s in range(slots):
            for e in range(2):
                at = (s * 2 + e) * per_node
                coarse_s[e, pl.ds(w * slots + s, per_node, stride=z.coarse_columns), :] = out[at : at + per_node]

    both_c = 2 * z.coarse_columns
    for a in range(z.levels):
        pieces = [coarse_s[e, a * both_c : (a + 1) * both_c, :].astype(bf) for e in range(2)]
        grid = matmul(coarse_wave_ref[...], jnp.concatenate(pieces, 1))
        product = (grid * grid).astype(bf)
        back = matmul(coarse_quad_ref[a], product)
        for e in range(2):
            coarse_back_s[e, a * both_c : (a + 1) * both_c, :] = back[:, e * LANES : (e + 1) * LANES]

    tends = []
    for w in range(z.n_wave):
        left = jnp.concatenate(
            [
                coarse_back_s[e, pl.ds(w * slots + s, per_node, stride=z.coarse_columns), :].astype(bf)
                for s in range(slots)
                for e in range(2)
            ],
            0,
        )
        out = matmul(left, weighted(w)[:, :LANES])
        for e in range(2):
            total = None
            for s in range(slots):
                at = (s * 2 + e) * per_node
                term = slot(w, s) * out[at : at + per_node]
                total = term if total is None else total + term
            tends.append(total)
    coarse_modes = matmul_split(mix_back_ref[...], jnp.concatenate(tends, 1))
    for w in range(z.n_wave):
        before = coarse_modes[:, 2 * w * LANES : (2 * w + 1) * LANES]
        fresh = coarse_modes[:, (2 * w + 1) * LANES : (2 * w + 2) * LANES]
        end, divisor = later[w]
        end = (end + STEP_HALF * (fresh - before)) / divisor
        change_s[w, :per_node, :] = mid_of[w] - old_of[w][1]
        change_s[w, per_node:, :] = end - old_of[w][2]

    place = lax.axis_index("wave")
    begin = pl.multiple_of(lax.div(lax.axis_index("lev"), 2) * (2 * z.dev_rows), SUBLANES)
    mine = tend_s[place, pl.ds(begin, z.state_rows), :]
    raised = matmul_split(lift_ref[...], change_s[place])
    lane = lax.broadcasted_iota(jnp.int32, (z.state_rows, wide), 1)
    for s in range(slots):
        low = mine if s == 0 else pltpu.roll(mine, wide - s * z.coarse, 1)
        high = pltpu.roll(mine, wide - (z.head + s * z.rest - z.coarse), 1)
        values = jnp.where(lane < z.coarse, low, high)
        for n in range(0, z.dev_rows, 2):
            tend_ref[n // (z.nodes * 2), n // 2 % z.nodes, s] = values[n : n + 2, : z.fine_rows]
        low = raised if s == 0 else pltpu.roll(raised, LANES - s * z.coarse, 1)
        low = jnp.where(lane[: low.shape[0], :LANES] < z.coarse, low, 0.0)
        for n in range(0, low.shape[0], 2):
            a, b = n // (2 * (z.nodes - 1)), n // 2 % (z.nodes - 1)
            corrected_ref[a, b, s] = state_ref[a, b + 1, s] + low[n : n + 2, : z.fine_rows]


def mix_constants(z):
    level, node, part = np.arange(z.levels), np.arange(z.nodes), np.arange(2)

    def pick(index):
        return (np.asarray(index)[:, None] == level[None, :]).astype(np.float32)

    def grid(*axes):
        return [m.reshape(-1) for m in np.meshgrid(*axes, indexing="ij")]

    def ordered(index, core):
        lev, inner = index // z.lev_dev, index % z.lev_dev
        return (lev ^ core) * z.lev_dev + inner

    def thrice(matrix):
        return np.concatenate([matrix] * 3, -1)

    rb, rq, rc = grid(node, level, part)
    ca, cb, cc = grid(level, node, part)
    sa, sc = grid(level, part)
    to_mask = (rb[:, None] == cb[None]) & (rc[:, None] == cc[None])
    same_part = sc[:, None] == sc[None]
    la, lb, lc = grid(np.arange(z.lev_dev), np.arange(z.nodes - 1), part)
    kb, kq, kc = grid(np.arange(z.nodes - 1), level, part)
    lift_mask = (lb[:, None] == kb[None]) & (lc[:, None] == kc[None])
    by_core = range(2)
    constants = (
        pick(rq),
        np.stack([thrice(pick(ordered(ca, k)).T) for k in by_core]),
        thrice(to_mask),
        np.stack([pick(ordered(sa, k)) for k in by_core]),
        thrice(pick(sa).T),
        thrice(same_part),
        pick(sa),
        np.stack([thrice(pick(ordered(sa, k)).T) for k in by_core]),
        np.stack([pick(k * z.lev_dev + la) for k in range(z.n_lev)]),
        thrice(pick(kq).T),
        thrice(lift_mask),
    )
    return [jnp.asarray(c, jnp.float32) for c in constants]


def replicated_plan(
    fine_state, fold_pairs, legendre, gauss_weights, grid_coef, modes_from, modes_to, mode_rates
):
    z = Sizes(fine_state, legendre)
    bf, f32 = jnp.bfloat16, jnp.float32
    longitudes = grid_coef.shape[1]
    vmem = pl.BlockSpec(memory_space=pltpu.VMEM)
    smem = pl.BlockSpec(memory_space=pltpu.SMEM)
    shape = jax.ShapeDtypeStruct
    stored = jnp.swapaxes(fine_state, 2, 3)
    block = pl.pallas_call(
        functools.partial(pack_kernel, z),
        out_shape=shape((z.chips, z.block_rows, LANES), bf),
        in_specs=[vmem] * 3,
        out_specs=vmem,
        scratch_shapes=[pltpu.VMEM((z.slots, z.state_rows, z.fine_rows), f32)],
        name="pack",
        compiler_params=pltpu.CompilerParams(vmem_limit_bytes=VMEM_BYTES),
    )(stored, legendre, gauss_weights[None])
    groups = [[2 * i + c for i in range(z.chips)] for c in range(2)]
    own = lax.all_to_all(
        block, ("wave", "lev"), 0, 0, tiled=True, axis_index_groups=groups
    )
    fine_amp, coarse_amp = z.fine_width**-0.5, z.coarse**-0.5
    basis = wave_rows(z.fine_width, longitudes, fine_amp)
    spread = interpolation(z.points, longitudes, 2 * (z.fine_width - 1))
    spread *= 2.0 * z.fine_width / longitudes
    coarse_spread = interpolation(z.coarse_points, longitudes, 2 * (z.coarse - 1))
    coarse_spread *= 2.0 * z.coarse / (longitudes // 2) * (coarse_amp / fine_amp)
    coarse_spread[1::2] = 0.0
    sampled = wave_rows(z.fine_width, z.points, fine_amp).T
    coarse_sampled = wave_rows(z.coarse, z.coarse_points, coarse_amp).T
    constants = [jnp.asarray(c, bf) for c in (basis, spread, coarse_spread, sampled, coarse_sampled)]
    mixes = mix_constants(z)
    wide = 2 * LANES
    n_lift = z.lev_dev * (z.nodes - 1) * 2
    tables = pl.pallas_call(
        functools.partial(tables_kernel, z),
        out_shape=(
            shape((z.points, 2 * z.fine_columns), bf),
            shape((z.levels, 2 * z.fine_columns, z.points), bf),
            shape((z.coarse_points, 2 * z.coarse_columns), bf),
            shape((z.levels, 2 * z.coarse_columns, z.coarse_points), bf),
            shape((z.rows, 3 * z.rows), bf),
            shape((z.per_node, 3 * z.per_node), bf),
            shape((z.per_node, 3 * z.per_node), bf),
            shape((n_lift, 3 * (z.nodes - 1) * z.per_node), bf),
            shape((z.fine_columns, wide), f32),
            shape((z.coarse_columns, LANES), f32),
            shape((z.n_wave, LANES), f32),
            shape((z.n_wave, z.per_node, LANES), f32),
        ),
        in_specs=[smem, smem] + [vmem] * (4 + len(constants) + len(mixes)),
        out_specs=(vmem,) * 12,
        scratch_shapes=[
            pltpu.VMEM((z.levels * 2 * z.fine_width, longitudes), bf),
            pltpu.VMEM((z.levels * 2 * z.coarse, longitudes), bf),
        ],
        compiler_params=pltpu.CompilerParams(vmem_limit_bytes=VMEM_BYTES),
        cost_estimate=pl.CostEstimate(flops=10**9, bytes_accessed=4 * 10**6, transcendentals=0),
        name="tables",
    )(mode_rates, fold_pairs, fold_pairs[None], grid_coef, modes_to, modes_from, *constants, *mixes)

    own, *tables = lax.optimization_barrier((own, *tables))
    other = lax.ppermute(own, ("wave", "lev"), [(i, i ^ 1) for i in range(2 * z.chips)])

    lat_rows = round_up(z.n_lev * z.lats, LANES)
    corrected, fine_tend = pl.pallas_call(
        functools.partial(sweep_kernel, z),
        out_shape=(
            shape((z.lev_dev, z.nodes - 1, z.slots, 2, z.fine_rows), f32),
            shape(stored.shape, f32),
        ),
        in_specs=[vmem] * 15,
        out_specs=(vmem, vmem),
        scratch_shapes=[
            pltpu.VMEM((z.n_wave, lat_rows, wide), f32),
            pltpu.VMEM((z.n_wave, z.rows, wide), f32),
            pltpu.VMEM((z.rows * z.fine_columns, lat_rows), f32),
            pltpu.VMEM((z.rows * z.fine_columns, lat_rows), f32),
            pltpu.VMEM((z.n_wave, z.rows + SUBLANES, wide), f32),
            pltpu.VMEM((2, z.per_node * z.coarse_columns, lat_rows), f32),
            pltpu.VMEM((2, z.per_node * z.coarse_columns, lat_rows), f32),
            pltpu.VMEM((z.n_wave, (z.nodes - 1) * z.per_node, LANES), f32),
        ],
        compiler_params=pltpu.CompilerParams(vmem_limit_bytes=VMEM_BYTES),
        name="sweep",
    )(own, other, stored, *tables)
    return (jnp.swapaxes(corrected, 2, 3), jnp.swapaxes(fine_tend, 2, 3))


def fits_replicated(fine_state, legendre):
    n_wave, n_lev = lax.axis_size("wave"), lax.axis_size("lev")
    if n_lev % 2 or fine_state.shape[1] != len(quad_weights[0]):
        return False
    z = Sizes(fine_state, legendre)
    gathered = 32 * n_wave * n_lev * (legendre.size + fine_state.size)
    return (
        z.head <= LANES
        and z.used > LANES
        and z.used + 2 - LANES <= z.unit
        and z.lats % SUBLANES == 0
        and n_lev * z.lats <= LANES
        and gathered <= REPLICATED_BYTES
    )


def per_device(fine_state, fold_pairs, legendre, *rest):
    plan = replicated_plan if fits_replicated(fine_state, legendre) else split_plan
    return plan(fine_state, fold_pairs, legendre, *rest)


def solution(mesh):
    placed = (
        P("lev", None, None, "wave", None),
        P(),
        P("wave", "lev", None),
        P("lev"),
        P(),
        P(),
        P(),
        P(),
    )
    return jax.shard_map(
        per_device,
        mesh=mesh,
        in_specs=placed,
        out_specs=(P("lev", None, None, "wave", None), P("lev", None, None, "wave", None)),
        check_vma=False,
    )
```

```python
import functools
import math

import jax
import jax.numpy as jnp
import numpy as np
from jax import lax
from jax.experimental import pallas as pl
from jax.experimental.pallas import tpu as pltpu
from jax.sharding import PartitionSpec as P

STEP_HALF = 0.5
quad_weights = ((5.0 / 24.0, 1.0 / 3.0, -1.0 / 24.0), (-1.0 / 24.0, 1.0 / 3.0, 5.0 / 24.0))
HIGHEST = lax.Precision.HIGHEST


def fourier_table(waves, points, amplitude):
    steps = jnp.arange(points, dtype=jnp.int32)
    turns = waves[:, :, None] * steps[None, None, :] % points
    angles = turns.astype(jnp.float32) * (2.0 * math.pi / points)
    return jnp.stack([jnp.cos(angles) * amplitude, -jnp.sin(angles) * amplitude]).astype(
        jnp.bfloat16
    )


def fine_rows(small_wave, fine_width):
    row_ids = jnp.arange(fine_width + 1, dtype=jnp.int32)[None, :]
    return row_ids < fine_width - small_wave[:, None]


def coarse_rows(small_wave, coarse):
    row_ids = jnp.arange(coarse, dtype=jnp.int32)[None, :]
    coarse_keep = row_ids < coarse - small_wave[:, None]
    degree = (small_wave[:, None] + row_ids).astype(jnp.float32)
    return (coarse_keep, degree)


def legendre_inverse(spectral, legendre_table, row_mask):
    split_spec = spectral[:, :, :, :, None, :] * row_mask[None, None, None]
    return jnp.einsum(
        "abcpmr,plr->abcpml", split_spec, legendre_table, preferred_element_type=jnp.float32
    ).astype(jnp.bfloat16)


def legendre_forward(returned, legendre_table, row_mask):
    members = jnp.einsum(
        "abcpml,plr->abcpmr", returned, legendre_table, preferred_element_type=jnp.float32
    )
    return jnp.sum(members * row_mask.astype(jnp.float32)[None, None, None], axis=4)


def grid_step(fourier, wave_table, coef, weights, factor):
    grid_field = jnp.einsum(
        "abcpmz,cpmk->abzk", fourier, wave_table, preferred_element_type=jnp.float32
    )
    product = (coef[:, None, None, :] * grid_field * grid_field).astype(jnp.bfloat16)
    returned = jnp.einsum(
        "abzk,cpmk->abcpmz", product, wave_table, preferred_element_type=jnp.float32
    )
    return (returned * (weights * factor)).astype(jnp.bfloat16)


def mix(matrix, values):
    return jnp.einsum("ql,lbcpr->qbcpr", matrix, values, precision=HIGHEST)


def split_plan(
    fine_state, fold_pairs, legendre, gauss_weights, grid_coef, modes_from, modes_to, mode_rates
):
    n_wave = lax.axis_size("wave")
    wave_idx = lax.axis_index("wave")
    lev_idx = lax.axis_index("lev")
    lev_dev = fine_state.shape[0]
    pairs_dev = fine_state.shape[3]
    fine_width = fine_state.shape[4] - 1
    coarse = fine_width // 2
    longitudes = grid_coef.shape[1]
    band_size = legendre.shape[1] // n_wave
    small_wave = lax.dynamic_slice_in_dim(fold_pairs, wave_idx * pairs_dev, pairs_dev)
    first_member = fine_rows(small_wave, fine_width)
    member_mask = jnp.stack([first_member, jnp.logical_not(first_member)], 1).astype(jnp.bfloat16)
    coarse_keep, degree = coarse_rows(small_wave, coarse)
    keep_mask = coarse_keep[:, None, :].astype(jnp.bfloat16)
    keep_float = coarse_keep.astype(jnp.float32)
    fine_table = fourier_table(
        jnp.stack([fold_pairs, fine_width - 1 - fold_pairs], 1), longitudes, fine_width ** (-0.5)
    )
    coarse_table = fourier_table(fold_pairs[:, None], longitudes // 2, coarse ** (-0.5))
    coarse_leg = legendre[:, :, :coarse]
    coarse_coef = grid_coef[:, ::2]
    band_gauss = lax.dynamic_slice_in_dim(gauss_weights, wave_idx * band_size, band_size)
    local_to = lax.dynamic_slice_in_dim(modes_to, lev_idx * lev_dev, lev_dev, 1)
    local_from = lax.dynamic_slice_in_dim(modes_from, lev_idx * lev_dev, lev_dev, 1)
    mode_decay = lax.dynamic_slice_in_dim(mode_rates, lev_idx * lev_dev, lev_dev)

    def project(partial_sum):
        return mix(modes_to, partial_sum)

    def coarse_start(modes):
        gathered = lax.all_gather(modes, "lev", axis=0, tiled=True)
        levels = (mix(modes_from, gathered) * keep_float).astype(jnp.bfloat16)
        return legendre_inverse(levels, coarse_leg, keep_mask)

    def coarse_grid_step(fourier):
        return grid_step(
            fourier, coarse_table, coarse_coef, band_gauss, 2.0 * coarse / (longitudes // 2)
        )

    def coarse_finish(returned):
        partial_sum = legendre_forward(returned, coarse_leg, keep_mask)
        return lax.psum_scatter(
            project(partial_sum).astype(jnp.bfloat16), "lev", scatter_dimension=0, tiled=True
        ).astype(jnp.float32)

    def coarse_eval(modes):
        fourier = lax.all_to_all(
            coarse_start(modes), "wave", split_axis=5, concat_axis=3, tiled=True
        )
        returned = lax.all_to_all(
            coarse_grid_step(fourier), "wave", split_axis=3, concat_axis=5, tiled=True
        )
        return coarse_finish(returned)

    restricted = fine_state[..., :coarse] * keep_float
    fine_spec = lax.all_gather(fine_state.astype(jnp.bfloat16), "lev", axis=0, tiled=True)
    fine_fourier = legendre_inverse(fine_spec, legendre, member_mask)
    fine_fourier = lax.all_to_all(fine_fourier, "wave", split_axis=5, concat_axis=3, tiled=True)
    fine_back = lax.all_to_all(
        grid_step(fine_fourier, fine_table, grid_coef, band_gauss, 2.0 * fine_width / longitudes),
        "wave",
        split_axis=3,
        concat_axis=5,
        tiled=True,
    )
    fine_tend = lax.psum_scatter(
        legendre_forward(fine_back, legendre, member_mask).astype(jnp.bfloat16),
        "lev",
        scatter_dimension=0,
        tiled=True,
    ).astype(jnp.float32)
    restricted_tend = fine_tend[..., :coarse] * keep_float
    stacked = jnp.concatenate([restricted, restricted_tend], 1)
    both_modes = lax.psum_scatter(
        mix(local_to, stacked).astype(jnp.bfloat16), "lev", scatter_dimension=0, tiled=True
    ).astype(jnp.float32)
    nodes = fine_state.shape[1]
    old_state = both_modes[:, :nodes]
    old_tend = both_modes[:, nodes:]
    old_coarse = coarse_eval(old_state[:, 1:2])
    stiffness = (
        mode_decay[:, None, None, None]
        * (degree * (degree + 1.0) / (coarse * (coarse + 1.0)))[None, None]
    )
    source = old_tend - stiffness[:, None] * old_state
    integral_mid = (
        quad_weights[0][0] * source[:, 0]
        + quad_weights[0][1] * source[:, 1]
        + quad_weights[0][2] * source[:, 2]
    )
    integral_end = (
        quad_weights[1][0] * source[:, 0]
        + quad_weights[1][1] * source[:, 1]
        + quad_weights[1][2] * source[:, 2]
    )
    divisor = 1.0 + STEP_HALF * stiffness
    next_mid = (old_state[:, 0] + STEP_HALF * stiffness * old_state[:, 1] + integral_mid) / divisor
    coarse_fresh = coarse_eval(next_mid[:, None])
    next_end = (
        next_mid
        + STEP_HALF * (coarse_fresh[:, 0] - old_coarse[:, 0])
        + STEP_HALF * stiffness * old_state[:, 2]
        + integral_end
    ) / divisor
    change = jnp.stack([next_mid - old_state[:, 1], next_end - old_state[:, 2]], 1)
    lifted = lax.psum_scatter(
        mix(local_from, change).astype(jnp.bfloat16), "lev", scatter_dimension=0, tiled=True
    ).astype(jnp.float32)
    corrected = fine_state[:, 1:] + jnp.pad(
        lifted, ((0, 0), (0, 0), (0, 0), (0, 0), (0, fine_width + 1 - coarse))
    )
    return (corrected, fine_tend)


LANES = 128
SUBLANES = 8
REPLICATED_BYTES = 16 * 2**20
VMEM_BYTES = 56 * 10**6


def round_up(value, unit):
    return -(-value // unit) * unit


def interpolation(points, targets, degree):
    offset = (
        2.0 * np.pi * (np.arange(targets)[:, None] / targets - np.arange(points)[None, :] / points)
    )
    order = np.arange(1, degree + 1)
    return (1.0 + 2.0 * np.cos(offset[:, :, None] * order).sum(-1)) / points


def wave_rows(waves, points, amplitude):
    turns = np.arange(waves)[:, None] * np.arange(points)[None, :] % points
    angles = turns * (2.0 * np.pi / points)
    return np.concatenate([np.cos(angles), -np.sin(angles)]) * amplitude


def matmul(a, b):
    return jnp.dot(a, b, preferred_element_type=jnp.float32)


def matmul_nt(a, b):
    return lax.dot_general(a, b, (((1,), (1,)), ((), ())), preferred_element_type=jnp.float32)


def matmul_exact(a, b):
    return jnp.dot(a, b, preferred_element_type=jnp.float32, precision=lax.Precision.HIGHEST)


def high_low(values):
    high = values.astype(jnp.bfloat16)
    return high, (values - high.astype(jnp.float32)).astype(jnp.bfloat16)


def matmul_split(left, right):
    high, low = high_low(right)
    return matmul(left, jnp.concatenate([high, low, high], 0))


class Sizes:
    def __init__(self, fine_state, legendre):
        self.n_wave, self.n_lev = lax.axis_size("wave"), lax.axis_size("lev")
        self.lev_dev, self.nodes, _, self.slots, self.fine_rows = fine_state.shape
        self.lats = legendre.shape[1]
        self.n_pair = self.n_lev // 2
        self.fine_width = self.fine_rows - 1
        self.coarse = self.fine_width // 2
        self.levels = self.n_lev * self.lev_dev
        self.dev_rows = self.lev_dev * self.nodes * 2
        self.rows = self.levels * self.nodes * 2
        self.per_node = self.levels * 2
        self.head = self.slots * self.coarse
        self.rest = self.fine_rows - self.coarse
        self.used = self.slots * self.fine_rows
        self.state_rows = round_up(self.dev_rows, SUBLANES)
        self.groups = (self.lats + self.state_rows) // SUBLANES
        self.unit = LANES // self.groups
        self.block_rows = self.lats + SUBLANES + self.state_rows
        self.chips = self.n_wave * self.n_pair
        self.fine_columns = self.n_wave * self.slots * 2
        self.coarse_columns = self.n_wave * self.slots
        self.points = round_up(4 * (self.fine_width - 1) + 1, 32)
        self.coarse_points = round_up(4 * (self.coarse - 1) + 1, 32)


def parts(z):
    narrow = dict(
        wave=(z.points, 2 * z.fine_columns),
        quad=(z.levels * 2 * z.fine_columns, z.points),
        coarse_wave=(z.coarse_points, 2 * z.coarse_columns),
        coarse_quad=(z.levels * 2 * z.coarse_columns, z.coarse_points),
        mix_to=(z.rows, 3 * z.rows),
        mix_from=(z.per_node, 3 * z.per_node),
        mix_back=(z.per_node, 3 * z.per_node),
        lift=(z.lev_dev * (z.nodes - 1) * 2, 3 * (z.nodes - 1) * z.per_node),
    )
    full = dict(
        member=(z.fine_columns, 2 * LANES),
        slot=(z.coarse_columns, LANES),
        keep=(z.n_wave, LANES),
        stiff=(z.n_wave * z.per_node, LANES),
    )

    def placed(shapes, unit):
        out, at = {}, 0
        for name, (count, columns) in shapes.items():
            out[name] = (at, count, columns)
            at += round_up(count, unit)
        return out, (at, max(columns for _, columns in shapes.values()))

    return placed(narrow, 2 * SUBLANES), placed(full, SUBLANES)


class Table:
    def __init__(self, ref, place):
        self.ref, (self.at, self.count, self.columns) = ref, place

    def get(self, begin=0, count=None):
        begin = self.at + begin
        return self.ref[begin : begin + (count or self.count), : self.columns]

    def put(self, values, begin=0):
        begin = self.at + begin
        self.ref[begin : begin + values.shape[0], : self.columns] = values


def named(z, narrow_ref, full_ref):
    (narrow, _), (full, _) = parts(z)
    tables = {name: Table(narrow_ref, place) for name, place in narrow.items()}
    return tables | {name: Table(full_ref, place) for name, place in full.items()}


def copies_in(sources, targets, sems):
    copies = [
        pltpu.make_async_copy(source, target, sems.at[i])
        for i, (source, target) in enumerate(zip(sources, targets))
    ]
    for copy in copies:
        copy.start()
    return copies


def pack_kernel(z, state_hbm, leg_hbm, gauss_hbm, out_ref, state_ref, leg_ref, gauss_ref, sems, rows_s):
    bf, f32 = jnp.bfloat16, jnp.float32
    copies = copies_in((state_hbm, leg_hbm, gauss_hbm), (state_ref, leg_ref, gauss_ref), sems)
    for copy in copies:
        copy.wait()
    row = lax.broadcasted_iota(jnp.int32, (z.fine_rows, LANES), 0)
    lane = lax.broadcasted_iota(jnp.int32, (z.fine_rows, LANES), 1)
    for a in range(z.lev_dev):
        for b in range(z.nodes):
            n = (a * z.nodes + b) * 2
            for s in range(z.slots):
                rows_s[s, n : n + 2, :] = state_ref[a, b, s]
    if z.state_rows > z.dev_rows:
        for s in range(z.slots):
            rows_s[s, z.dev_rows :, :] = jnp.zeros((z.state_rows - z.dev_rows, z.fine_rows), f32)
    table = jnp.zeros((z.lats, LANES), f32)
    state = jnp.zeros((z.state_rows, LANES), f32)
    extra = jnp.zeros((SUBLANES, LANES), f32)
    for s in range(z.slots):
        target = jnp.where(row < z.coarse, s * z.coarse + row, z.head + s * z.rest + row - z.coarse)
        leg = leg_ref[s].astype(f32)
        spec = rows_s[s]
        place = (target == lane).astype(bf)
        table = table + matmul(leg.astype(bf), place)
        state = state + matmul(spec.astype(bf), place)
        if z.head + (s + 1) * z.rest > LANES:
            for q in range(z.groups):
                at = q * SUBLANES
                part = leg[at : at + SUBLANES] if at < z.lats else spec[at - z.lats : at - z.lats + SUBLANES]
                place = ((target >= LANES) & (target - LANES + q * z.unit == lane)).astype(bf)
                extra = extra + matmul(part.astype(bf), place)
    wide_row = lax.broadcasted_iota(jnp.int32, (SUBLANES, z.lats), 0)
    wide_lane = lax.broadcasted_iota(jnp.int32, (SUBLANES, z.lats), 1)
    out_lane = lax.broadcasted_iota(jnp.int32, (SUBLANES, LANES), 1)
    for q in range(z.lats // SUBLANES):
        chosen = jnp.where(wide_lane == wide_row + q * SUBLANES, gauss_ref[...], 0.0)
        column = jnp.sum(chosen, axis=1, keepdims=True)
        high = column.astype(bf).astype(f32)
        at = q * z.unit + z.used - LANES
        extra = extra + jnp.where(out_lane == at, high, 0.0)
        extra = extra + jnp.where(out_lane == at + 1, column - high, 0.0)
    block = jnp.concatenate([table, extra, state], 0).astype(bf)
    for i in range(z.chips):
        out_ref[i] = block


def mix_matrix(pick_left, matrix, pick_right, mask, cut):
    values = matmul_exact(matmul_exact(pick_left, matrix), pick_right) * mask
    high, low = high_low(values)
    lane = lax.broadcasted_iota(jnp.int32, values.shape, 1)
    return jnp.where(lane < cut, high.astype(jnp.float32), low.astype(jnp.float32)).astype(jnp.bfloat16)


def tables_kernel(z, layout, rate_ref, fold_smem, *refs):
    inputs, outputs, scratch = refs[:9], refs[9:11], refs[11:]
    (scaled_s, low_s, sems), staged = scratch[:3], scratch[3:]
    copies = copies_in(inputs, staged, sems)
    fold_ref, coef_ref, basis_ref, spread_ref, coarse_spread_ref = staged[:5]
    sampled_ref, coarse_sampled_ref, matrices_ref, picks_ref = staged[5:]
    out = named(z, *outputs)
    bf, f32 = jnp.bfloat16, jnp.float32
    lev = lax.axis_index("lev")
    core = lax.rem(lev, 2)
    waves, coarse = z.fine_width, z.coarse
    half = z.fine_columns

    for copy in copies[:3]:
        copy.wait()

    def wave_column(count, per_slot):
        row = lax.broadcasted_iota(jnp.int32, (count, z.coarse_columns), 0)
        lane = lax.broadcasted_iota(jnp.int32, (count, z.coarse_columns), 1)
        inside = (row >= lane * per_slot) & (row < (lane + 1) * per_slot)
        small = jnp.sum(jnp.where(inside, fold_ref[...].astype(f32), 0.0), axis=1, keepdims=True)
        if per_slot == 1:
            return small
        first = lax.broadcasted_iota(jnp.int32, (count, 1), 0) & 1
        return jnp.where(first == 0, small, waves - 1 - small)

    def one_hot(count, per_slot, width):
        column = wave_column(count, per_slot)
        lane = lax.broadcasted_iota(jnp.int32, (count, 2 * width), 1).astype(f32)
        top = (lane == column).astype(f32)
        bottom = (lane == column + width).astype(f32)
        return jnp.concatenate([top, bottom], 0).astype(bf)

    hot = one_hot(half, 2, waves)
    coarse_hot = one_hot(z.coarse_columns, 1, coarse)
    tall, short = 2 * waves, 2 * coarse
    table = basis_ref[...].astype(f32)
    for x in range(z.n_pair):
        for o in range(2):
            for al in range(z.lev_dev):
                a = (2 * x + o) * z.lev_dev + al
                level = (2 * x + (core if o == 0 else 1 - core)) * z.lev_dev + al
                scaled = coef_ref[pl.ds(level, 1), :] * table
                scaled_s[a * tall : (a + 1) * tall, :] = scaled.astype(bf)
                low = jnp.concatenate([scaled[:coarse], scaled[waves : waves + coarse]], 0)
                low_s[a * short : (a + 1) * short, :] = low.astype(bf)
    for copy in copies[3:]:
        copy.wait()
    out["wave"].put(matmul_nt(sampled_ref[...], hot).astype(bf))
    out["coarse_wave"].put(matmul_nt(coarse_sampled_ref[...], coarse_hot).astype(bf))
    quad = matmul(scaled_s[...], spread_ref[...]).astype(bf)
    coarse_quad = matmul(low_s[...], coarse_spread_ref[...]).astype(bf)
    for a in range(z.levels):
        values = matmul(hot, quad[a * tall : (a + 1) * tall]).astype(bf)
        out["quad"].put(values, a * values.shape[0])
        values = matmul(coarse_hot, coarse_quad[a * short : (a + 1) * short]).astype(bf)
        out["coarse_quad"].put(values, a * values.shape[0])

    def pick(name, index=0):
        at, rows, columns = layout[name]
        return picks_ref[pl.ds(pl.multiple_of(at + index * rows, SUBLANES), rows), :columns]

    def mix(left, matrix, right, mask):
        return mix_matrix(left, matrices_ref[matrix], right, mask, right.shape[1] // 3 * 2)

    out["mix_to"].put(mix(pick("to_left"), 1, pick("to_right", core), pick("to_mask")))
    out["mix_from"].put(mix(pick("from_left", core), 0, pick("from_right"), pick("from_mask")))
    out["mix_back"].put(mix(pick("back_left"), 1, pick("back_right", core), pick("from_mask")))
    out["lift"].put(mix(pick("lift_left", lev), 0, pick("lift_right"), pick("lift_mask")))

    wide = 2 * LANES
    lane = lax.broadcasted_iota(jnp.int32, (1, wide), 1)
    lane_slot = jnp.full((1, wide), -1, jnp.int32)
    lane_row = jnp.zeros((1, wide), jnp.int32)
    for s in range(z.slots):
        for begin, width, first in ((s * coarse, coarse, 0), (z.head + s * z.rest, z.rest, coarse)):
            inside = (lane >= begin) & (lane < begin + width)
            lane_slot = jnp.where(inside, s, lane_slot)
            lane_row = jnp.where(inside, lane - begin + first, lane_row)
    rate_row = lax.broadcasted_iota(jnp.int32, (z.per_node, LANES), 0)
    rates = jnp.zeros((z.per_node, LANES), f32)
    for q in range(z.levels):
        rates = jnp.where((rate_row >= 2 * q) & (rate_row < 2 * q + 2), rate_ref[q], rates)
    for w in range(z.n_wave):
        small = jnp.zeros((1, wide), jnp.int32)
        for s in range(z.slots):
            small = jnp.where(lane_slot == s, fold_smem[w * z.slots + s], small)
        first = lane_row < waves - small
        keep = (lane < z.head) & (lane_row < coarse - small)
        out["keep"].put(keep[:, :LANES].astype(f32), w)
        for s in range(z.slots):
            own = lane_slot == s
            at = (w * z.slots + s) * 2
            out["member"].put((own & first).astype(f32), at)
            out["member"].put((own & jnp.logical_not(first)).astype(f32), at + 1)
            out["slot"].put((own & keep)[:, :LANES].astype(f32), w * z.slots + s)
        degree = (small + lane_row)[:, :LANES].astype(f32)
        stiff = rates * (degree * (degree + 1.0) / (coarse * (coarse + 1.0)))
        out["stiff"].put(stiff, w * z.per_node)


def sweep_kernel(
    z,
    own_ref,
    other_ref,
    state_ref,
    narrow_hbm,
    full_hbm,
    corrected_ref,
    tend_ref,
    leg_s,
    state_s,
    fourier_s,
    back_s,
    tend_s,
    coarse_s,
    coarse_back_s,
    change_s,
    narrow_ref,
    full_ref,
    sems,
):
    bf, f32 = jnp.bfloat16, jnp.float32
    slots, rows, lats, per_node = z.slots, z.rows, z.lats, z.per_node
    table = named(z, narrow_ref, full_ref)
    copies = copies_in((full_hbm, narrow_hbm), (full_ref, narrow_ref), sems)
    wide = 2 * LANES
    all_lats = z.n_lev * lats

    def member(w, j):
        return table["member"].get(w * slots * 2 + j, 1)

    def slot(w, s):
        return table["slot"].get(w * slots + s, 1)

    def keep(w):
        return table["keep"].get(w, 1)

    for w in range(z.n_wave):
        for x in range(z.n_pair):
            for o, ref in enumerate((own_ref, other_ref)):
                d = 2 * x + o
                block = ref[w * z.n_pair + x].astype(f32)
                extra = block[lats : lats + SUBLANES]
                leg_s[w, d * lats : (d + 1) * lats, :LANES] = block[:lats]
                state_at = d * z.dev_rows
                begin = lats + SUBLANES
                state_s[w, state_at : state_at + z.dev_rows, :LANES] = block[begin : begin + z.dev_rows]
                for q in range(z.groups):
                    moved = extra if q == 0 else pltpu.roll(extra, LANES - q * z.unit, 1)
                    at = q * SUBLANES
                    if at < lats:
                        leg_s[w, d * lats + at : d * lats + at + SUBLANES, LANES:] = moved
                    else:
                        at = at - lats
                        count = min(SUBLANES, z.dev_rows - at)
                        state_s[w, state_at + at : state_at + at + count, LANES:] = moved[:count]
        if all_lats < leg_s.shape[1]:
            leg_s[w, all_lats:, :] = jnp.zeros((leg_s.shape[1] - all_lats, wide), f32)

    def legendre(w):
        return leg_s[w].astype(bf)

    def weighted(w):
        values = leg_s[w]
        column = values[:, z.used : z.used + 1] + values[:, z.used + 1 : z.used + 2]
        return (values * column).astype(bf)

    copies[0].wait()
    for w in range(z.n_wave):
        state = state_s[w]
        left = jnp.concatenate([state * member(w, j) for j in range(2 * slots)], 0).astype(bf)
        out = matmul_nt(left, legendre(w))
        for j in range(2 * slots):
            fourier_s[pl.ds(w * 2 * slots + j, rows, stride=z.fine_columns), :] = out[j * rows : (j + 1) * rows]

    copies[1].wait()
    both = 2 * z.fine_columns
    for a in range(z.levels):
        pieces = [
            fourier_s[(a * z.nodes + b) * both : (a * z.nodes + b + 1) * both, :].astype(bf)
            for b in range(z.nodes)
        ]
        grid = matmul(table["wave"].get(), jnp.concatenate(pieces, 1))
        product = (grid * grid).astype(bf)
        back = matmul(table["quad"].get(a * both, both), product)
        for b in range(z.nodes):
            back_s[(a * z.nodes + b) * both : (a * z.nodes + b + 1) * both, :] = back[:, b * LANES : (b + 1) * LANES]

    stacked = []
    for w in range(z.n_wave):
        left = jnp.concatenate(
            [
                back_s[pl.ds(w * 2 * slots + j, rows, stride=z.fine_columns), :].astype(bf)
                for j in range(2 * slots)
            ],
            0,
        )
        out = matmul(left, weighted(w))
        total = member(w, 0) * out[:rows]
        for j in range(1, 2 * slots):
            total = total + member(w, j) * out[j * rows : (j + 1) * rows]
        tend_s[w, :rows, :] = total
        stacked.append(state_s[w][:, :LANES] * keep(w))
        stacked.append(total[:, :LANES] * keep(w))

    modes = matmul_split(table["mix_to"].get(), jnp.concatenate(stacked, 1))
    evals, later, old_of, mid_of = [], [], [], []
    for w in range(z.n_wave):
        old, source = [], []
        stiff = table["stiff"].get(w * per_node, per_node)
        for b in range(z.nodes):
            part = modes[b * per_node : (b + 1) * per_node]
            old.append(part[:, 2 * w * LANES : (2 * w + 1) * LANES])
            source.append(part[:, (2 * w + 1) * LANES : (2 * w + 2) * LANES] - stiff * old[-1])
        divisor = 1.0 + STEP_HALF * stiff
        mid = sum(quad_weights[0][b] * source[b] for b in range(z.nodes))
        mid = (mid + old[0] + STEP_HALF * stiff * old[1]) / divisor
        end = sum(quad_weights[1][b] * source[b] for b in range(z.nodes))
        end = end + mid + STEP_HALF * stiff * old[2]
        evals.append(old[1])
        evals.append(mid)
        later.append((end, divisor))
        old_of.append(old)
        mid_of.append(mid)

    level_values = matmul_split(table["mix_from"].get(), jnp.concatenate(evals, 1))
    for w in range(z.n_wave):
        left = jnp.concatenate(
            [
                level_values[:, (2 * w + e) * LANES : (2 * w + e + 1) * LANES] * slot(w, s)
                for s in range(slots)
                for e in range(2)
            ],
            0,
        ).astype(bf)
        out = matmul_nt(left, legendre(w)[:, :LANES])
        for s in range(slots):
            for e in range(2):
                at = (s * 2 + e) * per_node
                coarse_s[e, pl.ds(w * slots + s, per_node, stride=z.coarse_columns), :] = out[at : at + per_node]

    both_c = 2 * z.coarse_columns
    for a in range(z.levels):
        pieces = [coarse_s[e, a * both_c : (a + 1) * both_c, :].astype(bf) for e in range(2)]
        grid = matmul(table["coarse_wave"].get(), jnp.concatenate(pieces, 1))
        product = (grid * grid).astype(bf)
        back = matmul(table["coarse_quad"].get(a * both_c, both_c), product)
        for e in range(2):
            coarse_back_s[e, a * both_c : (a + 1) * both_c, :] = back[:, e * LANES : (e + 1) * LANES]

    tends = []
    for w in range(z.n_wave):
        left = jnp.concatenate(
            [
                coarse_back_s[e, pl.ds(w * slots + s, per_node, stride=z.coarse_columns), :].astype(bf)
                for s in range(slots)
                for e in range(2)
            ],
            0,
        )
        out = matmul(left, weighted(w)[:, :LANES])
        for e in range(2):
            total = None
            for s in range(slots):
                at = (s * 2 + e) * per_node
                term = slot(w, s) * out[at : at + per_node]
                total = term if total is None else total + term
            tends.append(total)
    coarse_modes = matmul_split(table["mix_back"].get(), jnp.concatenate(tends, 1))
    for w in range(z.n_wave):
        before = coarse_modes[:, 2 * w * LANES : (2 * w + 1) * LANES]
        fresh = coarse_modes[:, (2 * w + 1) * LANES : (2 * w + 2) * LANES]
        end, divisor = later[w]
        end = (end + STEP_HALF * (fresh - before)) / divisor
        change_s[w, :per_node, :] = mid_of[w] - old_of[w][1]
        change_s[w, per_node:, :] = end - old_of[w][2]

    place = lax.axis_index("wave")
    begin = pl.multiple_of(lax.div(lax.axis_index("lev"), 2) * (2 * z.dev_rows), SUBLANES)
    mine = tend_s[place, pl.ds(begin, z.state_rows), :]
    raised = matmul_split(table["lift"].get(), change_s[place])
    lane = lax.broadcasted_iota(jnp.int32, (z.state_rows, wide), 1)
    for s in range(slots):
        low = mine if s == 0 else pltpu.roll(mine, wide - s * z.coarse, 1)
        high = pltpu.roll(mine, wide - (z.head + s * z.rest - z.coarse), 1)
        values = jnp.where(lane < z.coarse, low, high)
        for n in range(0, z.dev_rows, 2):
            tend_ref[n // (z.nodes * 2), n // 2 % z.nodes, s] = values[n : n + 2, : z.fine_rows]
        low = raised if s == 0 else pltpu.roll(raised, LANES - s * z.coarse, 1)
        low = jnp.where(lane[: low.shape[0], :LANES] < z.coarse, low, 0.0)
        for n in range(0, low.shape[0], 2):
            a, b = n // (2 * (z.nodes - 1)), n // 2 % (z.nodes - 1)
            corrected_ref[a, b, s] = state_ref[a, b + 1, s] + low[n : n + 2, : z.fine_rows]


def mix_constants(z):
    level, node, part = np.arange(z.levels), np.arange(z.nodes), np.arange(2)

    def pick(index):
        return (np.asarray(index)[:, None] == level[None, :]).astype(np.float32)

    def grid(*axes):
        return [m.reshape(-1) for m in np.meshgrid(*axes, indexing="ij")]

    def ordered(index, core):
        lev, inner = index // z.lev_dev, index % z.lev_dev
        return (lev ^ core) * z.lev_dev + inner

    def thrice(matrix):
        return np.concatenate([matrix] * 3, -1)

    rb, rq, rc = grid(node, level, part)
    ca, cb, cc = grid(level, node, part)
    sa, sc = grid(level, part)
    to_mask = (rb[:, None] == cb[None]) & (rc[:, None] == cc[None])
    same_part = sc[:, None] == sc[None]
    la, lb, lc = grid(np.arange(z.lev_dev), np.arange(z.nodes - 1), part)
    kb, kq, kc = grid(np.arange(z.nodes - 1), level, part)
    lift_mask = (lb[:, None] == kb[None]) & (lc[:, None] == kc[None])
    by_core = range(2)
    constants = dict(
        to_left=[pick(rq)],
        to_right=[thrice(pick(ordered(ca, k)).T) for k in by_core],
        to_mask=[thrice(to_mask)],
        from_left=[pick(ordered(sa, k)) for k in by_core],
        from_right=[thrice(pick(sa).T)],
        from_mask=[thrice(same_part)],
        back_left=[pick(sa)],
        back_right=[thrice(pick(ordered(sa, k)).T) for k in by_core],
        lift_left=[pick(k * z.lev_dev + la) for k in range(z.n_lev)],
        lift_right=[thrice(pick(kq).T)],
        lift_mask=[thrice(lift_mask)],
    )
    wide = max(m[0].shape[1] for m in constants.values())
    layout, rows, at = {}, [], 0
    for name, members in constants.items():
        count, columns = members[0].shape
        height = round_up(count, SUBLANES)
        layout[name] = (at, height, columns)
        at += height * len(members)
        rows += [np.pad(m, ((0, height - count), (0, wide - columns))) for m in members]
    return layout, jnp.asarray(np.concatenate(rows), jnp.float32)


def replicated_plan(
    fine_state, fold_pairs, legendre, gauss_weights, grid_coef, modes_from, modes_to, mode_rates
):
    z = Sizes(fine_state, legendre)
    bf, f32 = jnp.bfloat16, jnp.float32
    longitudes = grid_coef.shape[1]
    vmem = pl.BlockSpec(memory_space=pltpu.VMEM)
    smem = pl.BlockSpec(memory_space=pltpu.SMEM)
    hbm = pl.BlockSpec(memory_space=pltpu.HBM)
    shape = jax.ShapeDtypeStruct
    stored = jnp.swapaxes(fine_state, 2, 3)
    block = pl.pallas_call(
        functools.partial(pack_kernel, z),
        out_shape=shape((z.chips, z.block_rows, LANES), bf),
        in_specs=[hbm] * 3,
        out_specs=vmem,
        scratch_shapes=[
            pltpu.VMEM(stored.shape, f32),
            pltpu.VMEM(legendre.shape, bf),
            pltpu.VMEM((1, z.lats), f32),
            pltpu.SemaphoreType.DMA((3,)),
            pltpu.VMEM((z.slots, z.state_rows, z.fine_rows), f32),
        ],
        name="pack",
    )(stored, legendre, gauss_weights[None])
    groups = [[2 * i + c for i in range(z.chips)] for c in range(2)]
    own = lax.all_to_all(
        block, ("wave", "lev"), 0, 0, tiled=True, axis_index_groups=groups
    )
    fine_amp, coarse_amp = z.fine_width**-0.5, z.coarse**-0.5
    basis = wave_rows(z.fine_width, longitudes, fine_amp)
    spread = interpolation(z.points, longitudes, 2 * (z.fine_width - 1))
    spread *= 2.0 * z.fine_width / longitudes
    coarse_spread = interpolation(z.coarse_points, longitudes, 2 * (z.coarse - 1))
    coarse_spread *= 2.0 * z.coarse / (longitudes // 2) * (coarse_amp / fine_amp)
    coarse_spread[1::2] = 0.0
    sampled = wave_rows(z.fine_width, z.points, fine_amp).T
    coarse_sampled = wave_rows(z.coarse, z.coarse_points, coarse_amp).T
    constants = [jnp.asarray(c, bf) for c in (basis, spread, coarse_spread, sampled, coarse_sampled)]
    layout, picks = mix_constants(z)
    staged = [fold_pairs[None], grid_coef, *constants, jnp.stack([modes_from, modes_to]), picks]
    wide = 2 * LANES
    (_, narrow_shape), (_, full_shape) = parts(z)
    tables = pl.pallas_call(
        functools.partial(tables_kernel, z, layout),
        out_shape=(shape(narrow_shape, bf), shape(full_shape, f32)),
        in_specs=[smem, smem] + [hbm] * len(staged),
        out_specs=(vmem,) * 2,
        scratch_shapes=[
            pltpu.VMEM((z.levels * 2 * z.fine_width, longitudes), bf),
            pltpu.VMEM((z.levels * 2 * z.coarse, longitudes), bf),
            pltpu.SemaphoreType.DMA((len(staged),)),
        ]
        + [pltpu.VMEM(array.shape, array.dtype) for array in staged],
        cost_estimate=pl.CostEstimate(flops=10**9, bytes_accessed=4 * 10**6, transcendentals=0),
        name="tables",
    )(mode_rates, fold_pairs, *staged)

    own, *tables = lax.optimization_barrier((own, *tables))
    other = lax.ppermute(own, ("wave", "lev"), [(i, i ^ 1) for i in range(2 * z.chips)])

    lat_rows = round_up(z.n_lev * z.lats, LANES)
    corrected, fine_tend = pl.pallas_call(
        functools.partial(sweep_kernel, z),
        out_shape=(
            shape((z.lev_dev, z.nodes - 1, z.slots, 2, z.fine_rows), f32),
            shape(stored.shape, f32),
        ),
        in_specs=[vmem] * 3 + [hbm] * 2,
        out_specs=(vmem, vmem),
        scratch_shapes=[
            pltpu.VMEM((z.n_wave, lat_rows, wide), f32),
            pltpu.VMEM((z.n_wave, z.rows, wide), f32),
            pltpu.VMEM((z.rows * z.fine_columns, lat_rows), f32),
            pltpu.VMEM((z.rows * z.fine_columns, lat_rows), f32),
            pltpu.VMEM((z.n_wave, z.rows + SUBLANES, wide), f32),
            pltpu.VMEM((2, z.per_node * z.coarse_columns, lat_rows), f32),
            pltpu.VMEM((2, z.per_node * z.coarse_columns, lat_rows), f32),
            pltpu.VMEM((z.n_wave, (z.nodes - 1) * z.per_node, LANES), f32),
            pltpu.VMEM(narrow_shape, bf),
            pltpu.VMEM(full_shape, f32),
            pltpu.SemaphoreType.DMA((2,)),
        ],
        compiler_params=pltpu.CompilerParams(vmem_limit_bytes=VMEM_BYTES),
        name="sweep",
    )(own, other, stored, *tables)
    return (jnp.swapaxes(corrected, 2, 3), jnp.swapaxes(fine_tend, 2, 3))


def fits_replicated(fine_state, legendre):
    n_wave, n_lev = lax.axis_size("wave"), lax.axis_size("lev")
    if n_lev % 2 or fine_state.shape[1] != len(quad_weights[0]):
        return False
    z = Sizes(fine_state, legendre)
    gathered = 32 * n_wave * n_lev * (legendre.size + fine_state.size)
    return (
        z.head <= LANES
        and z.used > LANES
        and z.used + 2 - LANES <= z.unit
        and z.lats % SUBLANES == 0
        and n_lev * z.lats <= LANES
        and gathered <= REPLICATED_BYTES
    )


def per_device(fine_state, fold_pairs, legendre, *rest):
    plan = replicated_plan if fits_replicated(fine_state, legendre) else split_plan
    return plan(fine_state, fold_pairs, legendre, *rest)


def solution(mesh):
    placed = (
        P("lev", None, None, "wave", None),
        P(),
        P("wave", "lev", None),
        P("lev"),
        P(),
        P(),
        P(),
        P(),
    )
    return jax.shard_map(
        per_device,
        mesh=mesh,
        in_specs=placed,
        out_specs=(P("lev", None, None, "wave", None), P("lev", None, None, "wave", None)),
        check_vma=False,
    )
```

```python
import functools
import math

import jax
import jax.numpy as jnp
import numpy as np
from jax import lax
from jax.experimental import pallas as pl
from jax.experimental.pallas import tpu as pltpu
from jax.sharding import PartitionSpec as P

STEP_HALF = 0.5
quad_weights = ((5.0 / 24.0, 1.0 / 3.0, -1.0 / 24.0), (-1.0 / 24.0, 1.0 / 3.0, 5.0 / 24.0))
HIGHEST = lax.Precision.HIGHEST


def fourier_table(waves, points, amplitude):
    steps = jnp.arange(points, dtype=jnp.int32)
    turns = waves[:, :, None] * steps[None, None, :] % points
    angles = turns.astype(jnp.float32) * (2.0 * math.pi / points)
    return jnp.stack([jnp.cos(angles) * amplitude, -jnp.sin(angles) * amplitude]).astype(
        jnp.bfloat16
    )


def fine_rows(small_wave, fine_width):
    row_ids = jnp.arange(fine_width + 1, dtype=jnp.int32)[None, :]
    return row_ids < fine_width - small_wave[:, None]


def coarse_rows(small_wave, coarse):
    row_ids = jnp.arange(coarse, dtype=jnp.int32)[None, :]
    coarse_keep = row_ids < coarse - small_wave[:, None]
    degree = (small_wave[:, None] + row_ids).astype(jnp.float32)
    return (coarse_keep, degree)


def legendre_inverse(spectral, legendre_table, row_mask):
    split_spec = spectral[:, :, :, :, None, :] * row_mask[None, None, None]
    return jnp.einsum(
        "abcpmr,plr->abcpml", split_spec, legendre_table, preferred_element_type=jnp.float32
    ).astype(jnp.bfloat16)


def legendre_forward(returned, legendre_table, row_mask):
    members = jnp.einsum(
        "abcpml,plr->abcpmr", returned, legendre_table, preferred_element_type=jnp.float32
    )
    return jnp.sum(members * row_mask.astype(jnp.float32)[None, None, None], axis=4)


def grid_step(fourier, wave_table, coef, weights, factor):
    grid_field = jnp.einsum(
        "abcpmz,cpmk->abzk", fourier, wave_table, preferred_element_type=jnp.float32
    )
    product = (coef[:, None, None, :] * grid_field * grid_field).astype(jnp.bfloat16)
    returned = jnp.einsum(
        "abzk,cpmk->abcpmz", product, wave_table, preferred_element_type=jnp.float32
    )
    return (returned * (weights * factor)).astype(jnp.bfloat16)


def mix(matrix, values):
    return jnp.einsum("ql,lbcpr->qbcpr", matrix, values, precision=HIGHEST)


def split_plan(
    fine_state, fold_pairs, legendre, gauss_weights, grid_coef, modes_from, modes_to, mode_rates
):
    n_wave = lax.axis_size("wave")
    wave_idx = lax.axis_index("wave")
    lev_idx = lax.axis_index("lev")
    lev_dev = fine_state.shape[0]
    pairs_dev = fine_state.shape[3]
    fine_width = fine_state.shape[4] - 1
    coarse = fine_width // 2
    longitudes = grid_coef.shape[1]
    band_size = legendre.shape[1] // n_wave
    small_wave = lax.dynamic_slice_in_dim(fold_pairs, wave_idx * pairs_dev, pairs_dev)
    first_member = fine_rows(small_wave, fine_width)
    member_mask = jnp.stack([first_member, jnp.logical_not(first_member)], 1).astype(jnp.bfloat16)
    coarse_keep, degree = coarse_rows(small_wave, coarse)
    keep_mask = coarse_keep[:, None, :].astype(jnp.bfloat16)
    keep_float = coarse_keep.astype(jnp.float32)
    fine_table = fourier_table(
        jnp.stack([fold_pairs, fine_width - 1 - fold_pairs], 1), longitudes, fine_width ** (-0.5)
    )
    coarse_table = fourier_table(fold_pairs[:, None], longitudes // 2, coarse ** (-0.5))
    coarse_leg = legendre[:, :, :coarse]
    coarse_coef = grid_coef[:, ::2]
    band_gauss = lax.dynamic_slice_in_dim(gauss_weights, wave_idx * band_size, band_size)
    local_to = lax.dynamic_slice_in_dim(modes_to, lev_idx * lev_dev, lev_dev, 1)
    local_from = lax.dynamic_slice_in_dim(modes_from, lev_idx * lev_dev, lev_dev, 1)
    mode_decay = lax.dynamic_slice_in_dim(mode_rates, lev_idx * lev_dev, lev_dev)

    def project(partial_sum):
        return mix(modes_to, partial_sum)

    def coarse_start(modes):
        gathered = lax.all_gather(modes, "lev", axis=0, tiled=True)
        levels = (mix(modes_from, gathered) * keep_float).astype(jnp.bfloat16)
        return legendre_inverse(levels, coarse_leg, keep_mask)

    def coarse_grid_step(fourier):
        return grid_step(
            fourier, coarse_table, coarse_coef, band_gauss, 2.0 * coarse / (longitudes // 2)
        )

    def coarse_finish(returned):
        partial_sum = legendre_forward(returned, coarse_leg, keep_mask)
        return lax.psum_scatter(
            project(partial_sum).astype(jnp.bfloat16), "lev", scatter_dimension=0, tiled=True
        ).astype(jnp.float32)

    def coarse_eval(modes):
        fourier = lax.all_to_all(
            coarse_start(modes), "wave", split_axis=5, concat_axis=3, tiled=True
        )
        returned = lax.all_to_all(
            coarse_grid_step(fourier), "wave", split_axis=3, concat_axis=5, tiled=True
        )
        return coarse_finish(returned)

    restricted = fine_state[..., :coarse] * keep_float
    fine_spec = lax.all_gather(fine_state.astype(jnp.bfloat16), "lev", axis=0, tiled=True)
    fine_fourier = legendre_inverse(fine_spec, legendre, member_mask)
    fine_fourier = lax.all_to_all(fine_fourier, "wave", split_axis=5, concat_axis=3, tiled=True)
    fine_back = lax.all_to_all(
        grid_step(fine_fourier, fine_table, grid_coef, band_gauss, 2.0 * fine_width / longitudes),
        "wave",
        split_axis=3,
        concat_axis=5,
        tiled=True,
    )
    fine_tend = lax.psum_scatter(
        legendre_forward(fine_back, legendre, member_mask).astype(jnp.bfloat16),
        "lev",
        scatter_dimension=0,
        tiled=True,
    ).astype(jnp.float32)
    restricted_tend = fine_tend[..., :coarse] * keep_float
    stacked = jnp.concatenate([restricted, restricted_tend], 1)
    both_modes = lax.psum_scatter(
        mix(local_to, stacked).astype(jnp.bfloat16), "lev", scatter_dimension=0, tiled=True
    ).astype(jnp.float32)
    nodes = fine_state.shape[1]
    old_state = both_modes[:, :nodes]
    old_tend = both_modes[:, nodes:]
    old_coarse = coarse_eval(old_state[:, 1:2])
    stiffness = (
        mode_decay[:, None, None, None]
        * (degree * (degree + 1.0) / (coarse * (coarse + 1.0)))[None, None]
    )
    source = old_tend - stiffness[:, None] * old_state
    integral_mid = (
        quad_weights[0][0] * source[:, 0]
        + quad_weights[0][1] * source[:, 1]
        + quad_weights[0][2] * source[:, 2]
    )
    integral_end = (
        quad_weights[1][0] * source[:, 0]
        + quad_weights[1][1] * source[:, 1]
        + quad_weights[1][2] * source[:, 2]
    )
    divisor = 1.0 + STEP_HALF * stiffness
    next_mid = (old_state[:, 0] + STEP_HALF * stiffness * old_state[:, 1] + integral_mid) / divisor
    coarse_fresh = coarse_eval(next_mid[:, None])
    next_end = (
        next_mid
        + STEP_HALF * (coarse_fresh[:, 0] - old_coarse[:, 0])
        + STEP_HALF * stiffness * old_state[:, 2]
        + integral_end
    ) / divisor
    change = jnp.stack([next_mid - old_state[:, 1], next_end - old_state[:, 2]], 1)
    lifted = lax.psum_scatter(
        mix(local_from, change).astype(jnp.bfloat16), "lev", scatter_dimension=0, tiled=True
    ).astype(jnp.float32)
    corrected = fine_state[:, 1:] + jnp.pad(
        lifted, ((0, 0), (0, 0), (0, 0), (0, 0), (0, fine_width + 1 - coarse))
    )
    return (corrected, fine_tend)


LANES = 128
SUBLANES = 8
REPLICATED_BYTES = 16 * 2**20
VMEM_BYTES = 56 * 10**6


def round_up(value, unit):
    return -(-value // unit) * unit


def interpolation(points, targets, degree):
    offset = (
        2.0 * np.pi * (np.arange(targets)[:, None] / targets - np.arange(points)[None, :] / points)
    )
    order = np.arange(1, degree + 1)
    return (1.0 + 2.0 * np.cos(offset[:, :, None] * order).sum(-1)) / points


def wave_rows(waves, points, amplitude):
    turns = np.arange(waves)[:, None] * np.arange(points)[None, :] % points
    angles = turns * (2.0 * np.pi / points)
    return np.concatenate([np.cos(angles), -np.sin(angles)]) * amplitude


def matmul(a, b):
    return jnp.dot(a, b, preferred_element_type=jnp.float32)


def matmul_nt(a, b):
    return lax.dot_general(a, b, (((1,), (1,)), ((), ())), preferred_element_type=jnp.float32)


def matmul_exact(a, b):
    return jnp.dot(a, b, preferred_element_type=jnp.float32, precision=lax.Precision.HIGHEST)


def high_low(values):
    high = values.astype(jnp.bfloat16)
    return high, (values - high.astype(jnp.float32)).astype(jnp.bfloat16)


def matmul_split(left, right):
    high, low = high_low(right)
    return matmul(left, jnp.concatenate([high, low, high], 0))


class Sizes:
    def __init__(self, fine_state, legendre):
        self.n_wave, self.n_lev = lax.axis_size("wave"), lax.axis_size("lev")
        self.lev_dev, self.nodes, _, self.slots, self.fine_rows = fine_state.shape
        self.lats = legendre.shape[1]
        self.n_pair = self.n_lev // 2
        self.fine_width = self.fine_rows - 1
        self.coarse = self.fine_width // 2
        self.levels = self.n_lev * self.lev_dev
        self.dev_rows = self.lev_dev * self.nodes * 2
        self.rows = self.levels * self.nodes * 2
        self.per_node = self.levels * 2
        self.head = self.slots * self.coarse
        self.rest = self.fine_rows - self.coarse
        self.used = self.slots * self.fine_rows
        self.state_rows = round_up(self.dev_rows, SUBLANES)
        self.groups = (self.lats + self.state_rows) // SUBLANES
        self.unit = LANES // self.groups
        self.block_rows = self.lats + SUBLANES + self.state_rows
        self.chips = self.n_wave * self.n_pair
        self.fine_columns = self.n_wave * self.slots * 2
        self.coarse_columns = self.n_wave * self.slots
        self.points = round_up(4 * (self.fine_width - 1) + 1, 32)
        self.coarse_points = round_up(4 * (self.coarse - 1) + 1, 32)


def parts(z):
    narrow = dict(
        wave=(z.points, 2 * z.fine_columns),
        quad=(z.levels * 2 * z.fine_columns, z.points),
        coarse_wave=(z.coarse_points, 2 * z.coarse_columns),
        coarse_quad=(z.levels * 2 * z.coarse_columns, z.coarse_points),
        mix_to=(z.rows, 3 * z.rows),
        mix_from=(z.per_node, 3 * z.per_node),
        mix_back=(z.per_node, 3 * z.per_node),
        lift=(z.lev_dev * (z.nodes - 1) * 2, 3 * (z.nodes - 1) * z.per_node),
    )
    full = dict(
        member=(z.fine_columns, 2 * LANES),
        slot=(z.coarse_columns, LANES),
        keep=(z.n_wave, LANES),
        stiff=(z.n_wave * z.per_node, LANES),
        inverse=(z.n_wave * z.per_node, LANES),
    )

    def placed(shapes, unit):
        out, at = {}, 0
        for name, (count, columns) in shapes.items():
            out[name] = (at, count, columns)
            at += round_up(count, unit)
        return out, (at, max(columns for _, columns in shapes.values()))

    return placed(narrow, 2 * SUBLANES), placed(full, SUBLANES)


class Table:
    def __init__(self, ref, place):
        self.ref, (self.at, self.count, self.columns) = ref, place

    def get(self, begin=0, count=None):
        begin = self.at + begin
        return self.ref[begin : begin + (count or self.count), : self.columns]

    def put(self, values, begin=0):
        begin = self.at + begin
        self.ref[begin : begin + values.shape[0], : self.columns] = values


def named(z, narrow_ref, full_ref):
    (narrow, _), (full, _) = parts(z)
    tables = {name: Table(narrow_ref, place) for name, place in narrow.items()}
    return tables | {name: Table(full_ref, place) for name, place in full.items()}


def copies_in(sources, targets, sems):
    copies = [
        pltpu.make_async_copy(source, target, sems.at[i])
        for i, (source, target) in enumerate(zip(sources, targets))
    ]
    for copy in copies:
        copy.start()
    return copies


def pack_kernel(z, state_hbm, leg_hbm, gauss_hbm, out_ref, state_ref, leg_ref, gauss_ref, sems, rows_s):
    bf, f32 = jnp.bfloat16, jnp.float32
    copies = copies_in((state_hbm, leg_hbm, gauss_hbm), (state_ref, leg_ref, gauss_ref), sems)
    for copy in copies:
        copy.wait()
    row = lax.broadcasted_iota(jnp.int32, (z.fine_rows, LANES), 0)
    lane = lax.broadcasted_iota(jnp.int32, (z.fine_rows, LANES), 1)
    for a in range(z.lev_dev):
        for b in range(z.nodes):
            n = (a * z.nodes + b) * 2
            for s in range(z.slots):
                rows_s[s, n : n + 2, :] = state_ref[a, b, s]
    if z.state_rows > z.dev_rows:
        for s in range(z.slots):
            rows_s[s, z.dev_rows :, :] = jnp.zeros((z.state_rows - z.dev_rows, z.fine_rows), f32)
    table = jnp.zeros((z.lats, LANES), f32)
    state = jnp.zeros((z.state_rows, LANES), f32)
    extra = jnp.zeros((SUBLANES, LANES), f32)
    for s in range(z.slots):
        target = jnp.where(row < z.coarse, s * z.coarse + row, z.head + s * z.rest + row - z.coarse)
        leg = leg_ref[s].astype(f32)
        spec = rows_s[s]
        place = (target == lane).astype(bf)
        table = table + matmul(leg.astype(bf), place)
        state = state + matmul(spec.astype(bf), place)
        if z.head + (s + 1) * z.rest > LANES:
            for q in range(z.groups):
                at = q * SUBLANES
                part = leg[at : at + SUBLANES] if at < z.lats else spec[at - z.lats : at - z.lats + SUBLANES]
                place = ((target >= LANES) & (target - LANES + q * z.unit == lane)).astype(bf)
                extra = extra + matmul(part.astype(bf), place)
    wide_row = lax.broadcasted_iota(jnp.int32, (SUBLANES, z.lats), 0)
    wide_lane = lax.broadcasted_iota(jnp.int32, (SUBLANES, z.lats), 1)
    out_lane = lax.broadcasted_iota(jnp.int32, (SUBLANES, LANES), 1)
    for q in range(z.lats // SUBLANES):
        chosen = jnp.where(wide_lane == wide_row + q * SUBLANES, gauss_ref[...], 0.0)
        column = jnp.sum(chosen, axis=1, keepdims=True)
        high = column.astype(bf).astype(f32)
        at = q * z.unit + z.used - LANES
        extra = extra + jnp.where(out_lane == at, high, 0.0)
        extra = extra + jnp.where(out_lane == at + 1, column - high, 0.0)
    block = jnp.concatenate([table, extra, state], 0).astype(bf)
    for i in range(z.chips):
        out_ref[i] = block


def mix_matrix(pick_left, matrix, pick_right, mask, cut):
    values = matmul_exact(matmul_exact(pick_left, matrix), pick_right) * mask
    high, low = high_low(values)
    lane = lax.broadcasted_iota(jnp.int32, values.shape, 1)
    return jnp.where(lane < cut, high.astype(jnp.float32), low.astype(jnp.float32)).astype(jnp.bfloat16)


def tables_kernel(z, layout, rate_ref, fold_smem, *refs):
    inputs, outputs, scratch = refs[:10], refs[10:12], refs[12:]
    (scaled_s, sems), staged = scratch[:2], scratch[2:]
    copies = copies_in(inputs, staged, sems)
    fold_ref, coef_ref, basis_ref, spread_ref, coarse_spread_ref = staged[:5]
    sampled_ref, coarse_sampled_ref, from_ref, to_ref, picks_ref = staged[5:]
    out = named(z, *outputs)
    bf, f32 = jnp.bfloat16, jnp.float32
    lev = lax.axis_index("lev")
    core = lax.rem(lev, 2)
    waves, coarse = z.fine_width, z.coarse
    half = z.fine_columns

    for copy in copies[:3]:
        copy.wait()

    def wave_column(count, per_slot):
        row = lax.broadcasted_iota(jnp.int32, (count, z.coarse_columns), 0)
        lane = lax.broadcasted_iota(jnp.int32, (count, z.coarse_columns), 1)
        inside = (row >= lane * per_slot) & (row < (lane + 1) * per_slot)
        small = jnp.sum(jnp.where(inside, fold_ref[...].astype(f32), 0.0), axis=1, keepdims=True)
        if per_slot == 1:
            return small
        first = lax.broadcasted_iota(jnp.int32, (count, 1), 0) & 1
        return jnp.where(first == 0, small, waves - 1 - small)

    def one_hot(count, per_slot, width):
        column = wave_column(count, per_slot)
        lane = lax.broadcasted_iota(jnp.int32, (count, 2 * width), 1).astype(f32)
        extra = width - coarse
        top = lane == jnp.where(column < coarse, column, column + coarse)
        bottom = lane == jnp.where(column < coarse, column + coarse, column + coarse + extra)
        return jnp.concatenate([top.astype(f32), bottom.astype(f32)], 0).astype(bf)

    hot = one_hot(half, 2, waves)
    coarse_hot = one_hot(z.coarse_columns, 1, coarse)
    short, long = 2 * coarse, 2 * (waves - coarse)
    levels = [
        (2 * x + (core if o == 0 else 1 - core)) * z.lev_dev + al
        for x in range(z.n_pair)
        for o in range(2)
        for al in range(z.lev_dev)
    ]
    chunk = 2 * LANES
    for begin in range(0, basis_ref.shape[1], chunk):
        values = basis_ref[:, begin : begin + chunk].astype(f32)
        for a, level in enumerate(levels):
            scaled = coef_ref[pl.ds(level, 1), begin : begin + chunk] * values
            scaled_s[a * short : (a + 1) * short, begin : begin + chunk] = scaled[:short].astype(bf)
            at = z.levels * short + a * long
            scaled_s[at : at + long, begin : begin + chunk] = scaled[short:].astype(bf)
    for copy in copies[3:]:
        copy.wait()
    out["wave"].put(matmul_nt(sampled_ref[...], hot).astype(bf))
    out["coarse_wave"].put(matmul_nt(coarse_sampled_ref[...], coarse_hot).astype(bf))
    coarse_quad = matmul(scaled_s[: z.levels * short, :], coarse_spread_ref[...]).astype(bf)
    quad = matmul(scaled_s[...], spread_ref[...]).astype(bf)
    for a in range(z.levels):
        at = z.levels * short + a * long
        pair = jnp.concatenate([quad[a * short : (a + 1) * short], quad[at : at + long]], 0)
        values = matmul(hot, pair).astype(bf)
        out["quad"].put(values, a * values.shape[0])
        values = matmul(coarse_hot, coarse_quad[a * short : (a + 1) * short]).astype(bf)
        out["coarse_quad"].put(values, a * values.shape[0])

    def pick(name, index=0):
        at, rows, columns = layout[name]
        return picks_ref[pl.ds(pl.multiple_of(at + index * rows, SUBLANES), rows), :columns]

    def mix(left, matrix, right, mask):
        return mix_matrix(left, matrix[...], right, mask, right.shape[1] // 3 * 2)

    out["mix_to"].put(mix(pick("to_left"), to_ref, pick("to_right", core), pick("to_mask")))
    out["mix_from"].put(mix(pick("from_left", core), from_ref, pick("from_right"), pick("from_mask")))
    out["mix_back"].put(mix(pick("back_left"), to_ref, pick("back_right", core), pick("from_mask")))
    out["lift"].put(mix(pick("lift_left", lev), from_ref, pick("lift_right"), pick("lift_mask")))

    wide = 2 * LANES
    lane = lax.broadcasted_iota(jnp.int32, (1, wide), 1)
    lane_slot = jnp.full((1, wide), -1, jnp.int32)
    lane_row = jnp.zeros((1, wide), jnp.int32)
    for s in range(z.slots):
        for begin, width, first in ((s * coarse, coarse, 0), (z.head + s * z.rest, z.rest, coarse)):
            inside = (lane >= begin) & (lane < begin + width)
            lane_slot = jnp.where(inside, s, lane_slot)
            lane_row = jnp.where(inside, lane - begin + first, lane_row)
    rate_row = lax.broadcasted_iota(jnp.int32, (z.per_node, LANES), 0)
    rates = jnp.zeros((z.per_node, LANES), f32)
    for q in range(z.levels):
        rates = jnp.where((rate_row >= 2 * q) & (rate_row < 2 * q + 2), rate_ref[q], rates)
    for w in range(z.n_wave):
        small = jnp.zeros((1, wide), jnp.int32)
        for s in range(z.slots):
            small = jnp.where(lane_slot == s, fold_smem[w * z.slots + s], small)
        first = lane_row < waves - small
        keep = (lane < z.head) & (lane_row < coarse - small)
        out["keep"].put(keep[:, :LANES].astype(f32), w)
        for s in range(z.slots):
            own = lane_slot == s
            at = (w * z.slots + s) * 2
            out["member"].put((own & first).astype(f32), at)
            out["member"].put((own & jnp.logical_not(first)).astype(f32), at + 1)
            out["slot"].put((own & keep)[:, :LANES].astype(f32), w * z.slots + s)
        degree = (small + lane_row)[:, :LANES].astype(f32)
        stiff = rates * (degree * (degree + 1.0) / (coarse * (coarse + 1.0)))
        out["stiff"].put(stiff, w * z.per_node)
        out["inverse"].put(1.0 / (1.0 + STEP_HALF * stiff), w * z.per_node)


def sweep_kernel(
    z,
    own_ref,
    other_ref,
    state_ref,
    narrow_hbm,
    full_hbm,
    corrected_ref,
    tend_ref,
    leg_s,
    state_s,
    fourier_s,
    back_s,
    tend_s,
    coarse_s,
    coarse_back_s,
    change_s,
    narrow_ref,
    full_ref,
    sems,
    legendre_s,
    product_s,
    coarse_product_s,
):
    bf, f32 = jnp.bfloat16, jnp.float32
    slots, rows, lats, per_node = z.slots, z.rows, z.lats, z.per_node
    table = named(z, narrow_ref, full_ref)
    copies = copies_in((full_hbm, narrow_hbm), (full_ref, narrow_ref), sems)
    wide = 2 * LANES
    all_lats = z.n_lev * lats

    def member(w, j):
        return table["member"].get(w * slots * 2 + j, 1)

    def slot(w, s):
        return table["slot"].get(w * slots + s, 1)

    def keep(w):
        return table["keep"].get(w, 1)

    for w in range(z.n_wave):
        for x in range(z.n_pair):
            for o, ref in enumerate((own_ref, other_ref)):
                d = 2 * x + o
                block = ref[w * z.n_pair + x].astype(f32)
                extra = block[lats : lats + SUBLANES]
                leg_s[w, d * lats : (d + 1) * lats, :LANES] = block[:lats]
                state_at = d * z.dev_rows
                begin = lats + SUBLANES
                state_s[w, state_at : state_at + z.dev_rows, :LANES] = block[begin : begin + z.dev_rows]
                for q in range(z.groups):
                    moved = extra if q == 0 else pltpu.roll(extra, LANES - q * z.unit, 1)
                    at = q * SUBLANES
                    if at < lats:
                        leg_s[w, d * lats + at : d * lats + at + SUBLANES, LANES:] = moved
                    else:
                        at = at - lats
                        count = min(SUBLANES, z.dev_rows - at)
                        state_s[w, state_at + at : state_at + at + count, LANES:] = moved[:count]
        if all_lats < leg_s.shape[1]:
            leg_s[w, all_lats:, :] = jnp.zeros((leg_s.shape[1] - all_lats, wide), f32)
        legendre_s[w] = leg_s[w].astype(bf)

    lane = lax.broadcasted_iota(jnp.int32, (2 * SUBLANES, wide), 1)
    picked = ((lane == z.used) | (lane == z.used + 1)).astype(bf)
    gauss = matmul_nt(picked, legendre_s[0])[:1]

    copies[0].wait()
    for w in range(z.n_wave):
        state = state_s[w]
        left = jnp.concatenate([state * member(w, j) for j in range(2 * slots)], 0).astype(bf)
        fourier_s[w * 2 * slots * rows : (w + 1) * 2 * slots * rows, :] = matmul_nt(left, legendre_s[w])

    copies[1].wait()
    both = 2 * z.fine_columns
    half = z.fine_columns
    for a in range(z.levels):
        pieces = []
        for b in range(z.nodes):
            at = (a * z.nodes + b) * 2
            piece = [fourier_s[pl.ds(at + c, half, stride=rows), :] for c in range(2)]
            pieces.append(jnp.concatenate(piece, 0).astype(bf))
        grid = matmul(table["wave"].get(), jnp.concatenate(pieces, 1))
        product_s[a] = (grid * grid).astype(bf)
    for a in range(z.levels):
        back = matmul(table["quad"].get(a * both, both), product_s[a])
        for b in range(z.nodes):
            values = back[:, b * LANES : (b + 1) * LANES] * gauss
            back_s[(a * z.nodes + b) * both : (a * z.nodes + b + 1) * both, :] = values

    stacked = []
    for w in range(z.n_wave):
        left = jnp.concatenate(
            [
                back_s[pl.ds(w * 2 * slots + j, rows, stride=z.fine_columns), :].astype(bf)
                for j in range(2 * slots)
            ],
            0,
        )
        out = matmul(left, legendre_s[w])
        total = out[:rows]
        for j in range(1, 2 * slots):
            total = jnp.where(member(w, j) > 0.5, out[j * rows : (j + 1) * rows], total)
        tend_s[w, :rows, :] = total
        stacked.append(state_s[w][:, :LANES] * keep(w))
        stacked.append(total[:, :LANES] * keep(w))

    modes = matmul_split(table["mix_to"].get(), jnp.concatenate(stacked, 1))
    evals, later, old_of, mid_of = [], [], [], []
    for w in range(z.n_wave):
        old, source = [], []
        stiff = table["stiff"].get(w * per_node, per_node)
        for b in range(z.nodes):
            part = modes[b * per_node : (b + 1) * per_node]
            old.append(part[:, 2 * w * LANES : (2 * w + 1) * LANES])
            source.append(part[:, (2 * w + 1) * LANES : (2 * w + 2) * LANES] - stiff * old[-1])
        inverse = table["inverse"].get(w * per_node, per_node)
        mid = sum(quad_weights[0][b] * source[b] for b in range(z.nodes))
        mid = (mid + old[0] + STEP_HALF * stiff * old[1]) * inverse
        end = sum(quad_weights[1][b] * source[b] for b in range(z.nodes))
        end = end + mid + STEP_HALF * stiff * old[2]
        evals.append(old[1])
        evals.append(mid)
        later.append((end, inverse))
        old_of.append(old)
        mid_of.append(mid)

    level_values = matmul_split(table["mix_from"].get(), jnp.concatenate(evals, 1))
    for w in range(z.n_wave):
        left = jnp.concatenate(
            [
                level_values[:, (2 * w + e) * LANES : (2 * w + e + 1) * LANES] * slot(w, s)
                for s in range(slots)
                for e in range(2)
            ],
            0,
        ).astype(bf)
        out = matmul_nt(left, legendre_s[w, :, :LANES])
        coarse_s[w * slots * 2 * per_node : (w + 1) * slots * 2 * per_node, :] = out

    both_c = 2 * z.coarse_columns
    for a in range(z.levels):
        pieces = []
        for e in range(2):
            at = e * per_node + a * 2
            piece = [
                coarse_s[pl.ds(at + c, z.coarse_columns, stride=2 * per_node), :] for c in range(2)
            ]
            pieces.append(jnp.concatenate(piece, 0).astype(bf))
        grid = matmul(table["coarse_wave"].get(), jnp.concatenate(pieces, 1))
        coarse_product_s[a] = (grid * grid).astype(bf)
    for a in range(z.levels):
        back = matmul(table["coarse_quad"].get(a * both_c, both_c), coarse_product_s[a])
        for e in range(2):
            values = back[:, e * LANES : (e + 1) * LANES] * gauss
            coarse_back_s[e, a * both_c : (a + 1) * both_c, :] = values

    tends = []
    for w in range(z.n_wave):
        left = jnp.concatenate(
            [
                coarse_back_s[e, pl.ds(w * slots + s, per_node, stride=z.coarse_columns), :].astype(bf)
                for s in range(slots)
                for e in range(2)
            ],
            0,
        )
        out = matmul(left, legendre_s[w, :, :LANES])
        for e in range(2):
            total = None
            for s in range(slots):
                at = (s * 2 + e) * per_node
                term = slot(w, s) * out[at : at + per_node]
                total = term if total is None else total + term
            tends.append(total)
    coarse_modes = matmul_split(table["mix_back"].get(), jnp.concatenate(tends, 1))
    for w in range(z.n_wave):
        before = coarse_modes[:, 2 * w * LANES : (2 * w + 1) * LANES]
        fresh = coarse_modes[:, (2 * w + 1) * LANES : (2 * w + 2) * LANES]
        end, inverse = later[w]
        end = (end + STEP_HALF * (fresh - before)) * inverse
        change_s[w, :per_node, :] = mid_of[w] - old_of[w][1]
        change_s[w, per_node:, :] = end - old_of[w][2]

    place = lax.axis_index("wave")
    begin = pl.multiple_of(lax.div(lax.axis_index("lev"), 2) * (2 * z.dev_rows), SUBLANES)
    mine = tend_s[place, pl.ds(begin, z.state_rows), :]
    raised = matmul_split(table["lift"].get(), change_s[place])
    lane = lax.broadcasted_iota(jnp.int32, (z.state_rows, wide), 1)
    for s in range(slots):
        low = mine if s == 0 else pltpu.roll(mine, wide - s * z.coarse, 1)
        high = pltpu.roll(mine, wide - (z.head + s * z.rest - z.coarse), 1)
        values = jnp.where(lane < z.coarse, low, high)
        for n in range(0, z.dev_rows, 2):
            tend_ref[n // (z.nodes * 2), n // 2 % z.nodes, s] = values[n : n + 2, : z.fine_rows]
        low = raised if s == 0 else pltpu.roll(raised, LANES - s * z.coarse, 1)
        low = jnp.where(lane[: low.shape[0], :LANES] < z.coarse, low, 0.0)
        for n in range(0, low.shape[0], 2):
            a, b = n // (2 * (z.nodes - 1)), n // 2 % (z.nodes - 1)
            corrected_ref[a, b, s] = state_ref[a, b + 1, s] + low[n : n + 2, : z.fine_rows]


def mix_constants(z):
    level, node, part = np.arange(z.levels), np.arange(z.nodes), np.arange(2)

    def pick(index):
        return (np.asarray(index)[:, None] == level[None, :]).astype(np.float32)

    def grid(*axes):
        return [m.reshape(-1) for m in np.meshgrid(*axes, indexing="ij")]

    def ordered(index, core):
        lev, inner = index // z.lev_dev, index % z.lev_dev
        return (lev ^ core) * z.lev_dev + inner

    def thrice(matrix):
        return np.concatenate([matrix] * 3, -1)

    rb, rq, rc = grid(node, level, part)
    ca, cb, cc = grid(level, node, part)
    sa, sc = grid(level, part)
    to_mask = (rb[:, None] == cb[None]) & (rc[:, None] == cc[None])
    same_part = sc[:, None] == sc[None]
    la, lb, lc = grid(np.arange(z.lev_dev), np.arange(z.nodes - 1), part)
    kb, kq, kc = grid(np.arange(z.nodes - 1), level, part)
    lift_mask = (lb[:, None] == kb[None]) & (lc[:, None] == kc[None])
    by_core = range(2)
    constants = dict(
        to_left=[pick(rq)],
        to_right=[thrice(pick(ordered(ca, k)).T) for k in by_core],
        to_mask=[thrice(to_mask)],
        from_left=[pick(ordered(sa, k)) for k in by_core],
        from_right=[thrice(pick(sa).T)],
        from_mask=[thrice(same_part)],
        back_left=[pick(sa)],
        back_right=[thrice(pick(ordered(sa, k)).T) for k in by_core],
        lift_left=[pick(k * z.lev_dev + la) for k in range(z.n_lev)],
        lift_right=[thrice(pick(kq).T)],
        lift_mask=[thrice(lift_mask)],
    )
    wide = max(m[0].shape[1] for m in constants.values())
    layout, rows, at = {}, [], 0
    for name, members in constants.items():
        count, columns = members[0].shape
        height = round_up(count, SUBLANES)
        layout[name] = (at, height, columns)
        at += height * len(members)
        rows += [np.pad(m, ((0, height - count), (0, wide - columns))) for m in members]
    return layout, jnp.asarray(np.concatenate(rows), jnp.float32)


def replicated_plan(
    fine_state, fold_pairs, legendre, gauss_weights, grid_coef, modes_from, modes_to, mode_rates
):
    z = Sizes(fine_state, legendre)
    bf, f32 = jnp.bfloat16, jnp.float32
    longitudes = grid_coef.shape[1]
    vmem = pl.BlockSpec(memory_space=pltpu.VMEM)
    smem = pl.BlockSpec(memory_space=pltpu.SMEM)
    hbm = pl.BlockSpec(memory_space=pltpu.HBM)
    shape = jax.ShapeDtypeStruct
    stored = jnp.swapaxes(fine_state, 2, 3)
    block = pl.pallas_call(
        functools.partial(pack_kernel, z),
        out_shape=shape((z.chips, z.block_rows, LANES), bf),
        in_specs=[hbm] * 3,
        out_specs=vmem,
        scratch_shapes=[
            pltpu.VMEM(stored.shape, f32),
            pltpu.VMEM(legendre.shape, bf),
            pltpu.VMEM((1, z.lats), f32),
            pltpu.SemaphoreType.DMA((3,)),
            pltpu.VMEM((z.slots, z.state_rows, z.fine_rows), f32),
        ],
        name="pack",
    )(stored, legendre, gauss_weights[None])
    groups = [[2 * i + c for i in range(z.chips)] for c in range(2)]
    own = lax.all_to_all(
        block, ("wave", "lev"), 0, 0, tiled=True, axis_index_groups=groups
    )
    fine_amp, coarse_amp = z.fine_width**-0.5, z.coarse**-0.5
    order = np.arange(2 * z.fine_width).reshape(2, -1)
    order = np.concatenate([order[:, : z.coarse].reshape(-1), order[:, z.coarse :].reshape(-1)])
    basis = wave_rows(z.fine_width, longitudes, fine_amp)[order]
    spread = interpolation(z.points, longitudes, 2 * (z.fine_width - 1))
    spread *= 2.0 * z.fine_width / longitudes
    coarse_spread = interpolation(z.coarse_points, longitudes, 2 * (z.coarse - 1))
    coarse_spread *= 2.0 * z.coarse / (longitudes // 2) * (coarse_amp / fine_amp)
    coarse_spread[1::2] = 0.0
    sampled = wave_rows(z.fine_width, z.points, fine_amp)[order].T
    coarse_sampled = wave_rows(z.coarse, z.coarse_points, coarse_amp).T
    constants = [jnp.asarray(c, bf) for c in (basis, spread, coarse_spread, sampled, coarse_sampled)]
    layout, picks = mix_constants(z)
    staged = [fold_pairs[None], grid_coef, *constants, modes_from, modes_to, picks]
    wide = 2 * LANES
    (_, narrow_shape), (_, full_shape) = parts(z)
    tables = pl.pallas_call(
        functools.partial(tables_kernel, z, layout),
        out_shape=(shape(narrow_shape, bf), shape(full_shape, f32)),
        in_specs=[smem, smem] + [hbm] * len(staged),
        out_specs=(vmem,) * 2,
        scratch_shapes=[
            pltpu.VMEM((z.levels * 2 * z.fine_width, longitudes), bf),
            pltpu.SemaphoreType.DMA((len(staged),)),
        ]
        + [pltpu.VMEM(array.shape, array.dtype) for array in staged],
        cost_estimate=pl.CostEstimate(flops=10**9, bytes_accessed=4 * 10**6, transcendentals=0),
        name="tables",
    )(mode_rates, fold_pairs, *staged)

    own, *tables = lax.optimization_barrier((own, *tables))
    other = lax.ppermute(own, ("wave", "lev"), [(i, i ^ 1) for i in range(2 * z.chips)])

    lat_rows = round_up(z.n_lev * z.lats, LANES)
    corrected, fine_tend = pl.pallas_call(
        functools.partial(sweep_kernel, z),
        out_shape=(
            shape((z.lev_dev, z.nodes - 1, z.slots, 2, z.fine_rows), f32),
            shape(stored.shape, f32),
        ),
        in_specs=[vmem] * 3 + [hbm] * 2,
        out_specs=(vmem, vmem),
        scratch_shapes=[
            pltpu.VMEM((z.n_wave, lat_rows, wide), f32),
            pltpu.VMEM((z.n_wave, z.rows, wide), f32),
            pltpu.VMEM((z.rows * z.fine_columns, lat_rows), f32),
            pltpu.VMEM((z.rows * z.fine_columns, lat_rows), f32),
            pltpu.VMEM((z.n_wave, z.rows + SUBLANES, wide), f32),
            pltpu.VMEM((2 * z.per_node * z.coarse_columns, lat_rows), f32),
            pltpu.VMEM((2, z.per_node * z.coarse_columns, lat_rows), f32),
            pltpu.VMEM((z.n_wave, (z.nodes - 1) * z.per_node, LANES), f32),
            pltpu.VMEM(narrow_shape, bf),
            pltpu.VMEM(full_shape, f32),
            pltpu.SemaphoreType.DMA((2,)),
            pltpu.VMEM((z.n_wave, lat_rows, wide), bf),
            pltpu.VMEM((z.levels, z.points, z.nodes * LANES), bf),
            pltpu.VMEM((z.levels, z.coarse_points, 2 * LANES), bf),
        ],
        compiler_params=pltpu.CompilerParams(vmem_limit_bytes=VMEM_BYTES),
        name="sweep",
    )(own, other, stored, *tables)
    return (jnp.swapaxes(corrected, 2, 3), jnp.swapaxes(fine_tend, 2, 3))


def fits_replicated(fine_state, legendre):
    n_wave, n_lev = lax.axis_size("wave"), lax.axis_size("lev")
    if n_lev % 2 or fine_state.shape[1] != len(quad_weights[0]):
        return False
    z = Sizes(fine_state, legendre)
    gathered = 32 * n_wave * n_lev * (legendre.size + fine_state.size)
    return (
        z.head <= LANES
        and z.used > LANES
        and z.used + 2 - LANES <= z.unit
        and z.lats % SUBLANES == 0
        and n_lev * z.lats <= LANES
        and gathered <= REPLICATED_BYTES
    )


def per_device(fine_state, fold_pairs, legendre, *rest):
    plan = replicated_plan if fits_replicated(fine_state, legendre) else split_plan
    return plan(fine_state, fold_pairs, legendre, *rest)


def solution(mesh):
    placed = (
        P("lev", None, None, "wave", None),
        P(),
        P("wave", "lev", None),
        P("lev"),
        P(),
        P(),
        P(),
        P(),
    )
    return jax.shard_map(
        per_device,
        mesh=mesh,
        in_specs=placed,
        out_specs=(P("lev", None, None, "wave", None), P("lev", None, None, "wave", None)),
        check_vma=False,
    )
```

```python
import functools
import math

import jax
import jax.numpy as jnp
import numpy as np
from jax import lax
from jax.experimental import pallas as pl
from jax.experimental.pallas import tpu as pltpu
from jax.sharding import PartitionSpec as P

STEP_HALF = 0.5
quad_weights = ((5.0 / 24.0, 1.0 / 3.0, -1.0 / 24.0), (-1.0 / 24.0, 1.0 / 3.0, 5.0 / 24.0))
HIGHEST = lax.Precision.HIGHEST


def fourier_table(waves, points, amplitude):
    steps = jnp.arange(points, dtype=jnp.int32)
    turns = waves[:, :, None] * steps[None, None, :] % points
    angles = turns.astype(jnp.float32) * (2.0 * math.pi / points)
    return jnp.stack([jnp.cos(angles) * amplitude, -jnp.sin(angles) * amplitude]).astype(
        jnp.bfloat16
    )


def fine_rows(small_wave, fine_width):
    row_ids = jnp.arange(fine_width + 1, dtype=jnp.int32)[None, :]
    return row_ids < fine_width - small_wave[:, None]


def coarse_rows(small_wave, coarse):
    row_ids = jnp.arange(coarse, dtype=jnp.int32)[None, :]
    coarse_keep = row_ids < coarse - small_wave[:, None]
    degree = (small_wave[:, None] + row_ids).astype(jnp.float32)
    return (coarse_keep, degree)


def legendre_inverse(spectral, legendre_table, row_mask):
    split_spec = spectral[:, :, :, :, None, :] * row_mask[None, None, None]
    return jnp.einsum(
        "abcpmr,plr->abcpml", split_spec, legendre_table, preferred_element_type=jnp.float32
    ).astype(jnp.bfloat16)


def legendre_forward(returned, legendre_table, row_mask):
    members = jnp.einsum(
        "abcpml,plr->abcpmr", returned, legendre_table, preferred_element_type=jnp.float32
    )
    return jnp.sum(members * row_mask.astype(jnp.float32)[None, None, None], axis=4)


def grid_step(fourier, wave_table, coef, weights, factor):
    grid_field = jnp.einsum(
        "abcpmz,cpmk->abzk", fourier, wave_table, preferred_element_type=jnp.float32
    )
    product = (coef[:, None, None, :] * grid_field * grid_field).astype(jnp.bfloat16)
    returned = jnp.einsum(
        "abzk,cpmk->abcpmz", product, wave_table, preferred_element_type=jnp.float32
    )
    return (returned * (weights * factor)).astype(jnp.bfloat16)


def mix(matrix, values):
    return jnp.einsum("ql,lbcpr->qbcpr", matrix, values, precision=HIGHEST)


def split_plan(
    fine_state, fold_pairs, legendre, gauss_weights, grid_coef, modes_from, modes_to, mode_rates
):
    n_wave = lax.axis_size("wave")
    wave_idx = lax.axis_index("wave")
    lev_idx = lax.axis_index("lev")
    lev_dev = fine_state.shape[0]
    pairs_dev = fine_state.shape[3]
    fine_width = fine_state.shape[4] - 1
    coarse = fine_width // 2
    longitudes = grid_coef.shape[1]
    band_size = legendre.shape[1] // n_wave
    small_wave = lax.dynamic_slice_in_dim(fold_pairs, wave_idx * pairs_dev, pairs_dev)
    first_member = fine_rows(small_wave, fine_width)
    member_mask = jnp.stack([first_member, jnp.logical_not(first_member)], 1).astype(jnp.bfloat16)
    coarse_keep, degree = coarse_rows(small_wave, coarse)
    keep_mask = coarse_keep[:, None, :].astype(jnp.bfloat16)
    keep_float = coarse_keep.astype(jnp.float32)
    fine_table = fourier_table(
        jnp.stack([fold_pairs, fine_width - 1 - fold_pairs], 1), longitudes, fine_width ** (-0.5)
    )
    coarse_table = fourier_table(fold_pairs[:, None], longitudes // 2, coarse ** (-0.5))
    coarse_leg = legendre[:, :, :coarse]
    coarse_coef = grid_coef[:, ::2]
    band_gauss = lax.dynamic_slice_in_dim(gauss_weights, wave_idx * band_size, band_size)
    local_to = lax.dynamic_slice_in_dim(modes_to, lev_idx * lev_dev, lev_dev, 1)
    local_from = lax.dynamic_slice_in_dim(modes_from, lev_idx * lev_dev, lev_dev, 1)
    mode_decay = lax.dynamic_slice_in_dim(mode_rates, lev_idx * lev_dev, lev_dev)

    def project(partial_sum):
        return mix(modes_to, partial_sum)

    def coarse_start(modes):
        gathered = lax.all_gather(modes, "lev", axis=0, tiled=True)
        levels = (mix(modes_from, gathered) * keep_float).astype(jnp.bfloat16)
        return legendre_inverse(levels, coarse_leg, keep_mask)

    def coarse_grid_step(fourier):
        return grid_step(
            fourier, coarse_table, coarse_coef, band_gauss, 2.0 * coarse / (longitudes // 2)
        )

    def coarse_finish(returned):
        partial_sum = legendre_forward(returned, coarse_leg, keep_mask)
        return lax.psum_scatter(
            project(partial_sum).astype(jnp.bfloat16), "lev", scatter_dimension=0, tiled=True
        ).astype(jnp.float32)

    def coarse_eval(modes):
        fourier = lax.all_to_all(
            coarse_start(modes), "wave", split_axis=5, concat_axis=3, tiled=True
        )
        returned = lax.all_to_all(
            coarse_grid_step(fourier), "wave", split_axis=3, concat_axis=5, tiled=True
        )
        return coarse_finish(returned)

    restricted = fine_state[..., :coarse] * keep_float
    fine_spec = lax.all_gather(fine_state.astype(jnp.bfloat16), "lev", axis=0, tiled=True)
    fine_fourier = legendre_inverse(fine_spec, legendre, member_mask)
    fine_fourier = lax.all_to_all(fine_fourier, "wave", split_axis=5, concat_axis=3, tiled=True)
    fine_back = lax.all_to_all(
        grid_step(fine_fourier, fine_table, grid_coef, band_gauss, 2.0 * fine_width / longitudes),
        "wave",
        split_axis=3,
        concat_axis=5,
        tiled=True,
    )
    fine_tend = lax.psum_scatter(
        legendre_forward(fine_back, legendre, member_mask).astype(jnp.bfloat16),
        "lev",
        scatter_dimension=0,
        tiled=True,
    ).astype(jnp.float32)
    restricted_tend = fine_tend[..., :coarse] * keep_float
    stacked = jnp.concatenate([restricted, restricted_tend], 1)
    both_modes = lax.psum_scatter(
        mix(local_to, stacked).astype(jnp.bfloat16), "lev", scatter_dimension=0, tiled=True
    ).astype(jnp.float32)
    nodes = fine_state.shape[1]
    old_state = both_modes[:, :nodes]
    old_tend = both_modes[:, nodes:]
    old_coarse = coarse_eval(old_state[:, 1:2])
    stiffness = (
        mode_decay[:, None, None, None]
        * (degree * (degree + 1.0) / (coarse * (coarse + 1.0)))[None, None]
    )
    source = old_tend - stiffness[:, None] * old_state
    integral_mid = (
        quad_weights[0][0] * source[:, 0]
        + quad_weights[0][1] * source[:, 1]
        + quad_weights[0][2] * source[:, 2]
    )
    integral_end = (
        quad_weights[1][0] * source[:, 0]
        + quad_weights[1][1] * source[:, 1]
        + quad_weights[1][2] * source[:, 2]
    )
    divisor = 1.0 + STEP_HALF * stiffness
    next_mid = (old_state[:, 0] + STEP_HALF * stiffness * old_state[:, 1] + integral_mid) / divisor
    coarse_fresh = coarse_eval(next_mid[:, None])
    next_end = (
        next_mid
        + STEP_HALF * (coarse_fresh[:, 0] - old_coarse[:, 0])
        + STEP_HALF * stiffness * old_state[:, 2]
        + integral_end
    ) / divisor
    change = jnp.stack([next_mid - old_state[:, 1], next_end - old_state[:, 2]], 1)
    lifted = lax.psum_scatter(
        mix(local_from, change).astype(jnp.bfloat16), "lev", scatter_dimension=0, tiled=True
    ).astype(jnp.float32)
    corrected = fine_state[:, 1:] + jnp.pad(
        lifted, ((0, 0), (0, 0), (0, 0), (0, 0), (0, fine_width + 1 - coarse))
    )
    return (corrected, fine_tend)


LANES = 128
SUBLANES = 8
REPLICATED_BYTES = 16 * 2**20
VMEM_BYTES = 56 * 10**6


def round_up(value, unit):
    return -(-value // unit) * unit


def interpolation(points, targets, degree):
    offset = (
        2.0 * np.pi * (np.arange(targets)[:, None] / targets - np.arange(points)[None, :] / points)
    )
    order = np.arange(1, degree + 1)
    return (1.0 + 2.0 * np.cos(offset[:, :, None] * order).sum(-1)) / points


def wave_rows(waves, points, amplitude):
    turns = np.arange(waves)[:, None] * np.arange(points)[None, :] % points
    angles = turns * (2.0 * np.pi / points)
    return np.concatenate([np.cos(angles), -np.sin(angles)]) * amplitude


def matmul(a, b):
    return jnp.dot(a, b, preferred_element_type=jnp.float32)


def matmul_nt(a, b):
    return lax.dot_general(a, b, (((1,), (1,)), ((), ())), preferred_element_type=jnp.float32)


def matmul_exact(a, b):
    return jnp.dot(a, b, preferred_element_type=jnp.float32, precision=lax.Precision.HIGHEST)


def high_low(values):
    high = values.astype(jnp.bfloat16)
    return high, (values - high.astype(jnp.float32)).astype(jnp.bfloat16)


def matmul_split(left, right):
    high, low = high_low(right)
    return matmul(left, jnp.concatenate([high, low, high], 0))


class Sizes:
    def __init__(self, fine_state, legendre):
        self.n_wave, self.n_lev = lax.axis_size("wave"), lax.axis_size("lev")
        self.lev_dev, self.nodes, _, self.slots, self.fine_rows = fine_state.shape
        self.lats = legendre.shape[1]
        self.n_pair = self.n_lev // 2
        self.fine_width = self.fine_rows - 1
        self.coarse = self.fine_width // 2
        self.levels = self.n_lev * self.lev_dev
        self.own_levels = self.n_pair * self.lev_dev
        self.dev_rows = self.lev_dev * self.nodes * 2
        self.rows = self.levels * self.nodes * 2
        self.per_node = self.levels * 2
        self.head = self.slots * self.coarse
        self.rest = self.fine_rows - self.coarse
        self.used = self.slots * self.fine_rows
        self.state_rows = round_up(self.dev_rows, SUBLANES)
        self.groups = (self.lats + self.state_rows) // SUBLANES
        self.unit = LANES // self.groups
        self.block_rows = self.lats + SUBLANES + self.state_rows
        self.chips = self.n_wave * self.n_pair
        lead = self.chips // 2 - 1
        self.order = [lead] + [i for i in range(self.chips) if i != lead]
        self.position = [self.order.index(i) for i in range(self.chips)]
        self.fine_columns = self.n_wave * self.slots * 2
        self.coarse_columns = self.n_wave * self.slots
        self.points = round_up(4 * (self.fine_width - 1) + 1, 32)
        self.coarse_points = round_up(4 * (self.coarse - 1) + 1, 32)


def parts(z):
    narrow = dict(
        wave=(z.points, 2 * z.fine_columns),
        coarse_wave=(z.coarse_points, 2 * z.coarse_columns),
        mix_to=(z.rows, 3 * z.rows),
        mix_from=(z.per_node, 3 * z.per_node),
        mix_back=(z.per_node, 3 * z.per_node),
        lift=(z.lev_dev * (z.nodes - 1) * 2, 3 * (z.nodes - 1) * z.per_node),
    )
    full = dict(
        member=(z.fine_columns, 2 * LANES),
        slot=(z.coarse_columns, LANES),
        keep=(z.n_wave, LANES),
        stiff=(z.n_wave * z.per_node, LANES),
        inverse=(z.n_wave * z.per_node, LANES),
    )

    def placed(shapes, unit):
        out, at = {}, 0
        for name, (count, columns) in shapes.items():
            out[name] = (at, count, columns)
            at += round_up(count, unit)
        return out, (at, max(columns for _, columns in shapes.values()))

    quads = dict(
        quad=(z.own_levels * 2 * z.fine_columns, z.points),
        coarse_quad=(z.own_levels * 2 * z.coarse_columns, z.coarse_points),
    )
    return [placed(shapes, 2 * SUBLANES) for shapes in (narrow, full, quads)]


class Table:
    def __init__(self, ref, place):
        self.ref, (self.at, self.count, self.columns) = ref, place

    def get(self, begin=0, count=None):
        begin = self.at + begin
        return self.ref[begin : begin + (count or self.count), : self.columns]

    def put(self, values, begin=0):
        begin = self.at + begin
        self.ref[begin : begin + values.shape[0], : self.columns] = values


def named(z, *refs):
    tables = {}
    for ref, (places, _) in zip(refs, parts(z)):
        tables |= {name: Table(ref, place) for name, place in places.items()}
    return tables


def copies_in(sources, targets, sems):
    copies = [
        pltpu.make_async_copy(source, target, sems.at[i])
        for i, (source, target) in enumerate(zip(sources, targets))
    ]
    for copy in copies:
        copy.start()
    return copies


def pack_kernel(z, state_hbm, leg_hbm, gauss_hbm, out_ref, state_ref, leg_ref, gauss_ref, sems, rows_s):
    bf, f32 = jnp.bfloat16, jnp.float32
    copies = copies_in((state_hbm, leg_hbm, gauss_hbm), (state_ref, leg_ref, gauss_ref), sems)
    for copy in copies:
        copy.wait()
    row = lax.broadcasted_iota(jnp.int32, (z.fine_rows, LANES), 0)
    lane = lax.broadcasted_iota(jnp.int32, (z.fine_rows, LANES), 1)
    for a in range(z.lev_dev):
        for b in range(z.nodes):
            n = (a * z.nodes + b) * 2
            for s in range(z.slots):
                rows_s[s, n : n + 2, :] = state_ref[a, b, s]
    if z.state_rows > z.dev_rows:
        for s in range(z.slots):
            rows_s[s, z.dev_rows :, :] = jnp.zeros((z.state_rows - z.dev_rows, z.fine_rows), f32)
    table = jnp.zeros((z.lats, LANES), f32)
    state = jnp.zeros((z.state_rows, LANES), f32)
    extra = jnp.zeros((SUBLANES, LANES), f32)
    for s in range(z.slots):
        target = jnp.where(row < z.coarse, s * z.coarse + row, z.head + s * z.rest + row - z.coarse)
        leg = leg_ref[s].astype(f32)
        spec = rows_s[s]
        place = (target == lane).astype(bf)
        table = table + matmul(leg.astype(bf), place)
        state = state + matmul(spec.astype(bf), place)
        if z.head + (s + 1) * z.rest > LANES:
            for q in range(z.groups):
                at = q * SUBLANES
                part = leg[at : at + SUBLANES] if at < z.lats else spec[at - z.lats : at - z.lats + SUBLANES]
                place = ((target >= LANES) & (target - LANES + q * z.unit == lane)).astype(bf)
                extra = extra + matmul(part.astype(bf), place)
    wide_row = lax.broadcasted_iota(jnp.int32, (SUBLANES, z.lats), 0)
    wide_lane = lax.broadcasted_iota(jnp.int32, (SUBLANES, z.lats), 1)
    out_lane = lax.broadcasted_iota(jnp.int32, (SUBLANES, LANES), 1)
    for q in range(z.lats // SUBLANES):
        chosen = jnp.where(wide_lane == wide_row + q * SUBLANES, gauss_ref[...], 0.0)
        column = jnp.sum(chosen, axis=1, keepdims=True)
        high = column.astype(bf).astype(f32)
        at = q * z.unit + z.used - LANES
        extra = extra + jnp.where(out_lane == at, high, 0.0)
        extra = extra + jnp.where(out_lane == at + 1, column - high, 0.0)
    block = jnp.concatenate([table, extra, state], 0).astype(bf)
    for i in range(z.chips):
        out_ref[i] = block


def mix_matrix(pick_left, matrix, pick_right, mask):
    bf, f32 = jnp.bfloat16, jnp.float32
    high, low = high_low(matrix)
    left = pick_left.astype(bf)
    halves = jnp.concatenate([matmul(left, high).astype(bf), matmul(left, low).astype(bf)], 1)
    return (matmul(halves, pick_right.astype(bf)) * mask.astype(f32)).astype(bf)


def tables_kernel(z, layout, rate_ref, fold_smem, *refs):
    inputs, outputs, scratch = refs[:10], refs[10:13], refs[13:]
    (scaled_s, sems), staged = scratch[:2], scratch[2:]
    copies = copies_in(inputs, staged, sems)
    fold_ref, coef_ref, basis_ref, spread_ref, coarse_spread_ref = staged[:5]
    sampled_ref, coarse_sampled_ref, from_ref, to_ref, picks_ref = staged[5:]
    out = named(z, *outputs)
    bf, f32 = jnp.bfloat16, jnp.float32
    lev = lax.axis_index("lev")
    core = lax.rem(lev, 2)
    waves, coarse = z.fine_width, z.coarse
    half = z.fine_columns

    wide = 2 * LANES
    lane = lax.broadcasted_iota(jnp.int32, (1, wide), 1)
    lane_slot = jnp.full((1, wide), -1, jnp.int32)
    lane_row = jnp.zeros((1, wide), jnp.int32)
    for s in range(z.slots):
        for begin, width, first in ((s * coarse, coarse, 0), (z.head + s * z.rest, z.rest, coarse)):
            inside = (lane >= begin) & (lane < begin + width)
            lane_slot = jnp.where(inside, s, lane_slot)
            lane_row = jnp.where(inside, lane - begin + first, lane_row)
    rate_row = lax.broadcasted_iota(jnp.int32, (z.per_node, LANES), 0)
    rates = jnp.zeros((z.per_node, LANES), f32)
    for q in range(z.levels):
        rates = jnp.where((rate_row >= 2 * q) & (rate_row < 2 * q + 2), rate_ref[q], rates)
    for w in range(z.n_wave):
        small = jnp.zeros((1, wide), jnp.int32)
        for s in range(z.slots):
            small = jnp.where(lane_slot == s, fold_smem[w * z.slots + s], small)
        first = lane_row < waves - small
        keep = (lane < z.head) & (lane_row < coarse - small)
        out["keep"].put(keep[:, :LANES].astype(f32), w)
        for s in range(z.slots):
            own = lane_slot == s
            at = (w * z.slots + s) * 2
            out["member"].put((own & first).astype(f32), at)
            out["member"].put((own & jnp.logical_not(first)).astype(f32), at + 1)
            out["slot"].put((own & keep)[:, :LANES].astype(f32), w * z.slots + s)
        degree = (small + lane_row)[:, :LANES].astype(f32)
        stiff = rates * (degree * (degree + 1.0) / (coarse * (coarse + 1.0)))
        out["stiff"].put(stiff, w * z.per_node)
        out["inverse"].put(1.0 / (1.0 + STEP_HALF * stiff), w * z.per_node)

    for copy in copies[:3]:
        copy.wait()

    def wave_column(count, per_slot):
        row = lax.broadcasted_iota(jnp.int32, (count, z.coarse_columns), 0)
        lane = lax.broadcasted_iota(jnp.int32, (count, z.coarse_columns), 1)
        inside = (row >= lane * per_slot) & (row < (lane + 1) * per_slot)
        small = jnp.sum(jnp.where(inside, fold_ref[...].astype(f32), 0.0), axis=1, keepdims=True)
        if per_slot == 1:
            return small
        first = lax.broadcasted_iota(jnp.int32, (count, 1), 0) & 1
        return jnp.where(first == 0, small, waves - 1 - small)

    def one_hot(count, per_slot, width):
        column = wave_column(count, per_slot)
        lane = lax.broadcasted_iota(jnp.int32, (count, 2 * width), 1).astype(f32)
        extra = width - coarse
        top = lane == jnp.where(column < coarse, column, column + coarse)
        bottom = lane == jnp.where(column < coarse, column + coarse, column + coarse + extra)
        return jnp.concatenate([top.astype(f32), bottom.astype(f32)], 0).astype(bf)

    hot = one_hot(half, 2, waves)
    coarse_hot = one_hot(z.coarse_columns, 1, coarse)
    short, long = 2 * coarse, 2 * (waves - coarse)
    levels = [(2 * x + core) * z.lev_dev + al for x in range(z.n_pair) for al in range(z.lev_dev)]
    chunk = 2 * LANES
    for begin in range(0, basis_ref.shape[1], chunk):
        values = basis_ref[:, begin : begin + chunk].astype(f32)
        for a, level in enumerate(levels):
            scaled = coef_ref[pl.ds(level, 1), begin : begin + chunk] * values
            scaled_s[a * short : (a + 1) * short, begin : begin + chunk] = scaled[:short].astype(bf)
            at = z.own_levels * short + a * long
            scaled_s[at : at + long, begin : begin + chunk] = scaled[short:].astype(bf)
    for copy in copies[3:]:
        copy.wait()
    out["wave"].put(matmul_nt(sampled_ref[...], hot).astype(bf))
    out["coarse_wave"].put(matmul_nt(coarse_sampled_ref[...], coarse_hot).astype(bf))
    coarse_quad = matmul(scaled_s[: z.own_levels * short, :], coarse_spread_ref[...]).astype(bf)
    quad = matmul(scaled_s[...], spread_ref[...]).astype(bf)
    for a in range(z.own_levels):
        at = z.own_levels * short + a * long
        pair = jnp.concatenate([quad[a * short : (a + 1) * short], quad[at : at + long]], 0)
        values = matmul(hot, pair).astype(bf)
        out["quad"].put(values, a * values.shape[0])
        values = matmul(coarse_hot, coarse_quad[a * short : (a + 1) * short]).astype(bf)
        out["coarse_quad"].put(values, a * values.shape[0])

    def pick(name, index=0):
        at, rows, columns = layout[name]
        return picks_ref[pl.ds(pl.multiple_of(at + index * rows, SUBLANES), rows), :columns]

    def mix(left, matrix, right, mask):
        return mix_matrix(left, matrix[...], right, mask)

    out["mix_to"].put(mix(pick("to_left"), to_ref, pick("to_right", core), pick("to_mask")))
    out["mix_from"].put(mix(pick("from_left", core), from_ref, pick("from_right"), pick("from_mask")))
    out["mix_back"].put(mix(pick("back_left"), to_ref, pick("back_right", core), pick("from_mask")))
    out["lift"].put(mix(pick("lift_left", lev), from_ref, pick("lift_right"), pick("lift_mask")))


def sweep_kernel(
    z,
    own_ref,
    other_ref,
    state_ref,
    narrow_hbm,
    full_hbm,
    quads_hbm,
    other_quads_hbm,
    corrected_ref,
    tend_ref,
    leg_s,
    state_s,
    fourier_s,
    back_s,
    tend_s,
    coarse_s,
    coarse_back_s,
    change_s,
    narrow_ref,
    full_ref,
    quads_ref,
    other_quads_ref,
    sems,
    legendre_s,
    product_s,
    coarse_product_s,
):
    bf, f32 = jnp.bfloat16, jnp.float32
    slots, rows, lats, per_node = z.slots, z.rows, z.lats, z.per_node
    table = named(z, narrow_ref, full_ref)
    quads = [named(z, *[ref] * 3) for ref in (quads_ref, other_quads_ref)]
    copies = copies_in(
        (full_hbm, narrow_hbm, quads_hbm, other_quads_hbm),
        (full_ref, narrow_ref, quads_ref, other_quads_ref),
        sems,
    )

    def quad(name, a, count):
        lev, inner = a // z.lev_dev, a % z.lev_dev
        return quads[lev % 2][name].get((lev // 2 * z.lev_dev + inner) * count, count)

    wide = 2 * LANES
    all_lats = z.n_lev * lats

    def member(w, j):
        return table["member"].get(w * slots * 2 + j, 1)

    def slot(w, s):
        return table["slot"].get(w * slots + s, 1)

    def keep(w):
        return table["keep"].get(w, 1)

    for w in range(z.n_wave):
        for x in range(z.n_pair):
            for o, ref in enumerate((own_ref, other_ref)):
                d = 2 * x + o
                block = ref[z.position[w * z.n_pair + x]].astype(f32)
                extra = block[lats : lats + SUBLANES]
                leg_s[w, d * lats : (d + 1) * lats, :LANES] = block[:lats]
                state_at = d * z.dev_rows
                begin = lats + SUBLANES
                state_s[w, state_at : state_at + z.dev_rows, :LANES] = block[begin : begin + z.dev_rows]
                for q in range(z.groups):
                    moved = extra if q == 0 else pltpu.roll(extra, LANES - q * z.unit, 1)
                    at = q * SUBLANES
                    if at < lats:
                        leg_s[w, d * lats + at : d * lats + at + SUBLANES, LANES:] = moved
                    else:
                        at = at - lats
                        count = min(SUBLANES, z.dev_rows - at)
                        state_s[w, state_at + at : state_at + at + count, LANES:] = moved[:count]
        if all_lats < leg_s.shape[1]:
            leg_s[w, all_lats:, :] = jnp.zeros((leg_s.shape[1] - all_lats, wide), f32)
        legendre_s[w] = leg_s[w].astype(bf)

    lane = lax.broadcasted_iota(jnp.int32, (2 * SUBLANES, wide), 1)
    picked = ((lane == z.used) | (lane == z.used + 1)).astype(bf)
    gauss = matmul_nt(picked, legendre_s[0])[:1]

    copies[0].wait()
    for w in range(z.n_wave):
        state = state_s[w]
        left = jnp.concatenate([state * member(w, j) for j in range(2 * slots)], 0).astype(bf)
        fourier_s[w * 2 * slots * rows : (w + 1) * 2 * slots * rows, :] = matmul_nt(left, legendre_s[w])

    for copy in copies[1:]:
        copy.wait()
    both = 2 * z.fine_columns
    half = z.fine_columns
    for a in range(z.levels):
        pieces = []
        for b in range(z.nodes):
            at = (a * z.nodes + b) * 2
            piece = [fourier_s[pl.ds(at + c, half, stride=rows), :] for c in range(2)]
            pieces.append(jnp.concatenate(piece, 0).astype(bf))
        grid = matmul(table["wave"].get(), jnp.concatenate(pieces, 1))
        product_s[a] = (grid * grid).astype(bf)
    for a in range(z.levels):
        back = matmul(quad("quad", a, both), product_s[a])
        for b in range(z.nodes):
            values = back[:, b * LANES : (b + 1) * LANES] * gauss
            back_s[(a * z.nodes + b) * both : (a * z.nodes + b + 1) * both, :] = values

    stacked = []
    for w in range(z.n_wave):
        left = jnp.concatenate(
            [
                back_s[pl.ds(w * 2 * slots + j, rows, stride=z.fine_columns), :].astype(bf)
                for j in range(2 * slots)
            ],
            0,
        )
        out = matmul(left, legendre_s[w])
        total = out[:rows]
        for j in range(1, 2 * slots):
            total = jnp.where(member(w, j) > 0.5, out[j * rows : (j + 1) * rows], total)
        tend_s[w, :rows, :] = total
        stacked.append(state_s[w][:, :LANES] * keep(w))
        stacked.append(total[:, :LANES] * keep(w))

    modes = matmul_split(table["mix_to"].get(), jnp.concatenate(stacked, 1))
    evals, later, old_of, mid_of = [], [], [], []
    for w in range(z.n_wave):
        old, source = [], []
        stiff = table["stiff"].get(w * per_node, per_node)
        for b in range(z.nodes):
            part = modes[b * per_node : (b + 1) * per_node]
            old.append(part[:, 2 * w * LANES : (2 * w + 1) * LANES])
            source.append(part[:, (2 * w + 1) * LANES : (2 * w + 2) * LANES] - stiff * old[-1])
        inverse = table["inverse"].get(w * per_node, per_node)
        mid = sum(quad_weights[0][b] * source[b] for b in range(z.nodes))
        mid = (mid + old[0] + STEP_HALF * stiff * old[1]) * inverse
        end = sum(quad_weights[1][b] * source[b] for b in range(z.nodes))
        end = end + mid + STEP_HALF * stiff * old[2]
        evals.append(old[1])
        evals.append(mid)
        later.append((end, inverse))
        old_of.append(old)
        mid_of.append(mid)

    level_values = matmul_split(table["mix_from"].get(), jnp.concatenate(evals, 1))
    for w in range(z.n_wave):
        left = jnp.concatenate(
            [
                level_values[:, (2 * w + e) * LANES : (2 * w + e + 1) * LANES] * slot(w, s)
                for s in range(slots)
                for e in range(2)
            ],
            0,
        ).astype(bf)
        out = matmul_nt(left, legendre_s[w, :, :LANES])
        coarse_s[w * slots * 2 * per_node : (w + 1) * slots * 2 * per_node, :] = out

    both_c = 2 * z.coarse_columns
    for a in range(z.levels):
        pieces = []
        for e in range(2):
            at = e * per_node + a * 2
            piece = [
                coarse_s[pl.ds(at + c, z.coarse_columns, stride=2 * per_node), :] for c in range(2)
            ]
            pieces.append(jnp.concatenate(piece, 0).astype(bf))
        grid = matmul(table["coarse_wave"].get(), jnp.concatenate(pieces, 1))
        coarse_product_s[a] = (grid * grid).astype(bf)
    for a in range(z.levels):
        back = matmul(quad("coarse_quad", a, both_c), coarse_product_s[a])
        for e in range(2):
            values = back[:, e * LANES : (e + 1) * LANES] * gauss
            coarse_back_s[e, a * both_c : (a + 1) * both_c, :] = values

    tends = []
    for w in range(z.n_wave):
        left = jnp.concatenate(
            [
                coarse_back_s[e, pl.ds(w * slots + s, per_node, stride=z.coarse_columns), :].astype(bf)
                for s in range(slots)
                for e in range(2)
            ],
            0,
        )
        out = matmul(left, legendre_s[w, :, :LANES])
        for e in range(2):
            total = None
            for s in range(slots):
                at = (s * 2 + e) * per_node
                term = slot(w, s) * out[at : at + per_node]
                total = term if total is None else total + term
            tends.append(total)
    coarse_modes = matmul_split(table["mix_back"].get(), jnp.concatenate(tends, 1))
    for w in range(z.n_wave):
        before = coarse_modes[:, 2 * w * LANES : (2 * w + 1) * LANES]
        fresh = coarse_modes[:, (2 * w + 1) * LANES : (2 * w + 2) * LANES]
        end, inverse = later[w]
        end = (end + STEP_HALF * (fresh - before)) * inverse
        change_s[w, :per_node, :] = mid_of[w] - old_of[w][1]
        change_s[w, per_node:, :] = end - old_of[w][2]

    place = lax.axis_index("wave")
    begin = pl.multiple_of(lax.div(lax.axis_index("lev"), 2) * (2 * z.dev_rows), SUBLANES)
    mine = tend_s[place, pl.ds(begin, z.state_rows), :]
    raised = matmul_split(table["lift"].get(), change_s[place])
    lane = lax.broadcasted_iota(jnp.int32, (z.state_rows, wide), 1)
    for s in range(slots):
        low = mine if s == 0 else pltpu.roll(mine, wide - s * z.coarse, 1)
        high = pltpu.roll(mine, wide - (z.head + s * z.rest - z.coarse), 1)
        values = jnp.where(lane < z.coarse, low, high)
        for n in range(0, z.dev_rows, 2):
            tend_ref[n // (z.nodes * 2), n // 2 % z.nodes, s] = values[n : n + 2, : z.fine_rows]
        low = raised if s == 0 else pltpu.roll(raised, LANES - s * z.coarse, 1)
        low = jnp.where(lane[: low.shape[0], :LANES] < z.coarse, low, 0.0)
        for n in range(0, low.shape[0], 2):
            a, b = n // (2 * (z.nodes - 1)), n // 2 % (z.nodes - 1)
            corrected_ref[a, b, s] = state_ref[a, b + 1, s] + low[n : n + 2, : z.fine_rows]


def mix_constants(z):
    level, node, part = np.arange(z.levels), np.arange(z.nodes), np.arange(2)

    def pick(index):
        return (np.asarray(index)[:, None] == level[None, :]).astype(np.float32)

    def grid(*axes):
        return [m.reshape(-1) for m in np.meshgrid(*axes, indexing="ij")]

    def ordered(index, core):
        lev, inner = index // z.lev_dev, index % z.lev_dev
        return (lev ^ core) * z.lev_dev + inner

    def thrice(matrix):
        return np.concatenate([matrix] * 3, -1)

    def halves(matrix):
        zero = np.zeros_like(matrix)
        return np.concatenate(
            [np.concatenate([matrix, matrix, zero], 1), np.concatenate([zero, zero, matrix], 1)]
        )

    rb, rq, rc = grid(node, level, part)
    ca, cb, cc = grid(level, node, part)
    sa, sc = grid(level, part)
    to_mask = (rb[:, None] == cb[None]) & (rc[:, None] == cc[None])
    same_part = sc[:, None] == sc[None]
    la, lb, lc = grid(np.arange(z.lev_dev), np.arange(z.nodes - 1), part)
    kb, kq, kc = grid(np.arange(z.nodes - 1), level, part)
    lift_mask = (lb[:, None] == kb[None]) & (lc[:, None] == kc[None])
    by_core = range(2)
    constants = dict(
        to_left=[pick(rq)],
        to_right=[halves(pick(ordered(ca, k)).T) for k in by_core],
        to_mask=[thrice(to_mask)],
        from_left=[pick(ordered(sa, k)) for k in by_core],
        from_right=[halves(pick(sa).T)],
        from_mask=[thrice(same_part)],
        back_left=[pick(sa)],
        back_right=[halves(pick(ordered(sa, k)).T) for k in by_core],
        lift_left=[pick(k * z.lev_dev + la) for k in range(z.n_lev)],
        lift_right=[halves(pick(kq).T)],
        lift_mask=[thrice(lift_mask)],
    )
    wide = max(m[0].shape[1] for m in constants.values())
    layout, rows, at = {}, [], 0
    for name, members in constants.items():
        count, columns = members[0].shape
        height = round_up(count, SUBLANES)
        layout[name] = (at, height, columns)
        at += height * len(members)
        rows += [np.pad(m, ((0, height - count), (0, wide - columns))) for m in members]
    return layout, jnp.asarray(np.concatenate(rows), jnp.float32)


def replicated_plan(
    fine_state, fold_pairs, legendre, gauss_weights, grid_coef, modes_from, modes_to, mode_rates
):
    z = Sizes(fine_state, legendre)
    bf, f32 = jnp.bfloat16, jnp.float32
    longitudes = grid_coef.shape[1]
    vmem = pl.BlockSpec(memory_space=pltpu.VMEM)
    smem = pl.BlockSpec(memory_space=pltpu.SMEM)
    hbm = pl.BlockSpec(memory_space=pltpu.HBM)
    shape = jax.ShapeDtypeStruct
    stored = jnp.swapaxes(fine_state, 2, 3)
    block = pl.pallas_call(
        functools.partial(pack_kernel, z),
        out_shape=shape((z.chips, z.block_rows, LANES), bf),
        in_specs=[hbm] * 3,
        out_specs=vmem,
        scratch_shapes=[
            pltpu.VMEM(stored.shape, f32),
            pltpu.VMEM(legendre.shape, bf),
            pltpu.VMEM((1, z.lats), f32),
            pltpu.SemaphoreType.DMA((3,)),
            pltpu.VMEM((z.slots, z.state_rows, z.fine_rows), f32),
        ],
        name="pack",
    )(stored, legendre, gauss_weights[None])
    groups = [[2 * i + c for i in z.order] for c in range(2)]
    own = lax.all_to_all(
        block, ("wave", "lev"), 0, 0, tiled=True, axis_index_groups=groups
    )
    fine_amp, coarse_amp = z.fine_width**-0.5, z.coarse**-0.5
    order = np.arange(2 * z.fine_width).reshape(2, -1)
    order = np.concatenate([order[:, : z.coarse].reshape(-1), order[:, z.coarse :].reshape(-1)])
    basis = wave_rows(z.fine_width, longitudes, fine_amp)[order]
    spread = interpolation(z.points, longitudes, 2 * (z.fine_width - 1))
    spread *= 2.0 * z.fine_width / longitudes
    coarse_spread = interpolation(z.coarse_points, longitudes, 2 * (z.coarse - 1))
    coarse_spread *= 2.0 * z.coarse / (longitudes // 2) * (coarse_amp / fine_amp)
    coarse_spread[1::2] = 0.0
    sampled = wave_rows(z.fine_width, z.points, fine_amp)[order].T
    coarse_sampled = wave_rows(z.coarse, z.coarse_points, coarse_amp).T
    constants = [jnp.asarray(c, bf) for c in (basis, spread, coarse_spread, sampled, coarse_sampled)]
    layout, picks = mix_constants(z)
    staged = [fold_pairs[None], grid_coef, *constants, modes_from, modes_to, picks]
    wide = 2 * LANES
    narrow_shape, full_shape, quads_shape = [entry[1] for entry in parts(z)]
    narrow, full, quads = pl.pallas_call(
        functools.partial(tables_kernel, z, layout),
        out_shape=(shape(narrow_shape, bf), shape(full_shape, f32), shape(quads_shape, bf)),
        in_specs=[smem, smem] + [hbm] * len(staged),
        out_specs=(vmem,) * 3,
        scratch_shapes=[
            pltpu.VMEM((z.own_levels * 2 * z.fine_width, longitudes), bf),
            pltpu.SemaphoreType.DMA((len(staged),)),
        ]
        + [pltpu.VMEM(array.shape, array.dtype) for array in staged],
        cost_estimate=pl.CostEstimate(flops=10**9, bytes_accessed=4 * 10**6, transcendentals=0),
        name="tables",
    )(mode_rates, fold_pairs, *staged)

    partners = [(i, i ^ 1) for i in range(2 * z.chips)]
    other_quads = lax.ppermute(quads, ("wave", "lev"), partners)
    own, narrow = lax.optimization_barrier((own, narrow))
    other = lax.ppermute(own, ("wave", "lev"), partners)

    lat_rows = round_up(z.n_lev * z.lats, LANES)
    corrected, fine_tend = pl.pallas_call(
        functools.partial(sweep_kernel, z),
        out_shape=(
            shape((z.lev_dev, z.nodes - 1, z.slots, 2, z.fine_rows), f32),
            shape(stored.shape, f32),
        ),
        in_specs=[vmem] * 3 + [hbm] * 4,
        out_specs=(vmem, vmem),
        scratch_shapes=[
            pltpu.VMEM((z.n_wave, lat_rows, wide), f32),
            pltpu.VMEM((z.n_wave, z.rows, wide), f32),
            pltpu.VMEM((z.rows * z.fine_columns, lat_rows), f32),
            pltpu.VMEM((z.rows * z.fine_columns, lat_rows), f32),
            pltpu.VMEM((z.n_wave, z.rows + SUBLANES, wide), f32),
            pltpu.VMEM((2 * z.per_node * z.coarse_columns, lat_rows), f32),
            pltpu.VMEM((2, z.per_node * z.coarse_columns, lat_rows), f32),
            pltpu.VMEM((z.n_wave, (z.nodes - 1) * z.per_node, LANES), f32),
            pltpu.VMEM(narrow_shape, bf),
            pltpu.VMEM(full_shape, f32),
            pltpu.VMEM(quads_shape, bf),
            pltpu.VMEM(quads_shape, bf),
            pltpu.SemaphoreType.DMA((4,)),
            pltpu.VMEM((z.n_wave, lat_rows, wide), bf),
            pltpu.VMEM((z.levels, z.points, z.nodes * LANES), bf),
            pltpu.VMEM((z.levels, z.coarse_points, 2 * LANES), bf),
        ],
        compiler_params=pltpu.CompilerParams(vmem_limit_bytes=VMEM_BYTES),
        name="sweep",
    )(own, other, stored, narrow, full, quads, other_quads)
    return (jnp.swapaxes(corrected, 2, 3), jnp.swapaxes(fine_tend, 2, 3))


def fits_replicated(fine_state, legendre):
    n_wave, n_lev = lax.axis_size("wave"), lax.axis_size("lev")
    if n_lev % 2 or fine_state.shape[1] != len(quad_weights[0]):
        return False
    z = Sizes(fine_state, legendre)
    gathered = 32 * n_wave * n_lev * (legendre.size + fine_state.size)
    return (
        z.head <= LANES
        and z.used > LANES
        and z.used + 2 - LANES <= z.unit
        and z.lats % SUBLANES == 0
        and n_lev * z.lats <= LANES
        and gathered <= REPLICATED_BYTES
    )


def per_device(fine_state, fold_pairs, legendre, *rest):
    plan = replicated_plan if fits_replicated(fine_state, legendre) else split_plan
    return plan(fine_state, fold_pairs, legendre, *rest)


def solution(mesh):
    placed = (
        P("lev", None, None, "wave", None),
        P(),
        P("wave", "lev", None),
        P("lev"),
        P(),
        P(),
        P(),
        P(),
    )
    return jax.shard_map(
        per_device,
        mesh=mesh,
        in_specs=placed,
        out_specs=(P("lev", None, None, "wave", None), P("lev", None, None, "wave", None)),
        check_vma=False,
    )
```

```python
import functools
import math

import jax
import jax.numpy as jnp
import numpy as np
from jax import lax
from jax.experimental import pallas as pl
from jax.experimental.pallas import tpu as pltpu
from jax.sharding import PartitionSpec as P

STEP_HALF = 0.5
quad_weights = ((5.0 / 24.0, 1.0 / 3.0, -1.0 / 24.0), (-1.0 / 24.0, 1.0 / 3.0, 5.0 / 24.0))
HIGHEST = lax.Precision.HIGHEST


def fourier_table(waves, points, amplitude):
    steps = jnp.arange(points, dtype=jnp.int32)
    turns = waves[:, :, None] * steps[None, None, :] % points
    angles = turns.astype(jnp.float32) * (2.0 * math.pi / points)
    return jnp.stack([jnp.cos(angles) * amplitude, -jnp.sin(angles) * amplitude]).astype(
        jnp.bfloat16
    )


def fine_rows(small_wave, fine_width):
    row_ids = jnp.arange(fine_width + 1, dtype=jnp.int32)[None, :]
    return row_ids < fine_width - small_wave[:, None]


def coarse_rows(small_wave, coarse):
    row_ids = jnp.arange(coarse, dtype=jnp.int32)[None, :]
    coarse_keep = row_ids < coarse - small_wave[:, None]
    degree = (small_wave[:, None] + row_ids).astype(jnp.float32)
    return (coarse_keep, degree)


def legendre_inverse(spectral, legendre_table, row_mask):
    split_spec = spectral[:, :, :, :, None, :] * row_mask[None, None, None]
    return jnp.einsum(
        "abcpmr,plr->abcpml", split_spec, legendre_table, preferred_element_type=jnp.float32
    ).astype(jnp.bfloat16)


def legendre_forward(returned, legendre_table, row_mask):
    members = jnp.einsum(
        "abcpml,plr->abcpmr", returned, legendre_table, preferred_element_type=jnp.float32
    )
    return jnp.sum(members * row_mask.astype(jnp.float32)[None, None, None], axis=4)


def grid_step(fourier, wave_table, coef, weights, factor):
    grid_field = jnp.einsum(
        "abcpmz,cpmk->abzk", fourier, wave_table, preferred_element_type=jnp.float32
    )
    product = (coef[:, None, None, :] * grid_field * grid_field).astype(jnp.bfloat16)
    returned = jnp.einsum(
        "abzk,cpmk->abcpmz", product, wave_table, preferred_element_type=jnp.float32
    )
    return (returned * (weights * factor)).astype(jnp.bfloat16)


def mix(matrix, values):
    return jnp.einsum("ql,lbcpr->qbcpr", matrix, values, precision=HIGHEST)


def split_plan(
    fine_state, fold_pairs, legendre, gauss_weights, grid_coef, modes_from, modes_to, mode_rates
):
    n_wave = lax.axis_size("wave")
    wave_idx = lax.axis_index("wave")
    lev_idx = lax.axis_index("lev")
    lev_dev = fine_state.shape[0]
    pairs_dev = fine_state.shape[3]
    fine_width = fine_state.shape[4] - 1
    coarse = fine_width // 2
    longitudes = grid_coef.shape[1]
    band_size = legendre.shape[1] // n_wave
    small_wave = lax.dynamic_slice_in_dim(fold_pairs, wave_idx * pairs_dev, pairs_dev)
    first_member = fine_rows(small_wave, fine_width)
    member_mask = jnp.stack([first_member, jnp.logical_not(first_member)], 1).astype(jnp.bfloat16)
    coarse_keep, degree = coarse_rows(small_wave, coarse)
    keep_mask = coarse_keep[:, None, :].astype(jnp.bfloat16)
    keep_float = coarse_keep.astype(jnp.float32)
    fine_table = fourier_table(
        jnp.stack([fold_pairs, fine_width - 1 - fold_pairs], 1), longitudes, fine_width ** (-0.5)
    )
    coarse_table = fourier_table(fold_pairs[:, None], longitudes // 2, coarse ** (-0.5))
    coarse_leg = legendre[:, :, :coarse]
    coarse_coef = grid_coef[:, ::2]
    band_gauss = lax.dynamic_slice_in_dim(gauss_weights, wave_idx * band_size, band_size)
    local_to = lax.dynamic_slice_in_dim(modes_to, lev_idx * lev_dev, lev_dev, 1)
    local_from = lax.dynamic_slice_in_dim(modes_from, lev_idx * lev_dev, lev_dev, 1)
    mode_decay = lax.dynamic_slice_in_dim(mode_rates, lev_idx * lev_dev, lev_dev)

    def project(partial_sum):
        return mix(modes_to, partial_sum)

    def coarse_start(modes):
        gathered = lax.all_gather(modes, "lev", axis=0, tiled=True)
        levels = (mix(modes_from, gathered) * keep_float).astype(jnp.bfloat16)
        return legendre_inverse(levels, coarse_leg, keep_mask)

    def coarse_grid_step(fourier):
        return grid_step(
            fourier, coarse_table, coarse_coef, band_gauss, 2.0 * coarse / (longitudes // 2)
        )

    def coarse_finish(returned):
        partial_sum = legendre_forward(returned, coarse_leg, keep_mask)
        return lax.psum_scatter(
            project(partial_sum).astype(jnp.bfloat16), "lev", scatter_dimension=0, tiled=True
        ).astype(jnp.float32)

    def coarse_eval(modes):
        fourier = lax.all_to_all(
            coarse_start(modes), "wave", split_axis=5, concat_axis=3, tiled=True
        )
        returned = lax.all_to_all(
            coarse_grid_step(fourier), "wave", split_axis=3, concat_axis=5, tiled=True
        )
        return coarse_finish(returned)

    restricted = fine_state[..., :coarse] * keep_float
    fine_spec = lax.all_gather(fine_state.astype(jnp.bfloat16), "lev", axis=0, tiled=True)
    fine_fourier = legendre_inverse(fine_spec, legendre, member_mask)
    fine_fourier = lax.all_to_all(fine_fourier, "wave", split_axis=5, concat_axis=3, tiled=True)
    fine_back = lax.all_to_all(
        grid_step(fine_fourier, fine_table, grid_coef, band_gauss, 2.0 * fine_width / longitudes),
        "wave",
        split_axis=3,
        concat_axis=5,
        tiled=True,
    )
    fine_tend = lax.psum_scatter(
        legendre_forward(fine_back, legendre, member_mask).astype(jnp.bfloat16),
        "lev",
        scatter_dimension=0,
        tiled=True,
    ).astype(jnp.float32)
    restricted_tend = fine_tend[..., :coarse] * keep_float
    stacked = jnp.concatenate([restricted, restricted_tend], 1)
    both_modes = lax.psum_scatter(
        mix(local_to, stacked).astype(jnp.bfloat16), "lev", scatter_dimension=0, tiled=True
    ).astype(jnp.float32)
    nodes = fine_state.shape[1]
    old_state = both_modes[:, :nodes]
    old_tend = both_modes[:, nodes:]
    old_coarse = coarse_eval(old_state[:, 1:2])
    stiffness = (
        mode_decay[:, None, None, None]
        * (degree * (degree + 1.0) / (coarse * (coarse + 1.0)))[None, None]
    )
    source = old_tend - stiffness[:, None] * old_state
    integral_mid = (
        quad_weights[0][0] * source[:, 0]
        + quad_weights[0][1] * source[:, 1]
        + quad_weights[0][2] * source[:, 2]
    )
    integral_end = (
        quad_weights[1][0] * source[:, 0]
        + quad_weights[1][1] * source[:, 1]
        + quad_weights[1][2] * source[:, 2]
    )
    divisor = 1.0 + STEP_HALF * stiffness
    next_mid = (old_state[:, 0] + STEP_HALF * stiffness * old_state[:, 1] + integral_mid) / divisor
    coarse_fresh = coarse_eval(next_mid[:, None])
    next_end = (
        next_mid
        + STEP_HALF * (coarse_fresh[:, 0] - old_coarse[:, 0])
        + STEP_HALF * stiffness * old_state[:, 2]
        + integral_end
    ) / divisor
    change = jnp.stack([next_mid - old_state[:, 1], next_end - old_state[:, 2]], 1)
    lifted = lax.psum_scatter(
        mix(local_from, change).astype(jnp.bfloat16), "lev", scatter_dimension=0, tiled=True
    ).astype(jnp.float32)
    corrected = fine_state[:, 1:] + jnp.pad(
        lifted, ((0, 0), (0, 0), (0, 0), (0, 0), (0, fine_width + 1 - coarse))
    )
    return (corrected, fine_tend)


LANES = 128
SUBLANES = 8
REPLICATED_BYTES = 16 * 2**20
VMEM_BYTES = 56 * 10**6


def round_up(value, unit):
    return -(-value // unit) * unit


def interpolation(points, targets, degree):
    offset = (
        2.0 * np.pi * (np.arange(targets)[:, None] / targets - np.arange(points)[None, :] / points)
    )
    order = np.arange(1, degree + 1)
    return (1.0 + 2.0 * np.cos(offset[:, :, None] * order).sum(-1)) / points


def wave_rows(waves, points, amplitude):
    turns = np.arange(waves)[:, None] * np.arange(points)[None, :] % points
    angles = turns * (2.0 * np.pi / points)
    return np.concatenate([np.cos(angles), -np.sin(angles)]) * amplitude


def folded(table, side):
    near = table[: table.shape[0] // 2]
    middle = table.shape[1] // 2
    return 0.5 * near[:, :middle] + side * near[:, middle:]


def matmul(a, b):
    return jnp.dot(a, b, preferred_element_type=jnp.float32)


def matmul_nt(a, b):
    return lax.dot_general(a, b, (((1,), (1,)), ((), ())), preferred_element_type=jnp.float32)


def matmul_exact(a, b):
    return jnp.dot(a, b, preferred_element_type=jnp.float32, precision=lax.Precision.HIGHEST)


def high_low(values):
    high = values.astype(jnp.bfloat16)
    return high, (values - high.astype(jnp.float32)).astype(jnp.bfloat16)


def matmul_split(left, right):
    high, low = high_low(right)
    return matmul(left, jnp.concatenate([high, low, high], 0))


class Sizes:
    def __init__(self, fine_state, legendre):
        self.n_wave, self.n_lev = lax.axis_size("wave"), lax.axis_size("lev")
        self.lev_dev, self.nodes, _, self.slots, self.fine_rows = fine_state.shape
        self.lats = legendre.shape[1]
        self.n_pair = self.n_lev // 2
        self.fine_width = self.fine_rows - 1
        self.coarse = self.fine_width // 2
        self.levels = self.n_lev * self.lev_dev
        self.own_levels = self.n_pair * self.lev_dev
        self.dev_rows = self.lev_dev * self.nodes * 2
        self.rows = self.levels * self.nodes * 2
        self.per_node = self.levels * 2
        self.head = self.slots * self.coarse
        self.rest = self.fine_rows - self.coarse
        self.used = self.slots * self.fine_rows
        self.state_rows = round_up(self.dev_rows, SUBLANES)
        self.groups = (self.lats + self.state_rows) // SUBLANES
        self.unit = LANES // self.groups
        self.block_rows = self.lats + SUBLANES + self.state_rows
        self.chips = self.n_wave * self.n_pair
        lead = self.chips // 2 - 1
        self.order = [lead] + [i for i in range(self.chips) if i != lead]
        self.position = [self.order.index(i) for i in range(self.chips)]
        self.fine_columns = self.n_wave * self.slots * 2
        self.coarse_columns = self.n_wave * self.slots
        self.points = round_up(4 * (self.fine_width - 1) + 1, 32)
        self.coarse_points = round_up(4 * (self.coarse - 1) + 1, 32)


def parts(z):
    narrow = dict(
        wave=(z.points, 2 * z.fine_columns),
        coarse_wave=(z.coarse_points, 2 * z.coarse_columns),
        mix_to=(z.rows, 3 * z.rows),
        mix_from=(z.per_node, 3 * z.per_node),
        mix_back=(z.per_node, 3 * z.per_node),
        lift=(z.lev_dev * (z.nodes - 1) * 2, 3 * (z.nodes - 1) * z.per_node),
    )
    full = dict(
        member=(z.fine_columns, 2 * LANES),
        slot=(z.coarse_columns, LANES),
        keep=(z.n_wave, LANES),
        stiff=(z.n_wave * z.per_node, LANES),
        inverse=(z.n_wave * z.per_node, LANES),
    )

    def placed(shapes, unit):
        out, at = {}, 0
        for name, (count, columns) in shapes.items():
            out[name] = (at, count, columns)
            at += round_up(count, unit)
        return out, (at, max(columns for _, columns in shapes.values()))

    quads = dict(
        quad=(z.own_levels * 2 * z.fine_columns, z.points),
        coarse_quad=(z.own_levels * 2 * z.coarse_columns, z.coarse_points),
    )
    return [placed(shapes, 2 * SUBLANES) for shapes in (narrow, full, quads)]


class Table:
    def __init__(self, ref, place):
        self.ref, (self.at, self.count, self.columns) = ref, place

    def get(self, begin=0, count=None):
        begin = self.at + begin
        return self.ref[begin : begin + (count or self.count), : self.columns]

    def put(self, values, begin=0):
        begin = self.at + begin
        self.ref[begin : begin + values.shape[0], : self.columns] = values


def named(z, *refs):
    tables = {}
    for ref, (places, _) in zip(refs, parts(z)):
        tables |= {name: Table(ref, place) for name, place in places.items()}
    return tables


def copies_in(sources, targets, sems):
    copies = [
        pltpu.make_async_copy(source, target, sems.at[i])
        for i, (source, target) in enumerate(zip(sources, targets))
    ]
    for copy in copies:
        copy.start()
    return copies


def pack_kernel(z, state_hbm, leg_hbm, gauss_hbm, out_ref, state_ref, leg_ref, gauss_ref, sems, rows_s):
    bf, f32 = jnp.bfloat16, jnp.float32
    copies = copies_in((state_hbm, leg_hbm, gauss_hbm), (state_ref, leg_ref, gauss_ref), sems)
    for copy in copies:
        copy.wait()
    row = lax.broadcasted_iota(jnp.int32, (z.fine_rows, LANES), 0)
    lane = lax.broadcasted_iota(jnp.int32, (z.fine_rows, LANES), 1)
    for a in range(z.lev_dev):
        for b in range(z.nodes):
            n = (a * z.nodes + b) * 2
            for s in range(z.slots):
                rows_s[s, n : n + 2, :] = state_ref[a, b, s]
    if z.state_rows > z.dev_rows:
        for s in range(z.slots):
            rows_s[s, z.dev_rows :, :] = jnp.zeros((z.state_rows - z.dev_rows, z.fine_rows), f32)
    table = jnp.zeros((z.lats, LANES), f32)
    state = jnp.zeros((z.state_rows, LANES), f32)
    extra = jnp.zeros((SUBLANES, LANES), f32)
    for s in range(z.slots):
        target = jnp.where(row < z.coarse, s * z.coarse + row, z.head + s * z.rest + row - z.coarse)
        leg = leg_ref[s].astype(f32)
        spec = rows_s[s]
        place = (target == lane).astype(bf)
        table = table + matmul(leg.astype(bf), place)
        state = state + matmul(spec.astype(bf), place)
        if z.head + (s + 1) * z.rest > LANES:
            for q in range(z.groups):
                at = q * SUBLANES
                part = leg[at : at + SUBLANES] if at < z.lats else spec[at - z.lats : at - z.lats + SUBLANES]
                place = ((target >= LANES) & (target - LANES + q * z.unit == lane)).astype(bf)
                extra = extra + matmul(part.astype(bf), place)
    wide_row = lax.broadcasted_iota(jnp.int32, (SUBLANES, z.lats), 0)
    wide_lane = lax.broadcasted_iota(jnp.int32, (SUBLANES, z.lats), 1)
    out_lane = lax.broadcasted_iota(jnp.int32, (SUBLANES, LANES), 1)
    for q in range(z.lats // SUBLANES):
        chosen = jnp.where(wide_lane == wide_row + q * SUBLANES, gauss_ref[...], 0.0)
        column = jnp.sum(chosen, axis=1, keepdims=True)
        high = column.astype(bf).astype(f32)
        at = q * z.unit + z.used - LANES
        extra = extra + jnp.where(out_lane == at, high, 0.0)
        extra = extra + jnp.where(out_lane == at + 1, column - high, 0.0)
    block = jnp.concatenate([table, extra, state], 0).astype(bf)
    for i in range(z.chips):
        out_ref[i] = block


def mix_matrix(pick_left, matrix, pick_right, mask):
    bf, f32 = jnp.bfloat16, jnp.float32
    high, low = high_low(matrix)
    left = pick_left.astype(bf)
    halves = jnp.concatenate([matmul(left, high).astype(bf), matmul(left, low).astype(bf)], 1)
    return (matmul(halves, pick_right.astype(bf)) * mask.astype(f32)).astype(bf)


def tables_kernel(z, layout, rate_ref, fold_smem, *refs):
    inputs, outputs, scratch = refs[:9], refs[9:12], refs[12:]
    (scaled_s, sems), staged = scratch[:2], scratch[2:]
    copies = copies_in(inputs, staged, sems)
    fold_ref, coef_ref, basis_ref, spread_ref = staged[:4]
    sampled_ref, coarse_sampled_ref, from_ref, to_ref, picks_ref = staged[4:]
    out = named(z, *outputs)
    bf, f32 = jnp.bfloat16, jnp.float32
    lev = lax.axis_index("lev")
    core = lax.rem(lev, 2)
    waves, coarse = z.fine_width, z.coarse
    half = z.fine_columns

    wide = 2 * LANES
    lane = lax.broadcasted_iota(jnp.int32, (1, wide), 1)
    lane_slot = jnp.full((1, wide), -1, jnp.int32)
    lane_row = jnp.zeros((1, wide), jnp.int32)
    for s in range(z.slots):
        for begin, width, first in ((s * coarse, coarse, 0), (z.head + s * z.rest, z.rest, coarse)):
            inside = (lane >= begin) & (lane < begin + width)
            lane_slot = jnp.where(inside, s, lane_slot)
            lane_row = jnp.where(inside, lane - begin + first, lane_row)
    rate_row = lax.broadcasted_iota(jnp.int32, (z.per_node, LANES), 0)
    rates = jnp.zeros((z.per_node, LANES), f32)
    for q in range(z.levels):
        rates = jnp.where((rate_row >= 2 * q) & (rate_row < 2 * q + 2), rate_ref[q], rates)
    for w in range(z.n_wave):
        small = jnp.zeros((1, wide), jnp.int32)
        for s in range(z.slots):
            small = jnp.where(lane_slot == s, fold_smem[w * z.slots + s], small)
        first = lane_row < waves - small
        keep = (lane < z.head) & (lane_row < coarse - small)
        out["keep"].put(keep[:, :LANES].astype(f32), w)
        for s in range(z.slots):
            own = lane_slot == s
            at = (w * z.slots + s) * 2
            out["member"].put((own & first).astype(f32), at)
            out["member"].put((own & jnp.logical_not(first)).astype(f32), at + 1)
            out["slot"].put((own & keep)[:, :LANES].astype(f32), w * z.slots + s)
        degree = (small + lane_row)[:, :LANES].astype(f32)
        stiff = rates * (degree * (degree + 1.0) / (coarse * (coarse + 1.0)))
        out["stiff"].put(stiff, w * z.per_node)
        out["inverse"].put(1.0 / (1.0 + STEP_HALF * stiff), w * z.per_node)

    for copy in copies[:3]:
        copy.wait()

    def wave_column(count, per_slot):
        row = lax.broadcasted_iota(jnp.int32, (count, z.coarse_columns), 0)
        lane = lax.broadcasted_iota(jnp.int32, (count, z.coarse_columns), 1)
        inside = (row >= lane * per_slot) & (row < (lane + 1) * per_slot)
        small = jnp.sum(jnp.where(inside, fold_ref[...].astype(f32), 0.0), axis=1, keepdims=True)
        if per_slot == 1:
            return small
        first = lax.broadcasted_iota(jnp.int32, (count, 1), 0) & 1
        return jnp.where(first == 0, small, waves - 1 - small)

    def one_hot(count, per_slot, width):
        column = wave_column(count, per_slot)
        lane = lax.broadcasted_iota(jnp.int32, (count, 2 * width), 1).astype(f32)
        extra = width - coarse
        top = lane == jnp.where(column < coarse, column, column + coarse)
        bottom = lane == jnp.where(column < coarse, column + coarse, column + coarse + extra)
        return jnp.concatenate([top.astype(f32), bottom.astype(f32)], 0).astype(bf)

    hot = one_hot(half, 2, waves)
    coarse_hot = one_hot(z.coarse_columns, 1, coarse)
    short, long = 2 * coarse, 2 * (waves - coarse)
    levels = [(2 * x + core) * z.lev_dev + al for x in range(z.n_pair) for al in range(z.lev_dev)]
    period = basis_ref.shape[1]
    row = lax.broadcasted_iota(jnp.int32, (2 * waves, 1), 0)
    count = jnp.where(row < short, coarse, waves - coarse)
    wave = jnp.where(row < short, row, row - short)
    wave = jnp.where(wave < count, wave, wave - count) + jnp.where(row < short, 0, coarse)
    sign = (1 - 2 * (wave & 1)).astype(f32)
    chunk = LANES
    lines = [coef_ref[pl.ds(level, 1), :] for level in levels]
    for begin in range(0, period, chunk):
        span = slice(begin, begin + chunk)
        values = basis_ref[:, span].astype(f32)
        signed = values * sign
        for a, line in enumerate(lines):
            near = line[:, span] * values
            far = line[:, period + begin : period + begin + chunk] * signed
            for side, scaled in enumerate((near + far, near - far)):
                scaled_s[side, a * short : (a + 1) * short, span] = scaled[:short].astype(bf)
                at = z.own_levels * short + a * long
                scaled_s[side, at : at + long, span] = scaled[short:].astype(bf)
    for copy in copies[3:]:
        copy.wait()
    out["wave"].put(matmul_nt(sampled_ref[...], hot).astype(bf))
    out["coarse_wave"].put(matmul_nt(coarse_sampled_ref[...], coarse_hot).astype(bf))
    even = matmul(scaled_s[0], spread_ref[0])
    odd = matmul(scaled_s[1], spread_ref[1])
    total, delta = even + odd, even - odd
    middle, top = z.points // 2, z.own_levels * short
    quad = jnp.concatenate([total[:, :middle], delta[:, :middle]], 1).astype(bf)
    coarse_quad = jnp.concatenate([total[:top, middle:], delta[:top, middle:]], 1).astype(bf)
    for a in range(z.own_levels):
        at = z.own_levels * short + a * long
        pair = jnp.concatenate([quad[a * short : (a + 1) * short], quad[at : at + long]], 0)
        values = matmul(hot, pair).astype(bf)
        out["quad"].put(values, a * values.shape[0])
        values = matmul(coarse_hot, coarse_quad[a * short : (a + 1) * short]).astype(bf)
        out["coarse_quad"].put(values, a * values.shape[0])

    def pick(name, index=0):
        at, height, count, columns = layout[name]
        return picks_ref[pl.ds(pl.multiple_of(at + index * height, 2 * SUBLANES), count), :columns]

    def mix(left, matrix, right, mask):
        return mix_matrix(left, matrix[...], right, mask)

    out["mix_to"].put(mix(pick("to_left"), to_ref, pick("to_right", core), pick("to_mask")))
    out["mix_from"].put(mix(pick("from_left", core), from_ref, pick("from_right"), pick("from_mask")))
    out["mix_back"].put(mix(pick("back_left"), to_ref, pick("back_right", core), pick("from_mask")))
    out["lift"].put(mix(pick("lift_left", lev), from_ref, pick("lift_right"), pick("lift_mask")))


def sweep_kernel(
    z,
    own_ref,
    other_ref,
    state_ref,
    narrow_hbm,
    full_hbm,
    quads_hbm,
    other_quads_hbm,
    corrected_ref,
    tend_ref,
    leg_s,
    state_s,
    fourier_s,
    back_s,
    tend_s,
    coarse_s,
    coarse_back_s,
    change_s,
    narrow_ref,
    full_ref,
    quads_ref,
    other_quads_ref,
    sems,
    legendre_s,
    product_s,
    coarse_product_s,
):
    bf, f32 = jnp.bfloat16, jnp.float32
    slots, rows, lats, per_node = z.slots, z.rows, z.lats, z.per_node
    table = named(z, narrow_ref, full_ref)
    quads = [named(z, *[ref] * 3) for ref in (quads_ref, other_quads_ref)]
    copies = copies_in(
        (full_hbm, narrow_hbm, quads_hbm, other_quads_hbm),
        (full_ref, narrow_ref, quads_ref, other_quads_ref),
        sems,
    )

    def quad(name, a, count):
        lev, inner = a // z.lev_dev, a % z.lev_dev
        return quads[lev % 2][name].get((lev // 2 * z.lev_dev + inner) * count, count)

    wide = 2 * LANES
    all_lats = z.n_lev * lats

    def member(w, j):
        return table["member"].get(w * slots * 2 + j, 1)

    def slot(w, s):
        return table["slot"].get(w * slots + s, 1)

    def keep(w):
        return table["keep"].get(w, 1)

    for w in range(z.n_wave):
        for x in range(z.n_pair):
            for o, ref in enumerate((own_ref, other_ref)):
                d = 2 * x + o
                block = ref[z.position[w * z.n_pair + x]].astype(f32)
                extra = block[lats : lats + SUBLANES]
                leg_s[w, d * lats : (d + 1) * lats, :LANES] = block[:lats]
                state_at = d * z.dev_rows
                begin = lats + SUBLANES
                state_s[w, state_at : state_at + z.dev_rows, :LANES] = block[begin : begin + z.dev_rows]
                for q in range(z.groups):
                    moved = extra if q == 0 else pltpu.roll(extra, LANES - q * z.unit, 1)
                    at = q * SUBLANES
                    if at < lats:
                        leg_s[w, d * lats + at : d * lats + at + SUBLANES, LANES:] = moved
                    else:
                        at = at - lats
                        count = min(SUBLANES, z.dev_rows - at)
                        state_s[w, state_at + at : state_at + at + count, LANES:] = moved[:count]
        if all_lats < leg_s.shape[1]:
            leg_s[w, all_lats:, :] = jnp.zeros((leg_s.shape[1] - all_lats, wide), f32)
        legendre_s[w] = leg_s[w].astype(bf)

    lane = lax.broadcasted_iota(jnp.int32, (2 * SUBLANES, wide), 1)
    picked = ((lane == z.used) | (lane == z.used + 1)).astype(bf)
    gauss = matmul_nt(picked, legendre_s[0])[:1]

    inner = 2 * sum(z.head + (s + 1) * z.rest <= LANES for s in range(slots))
    spans = [(0, inner, LANES), (inner, 2 * slots, wide)]
    copies[0].wait()
    for w in range(z.n_wave):
        state = state_s[w]
        for first, last, width in spans:
            left = [state[:, :width] * member(w, j)[:, :width] for j in range(first, last)]
            left = jnp.concatenate(left, 0).astype(bf)
            at = (w * 2 * slots + first) * rows
            fourier_s[at : at + left.shape[0], :] = matmul_nt(left, legendre_s[w, :, :width])

    for copy in copies[1:]:
        copy.wait()
    both = 2 * z.fine_columns
    half = z.fine_columns
    for a in range(z.levels):
        pieces = []
        for b in range(z.nodes):
            at = (a * z.nodes + b) * 2
            piece = [fourier_s[pl.ds(at + c, half, stride=rows), :] for c in range(2)]
            pieces.append(jnp.concatenate(piece, 0).astype(bf))
        grid = matmul(table["wave"].get(), jnp.concatenate(pieces, 1))
        product_s[a] = (grid * grid).astype(bf)
    for a in range(z.levels):
        back = matmul(quad("quad", a, both), product_s[a])
        for b in range(z.nodes):
            values = back[:, b * LANES : (b + 1) * LANES] * gauss
            back_s[(a * z.nodes + b) * both : (a * z.nodes + b + 1) * both, :] = values

    stacked = []
    for w in range(z.n_wave):
        outs = []
        for first, last, width in spans:
            left = [
                back_s[pl.ds(w * 2 * slots + j, rows, stride=z.fine_columns), :].astype(bf)
                for j in range(first, last)
            ]
            out = matmul(jnp.concatenate(left, 0), legendre_s[w, :, :width])
            outs += [out[i * rows : (i + 1) * rows] for i in range(last - first)]
        total, beyond = outs[-1][:, :LANES], outs[-1][:, LANES:]
        for j in range(2 * slots - 1):
            chosen = member(w, j) > 0.5
            total = jnp.where(chosen[:, :LANES], outs[j][:, :LANES], total)
            if j >= inner:
                beyond = jnp.where(chosen[:, LANES:], outs[j][:, LANES:], beyond)
        tend_s[w, :rows, :LANES] = total
        tend_s[w, :rows, LANES:] = beyond
        stacked.append(state_s[w][:, :LANES] * keep(w))
        stacked.append(total * keep(w))

    modes = matmul_split(table["mix_to"].get(), jnp.concatenate(stacked, 1))
    evals, later, old_of, mid_of = [], [], [], []
    for w in range(z.n_wave):
        old, source = [], []
        stiff = table["stiff"].get(w * per_node, per_node)
        for b in range(z.nodes):
            part = modes[b * per_node : (b + 1) * per_node]
            old.append(part[:, 2 * w * LANES : (2 * w + 1) * LANES])
            source.append(part[:, (2 * w + 1) * LANES : (2 * w + 2) * LANES] - stiff * old[-1])
        inverse = table["inverse"].get(w * per_node, per_node)
        mid = sum(quad_weights[0][b] * source[b] for b in range(z.nodes))
        mid = (mid + old[0] + STEP_HALF * stiff * old[1]) * inverse
        end = sum(quad_weights[1][b] * source[b] for b in range(z.nodes))
        end = end + mid + STEP_HALF * stiff * old[2]
        evals.append(old[1])
        evals.append(mid)
        later.append((end, inverse))
        old_of.append(old)
        mid_of.append(mid)

    level_values = matmul_split(table["mix_from"].get(), jnp.concatenate(evals, 1))
    for w in range(z.n_wave):
        left = jnp.concatenate(
            [
                level_values[:, (2 * w + e) * LANES : (2 * w + e + 1) * LANES] * slot(w, s)
                for s in range(slots)
                for e in range(2)
            ],
            0,
        ).astype(bf)
        out = matmul_nt(left, legendre_s[w, :, :LANES])
        coarse_s[w * slots * 2 * per_node : (w + 1) * slots * 2 * per_node, :] = out

    both_c = 2 * z.coarse_columns
    for a in range(z.levels):
        pieces = []
        for e in range(2):
            at = e * per_node + a * 2
            piece = [
                coarse_s[pl.ds(at + c, z.coarse_columns, stride=2 * per_node), :] for c in range(2)
            ]
            pieces.append(jnp.concatenate(piece, 0).astype(bf))
        grid = matmul(table["coarse_wave"].get(), jnp.concatenate(pieces, 1))
        before, fresh = grid[:, :LANES], grid[:, LANES:]
        coarse_product_s[a] = (fresh * fresh - before * before).astype(bf)
    for a in range(z.levels):
        back = matmul(quad("coarse_quad", a, both_c), coarse_product_s[a])
        coarse_back_s[a * both_c : (a + 1) * both_c, :] = back * gauss

    tends = []
    for w in range(z.n_wave):
        left = jnp.concatenate(
            [
                coarse_back_s[pl.ds(w * slots + s, per_node, stride=z.coarse_columns), :].astype(bf)
                for s in range(slots)
            ],
            0,
        )
        out = matmul(left, legendre_s[w, :, :LANES])
        total = None
        for s in range(slots):
            term = slot(w, s) * out[s * per_node : (s + 1) * per_node]
            total = term if total is None else total + term
        tends.append(total)
    coarse_modes = matmul_split(table["mix_back"].get(), jnp.concatenate(tends, 1))
    for w in range(z.n_wave):
        end, inverse = later[w]
        end = (end + STEP_HALF * coarse_modes[:, w * LANES : (w + 1) * LANES]) * inverse
        change_s[w, :per_node, :] = mid_of[w] - old_of[w][1]
        change_s[w, per_node:, :] = end - old_of[w][2]

    place = lax.axis_index("wave")
    begin = pl.multiple_of(lax.div(lax.axis_index("lev"), 2) * (2 * z.dev_rows), SUBLANES)
    mine = tend_s[place, pl.ds(begin, z.state_rows), :]
    raised = matmul_split(table["lift"].get(), change_s[place])
    lane = lax.broadcasted_iota(jnp.int32, (z.state_rows, wide), 1)
    for s in range(slots):
        low = mine if s == 0 else pltpu.roll(mine, wide - s * z.coarse, 1)
        high = pltpu.roll(mine, wide - (z.head + s * z.rest - z.coarse), 1)
        values = jnp.where(lane < z.coarse, low, high)
        for n in range(0, z.dev_rows, 2):
            tend_ref[n // (z.nodes * 2), n // 2 % z.nodes, s] = values[n : n + 2, : z.fine_rows]
        low = raised if s == 0 else pltpu.roll(raised, LANES - s * z.coarse, 1)
        low = jnp.where(lane[: low.shape[0], :LANES] < z.coarse, low, 0.0)
        for n in range(0, low.shape[0], 2):
            a, b = n // (2 * (z.nodes - 1)), n // 2 % (z.nodes - 1)
            corrected_ref[a, b, s] = state_ref[a, b + 1, s] + low[n : n + 2, : z.fine_rows]


def mix_constants(z):
    level, node, part = np.arange(z.levels), np.arange(z.nodes), np.arange(2)

    def pick(index):
        return (np.asarray(index)[:, None] == level[None, :]).astype(np.float32)

    def grid(*axes):
        return [m.reshape(-1) for m in np.meshgrid(*axes, indexing="ij")]

    def ordered(index, core):
        lev, inner = index // z.lev_dev, index % z.lev_dev
        return (lev ^ core) * z.lev_dev + inner

    def thrice(matrix):
        return np.concatenate([matrix] * 3, -1)

    def halves(matrix):
        zero = np.zeros_like(matrix)
        return np.concatenate(
            [np.concatenate([matrix, matrix, zero], 1), np.concatenate([zero, zero, matrix], 1)]
        )

    rb, rq, rc = grid(node, level, part)
    ca, cb, cc = grid(level, node, part)
    sa, sc = grid(level, part)
    to_mask = (rb[:, None] == cb[None]) & (rc[:, None] == cc[None])
    same_part = sc[:, None] == sc[None]
    la, lb, lc = grid(np.arange(z.lev_dev), np.arange(z.nodes - 1), part)
    kb, kq, kc = grid(np.arange(z.nodes - 1), level, part)
    lift_mask = (lb[:, None] == kb[None]) & (lc[:, None] == kc[None])
    by_core = range(2)
    constants = dict(
        to_left=[pick(rq)],
        to_right=[halves(pick(ordered(ca, k)).T) for k in by_core],
        to_mask=[thrice(to_mask)],
        from_left=[pick(ordered(sa, k)) for k in by_core],
        from_right=[halves(pick(sa).T)],
        from_mask=[thrice(same_part)],
        back_left=[pick(sa)],
        back_right=[halves(pick(ordered(sa, k)).T) for k in by_core],
        lift_left=[pick(k * z.lev_dev + la) for k in range(z.n_lev)],
        lift_right=[halves(pick(kq).T)],
        lift_mask=[thrice(lift_mask)],
    )
    wide = max(m[0].shape[1] for m in constants.values())
    layout, rows, at = {}, [], 0
    for name, members in constants.items():
        count, columns = members[0].shape
        height = round_up(count, 2 * SUBLANES)
        layout[name] = (at, height, count, columns)
        at += height * len(members)
        rows += [np.pad(m, ((0, height - count), (0, wide - columns))) for m in members]
    return layout, jnp.asarray(np.concatenate(rows), jnp.bfloat16)


def replicated_plan(
    fine_state, fold_pairs, legendre, gauss_weights, grid_coef, modes_from, modes_to, mode_rates
):
    z = Sizes(fine_state, legendre)
    bf, f32 = jnp.bfloat16, jnp.float32
    longitudes = grid_coef.shape[1]
    vmem = pl.BlockSpec(memory_space=pltpu.VMEM)
    smem = pl.BlockSpec(memory_space=pltpu.SMEM)
    hbm = pl.BlockSpec(memory_space=pltpu.HBM)
    shape = jax.ShapeDtypeStruct
    stored = jnp.swapaxes(fine_state, 2, 3)
    block = pl.pallas_call(
        functools.partial(pack_kernel, z),
        out_shape=shape((z.chips, z.block_rows, LANES), bf),
        in_specs=[hbm] * 3,
        out_specs=vmem,
        scratch_shapes=[
            pltpu.VMEM(stored.shape, f32),
            pltpu.VMEM(legendre.shape, bf),
            pltpu.VMEM((1, z.lats), f32),
            pltpu.SemaphoreType.DMA((3,)),
            pltpu.VMEM((z.slots, z.state_rows, z.fine_rows), f32),
        ],
        name="pack",
    )(stored, legendre, gauss_weights[None])
    groups = [[2 * i + c for i in z.order] for c in range(2)]
    own = lax.all_to_all(
        block, ("wave", "lev"), 0, 0, tiled=True, axis_index_groups=groups
    )
    fine_amp, coarse_amp = z.fine_width**-0.5, z.coarse**-0.5
    order = np.arange(2 * z.fine_width).reshape(2, -1)
    order = np.concatenate([order[:, : z.coarse].reshape(-1), order[:, z.coarse :].reshape(-1)])
    basis = wave_rows(z.fine_width, longitudes, fine_amp)[order]
    spread = interpolation(z.points, longitudes, 2 * (z.fine_width - 1))
    spread *= 2.0 * z.fine_width / longitudes
    coarse_spread = interpolation(z.coarse_points, longitudes, 2 * (z.coarse - 1))
    coarse_spread *= 2.0 * z.coarse / (longitudes // 2) * (coarse_amp / fine_amp)
    coarse_spread[1::2] = 0.0
    spread = np.stack(
        [
            np.concatenate([folded(spread, side), folded(coarse_spread, side)], 1)
            for side in (0.5, -0.5)
        ]
    )
    sampled = wave_rows(z.fine_width, z.points, fine_amp)[order].T
    coarse_sampled = wave_rows(z.coarse, z.coarse_points, coarse_amp).T
    basis = basis[:, : longitudes // 2]
    constants = [jnp.asarray(c, bf) for c in (basis, spread, sampled, coarse_sampled)]
    layout, picks = mix_constants(z)
    staged = [fold_pairs[None], grid_coef, *constants, modes_from, modes_to, picks]
    wide = 2 * LANES
    narrow_shape, full_shape, quads_shape = [entry[1] for entry in parts(z)]
    narrow, full, quads = pl.pallas_call(
        functools.partial(tables_kernel, z, layout),
        out_shape=(shape(narrow_shape, bf), shape(full_shape, f32), shape(quads_shape, bf)),
        in_specs=[smem, smem] + [hbm] * len(staged),
        out_specs=(vmem,) * 3,
        scratch_shapes=[
            pltpu.VMEM((2, z.own_levels * 2 * z.fine_width, longitudes // 2), bf),
            pltpu.SemaphoreType.DMA((len(staged),)),
        ]
        + [pltpu.VMEM(array.shape, array.dtype) for array in staged],
        cost_estimate=pl.CostEstimate(flops=10**9, bytes_accessed=4 * 10**6, transcendentals=0),
        name="tables",
    )(mode_rates, fold_pairs, *staged)

    partners = [(i, i ^ 1) for i in range(2 * z.chips)]
    other_quads = lax.ppermute(quads, ("wave", "lev"), partners)
    own, narrow = lax.optimization_barrier((own, narrow))
    other = lax.ppermute(own, ("wave", "lev"), partners)

    lat_rows = round_up(z.n_lev * z.lats, LANES)
    corrected, fine_tend = pl.pallas_call(
        functools.partial(sweep_kernel, z),
        out_shape=(
            shape((z.lev_dev, z.nodes - 1, z.slots, 2, z.fine_rows), f32),
            shape(stored.shape, f32),
        ),
        in_specs=[vmem] * 3 + [hbm] * 4,
        out_specs=(vmem, vmem),
        scratch_shapes=[
            pltpu.VMEM((z.n_wave, lat_rows, wide), f32),
            pltpu.VMEM((z.n_wave, z.rows, wide), f32),
            pltpu.VMEM((z.rows * z.fine_columns, lat_rows), f32),
            pltpu.VMEM((z.rows * z.fine_columns, lat_rows), f32),
            pltpu.VMEM((z.n_wave, z.rows + SUBLANES, wide), f32),
            pltpu.VMEM((2 * z.per_node * z.coarse_columns, lat_rows), f32),
            pltpu.VMEM((z.per_node * z.coarse_columns, lat_rows), f32),
            pltpu.VMEM((z.n_wave, (z.nodes - 1) * z.per_node, LANES), f32),
            pltpu.VMEM(narrow_shape, bf),
            pltpu.VMEM(full_shape, f32),
            pltpu.VMEM(quads_shape, bf),
            pltpu.VMEM(quads_shape, bf),
            pltpu.SemaphoreType.DMA((4,)),
            pltpu.VMEM((z.n_wave, lat_rows, wide), bf),
            pltpu.VMEM((z.levels, z.points, z.nodes * LANES), bf),
            pltpu.VMEM((z.levels, z.coarse_points, LANES), bf),
        ],
        compiler_params=pltpu.CompilerParams(vmem_limit_bytes=VMEM_BYTES),
        name="sweep",
    )(own, other, stored, narrow, full, quads, other_quads)
    return (jnp.swapaxes(corrected, 2, 3), jnp.swapaxes(fine_tend, 2, 3))


def fits_replicated(fine_state, legendre):
    n_wave, n_lev = lax.axis_size("wave"), lax.axis_size("lev")
    if n_lev % 2 or fine_state.shape[1] != len(quad_weights[0]):
        return False
    z = Sizes(fine_state, legendre)
    gathered = 32 * n_wave * n_lev * (legendre.size + fine_state.size)
    return (
        z.head <= LANES
        and z.used > LANES
        and z.used + 2 - LANES <= z.unit
        and z.lats % SUBLANES == 0
        and z.head + z.rest <= LANES
        and n_lev * z.lats <= LANES
        and gathered <= REPLICATED_BYTES
    )


def per_device(fine_state, fold_pairs, legendre, *rest):
    plan = replicated_plan if fits_replicated(fine_state, legendre) else split_plan
    return plan(fine_state, fold_pairs, legendre, *rest)


def solution(mesh):
    placed = (
        P("lev", None, None, "wave", None),
        P(),
        P("wave", "lev", None),
        P("lev"),
        P(),
        P(),
        P(),
        P(),
    )
    return jax.shard_map(
        per_device,
        mesh=mesh,
        in_specs=placed,
        out_specs=(P("lev", None, None, "wave", None), P("lev", None, None, "wave", None)),
        check_vma=False,
    )
```

```python
import functools
import math

import jax
import jax.numpy as jnp
import numpy as np
from jax import lax
from jax.experimental import pallas as pl
from jax.experimental.pallas import tpu as pltpu
from jax.sharding import PartitionSpec as P

STEP_HALF = 0.5
quad_weights = ((5.0 / 24.0, 1.0 / 3.0, -1.0 / 24.0), (-1.0 / 24.0, 1.0 / 3.0, 5.0 / 24.0))
HIGHEST = lax.Precision.HIGHEST


def fourier_table(waves, points, amplitude):
    steps = jnp.arange(points, dtype=jnp.int32)
    turns = waves[:, :, None] * steps[None, None, :] % points
    angles = turns.astype(jnp.float32) * (2.0 * math.pi / points)
    return jnp.stack([jnp.cos(angles) * amplitude, -jnp.sin(angles) * amplitude]).astype(
        jnp.bfloat16
    )


def fine_rows(small_wave, fine_width):
    row_ids = jnp.arange(fine_width + 1, dtype=jnp.int32)[None, :]
    return row_ids < fine_width - small_wave[:, None]


def coarse_rows(small_wave, coarse):
    row_ids = jnp.arange(coarse, dtype=jnp.int32)[None, :]
    coarse_keep = row_ids < coarse - small_wave[:, None]
    degree = (small_wave[:, None] + row_ids).astype(jnp.float32)
    return (coarse_keep, degree)


def legendre_inverse(spectral, legendre_table, row_mask):
    split_spec = spectral[:, :, :, :, None, :] * row_mask[None, None, None]
    return jnp.einsum(
        "abcpmr,plr->abcpml", split_spec, legendre_table, preferred_element_type=jnp.float32
    ).astype(jnp.bfloat16)


def legendre_forward(returned, legendre_table, row_mask):
    members = jnp.einsum(
        "abcpml,plr->abcpmr", returned, legendre_table, preferred_element_type=jnp.float32
    )
    return jnp.sum(members * row_mask.astype(jnp.float32)[None, None, None], axis=4)


def grid_step(fourier, wave_table, coef, weights, factor):
    grid_field = jnp.einsum(
        "abcpmz,cpmk->abzk", fourier, wave_table, preferred_element_type=jnp.float32
    )
    product = (coef[:, None, None, :] * grid_field * grid_field).astype(jnp.bfloat16)
    returned = jnp.einsum(
        "abzk,cpmk->abcpmz", product, wave_table, preferred_element_type=jnp.float32
    )
    return (returned * (weights * factor)).astype(jnp.bfloat16)


def mix(matrix, values):
    return jnp.einsum("ql,lbcpr->qbcpr", matrix, values, precision=HIGHEST)


def split_plan(
    fine_state, fold_pairs, legendre, gauss_weights, grid_coef, modes_from, modes_to, mode_rates
):
    n_wave = lax.axis_size("wave")
    wave_idx = lax.axis_index("wave")
    lev_idx = lax.axis_index("lev")
    lev_dev = fine_state.shape[0]
    pairs_dev = fine_state.shape[3]
    fine_width = fine_state.shape[4] - 1
    coarse = fine_width // 2
    longitudes = grid_coef.shape[1]
    band_size = legendre.shape[1] // n_wave
    small_wave = lax.dynamic_slice_in_dim(fold_pairs, wave_idx * pairs_dev, pairs_dev)
    first_member = fine_rows(small_wave, fine_width)
    member_mask = jnp.stack([first_member, jnp.logical_not(first_member)], 1).astype(jnp.bfloat16)
    coarse_keep, degree = coarse_rows(small_wave, coarse)
    keep_mask = coarse_keep[:, None, :].astype(jnp.bfloat16)
    keep_float = coarse_keep.astype(jnp.float32)
    fine_table = fourier_table(
        jnp.stack([fold_pairs, fine_width - 1 - fold_pairs], 1), longitudes, fine_width ** (-0.5)
    )
    coarse_table = fourier_table(fold_pairs[:, None], longitudes // 2, coarse ** (-0.5))
    coarse_leg = legendre[:, :, :coarse]
    coarse_coef = grid_coef[:, ::2]
    band_gauss = lax.dynamic_slice_in_dim(gauss_weights, wave_idx * band_size, band_size)
    local_to = lax.dynamic_slice_in_dim(modes_to, lev_idx * lev_dev, lev_dev, 1)
    local_from = lax.dynamic_slice_in_dim(modes_from, lev_idx * lev_dev, lev_dev, 1)
    mode_decay = lax.dynamic_slice_in_dim(mode_rates, lev_idx * lev_dev, lev_dev)

    def project(partial_sum):
        return mix(modes_to, partial_sum)

    def coarse_start(modes):
        gathered = lax.all_gather(modes, "lev", axis=0, tiled=True)
        levels = (mix(modes_from, gathered) * keep_float).astype(jnp.bfloat16)
        return legendre_inverse(levels, coarse_leg, keep_mask)

    def coarse_grid_step(fourier):
        return grid_step(
            fourier, coarse_table, coarse_coef, band_gauss, 2.0 * coarse / (longitudes // 2)
        )

    def coarse_finish(returned):
        partial_sum = legendre_forward(returned, coarse_leg, keep_mask)
        return lax.psum_scatter(
            project(partial_sum).astype(jnp.bfloat16), "lev", scatter_dimension=0, tiled=True
        ).astype(jnp.float32)

    def coarse_eval(modes):
        fourier = lax.all_to_all(
            coarse_start(modes), "wave", split_axis=5, concat_axis=3, tiled=True
        )
        returned = lax.all_to_all(
            coarse_grid_step(fourier), "wave", split_axis=3, concat_axis=5, tiled=True
        )
        return coarse_finish(returned)

    restricted = fine_state[..., :coarse] * keep_float
    fine_spec = lax.all_gather(fine_state.astype(jnp.bfloat16), "lev", axis=0, tiled=True)
    fine_fourier = legendre_inverse(fine_spec, legendre, member_mask)
    fine_fourier = lax.all_to_all(fine_fourier, "wave", split_axis=5, concat_axis=3, tiled=True)
    fine_back = lax.all_to_all(
        grid_step(fine_fourier, fine_table, grid_coef, band_gauss, 2.0 * fine_width / longitudes),
        "wave",
        split_axis=3,
        concat_axis=5,
        tiled=True,
    )
    fine_tend = lax.psum_scatter(
        legendre_forward(fine_back, legendre, member_mask).astype(jnp.bfloat16),
        "lev",
        scatter_dimension=0,
        tiled=True,
    ).astype(jnp.float32)
    restricted_tend = fine_tend[..., :coarse] * keep_float
    stacked = jnp.concatenate([restricted, restricted_tend], 1)
    both_modes = lax.psum_scatter(
        mix(local_to, stacked).astype(jnp.bfloat16), "lev", scatter_dimension=0, tiled=True
    ).astype(jnp.float32)
    nodes = fine_state.shape[1]
    old_state = both_modes[:, :nodes]
    old_tend = both_modes[:, nodes:]
    old_coarse = coarse_eval(old_state[:, 1:2])
    stiffness = (
        mode_decay[:, None, None, None]
        * (degree * (degree + 1.0) / (coarse * (coarse + 1.0)))[None, None]
    )
    source = old_tend - stiffness[:, None] * old_state
    integral_mid = (
        quad_weights[0][0] * source[:, 0]
        + quad_weights[0][1] * source[:, 1]
        + quad_weights[0][2] * source[:, 2]
    )
    integral_end = (
        quad_weights[1][0] * source[:, 0]
        + quad_weights[1][1] * source[:, 1]
        + quad_weights[1][2] * source[:, 2]
    )
    divisor = 1.0 + STEP_HALF * stiffness
    next_mid = (old_state[:, 0] + STEP_HALF * stiffness * old_state[:, 1] + integral_mid) / divisor
    coarse_fresh = coarse_eval(next_mid[:, None])
    next_end = (
        next_mid
        + STEP_HALF * (coarse_fresh[:, 0] - old_coarse[:, 0])
        + STEP_HALF * stiffness * old_state[:, 2]
        + integral_end
    ) / divisor
    change = jnp.stack([next_mid - old_state[:, 1], next_end - old_state[:, 2]], 1)
    lifted = lax.psum_scatter(
        mix(local_from, change).astype(jnp.bfloat16), "lev", scatter_dimension=0, tiled=True
    ).astype(jnp.float32)
    corrected = fine_state[:, 1:] + jnp.pad(
        lifted, ((0, 0), (0, 0), (0, 0), (0, 0), (0, fine_width + 1 - coarse))
    )
    return (corrected, fine_tend)


LANES = 128
SUBLANES = 8
REPLICATED_BYTES = 16 * 2**20
VMEM_BYTES = 56 * 10**6


def round_up(value, unit):
    return -(-value // unit) * unit


def interpolation(points, targets, degree):
    offset = (
        2.0 * np.pi * (np.arange(targets)[:, None] / targets - np.arange(points)[None, :] / points)
    )
    order = np.arange(1, degree + 1)
    return (1.0 + 2.0 * np.cos(offset[:, :, None] * order).sum(-1)) / points


def wave_rows(waves, points, amplitude):
    turns = np.arange(waves)[:, None] * np.arange(points)[None, :] % points
    angles = turns * (2.0 * np.pi / points)
    return np.concatenate([np.cos(angles), -np.sin(angles)]) * amplitude


def folded(table, side):
    near = table[: table.shape[0] // 2]
    middle = table.shape[1] // 2
    return 0.5 * near[:, :middle] + side * near[:, middle:]


def matmul(a, b):
    return jnp.dot(a, b, preferred_element_type=jnp.float32)


def matmul_nt(a, b):
    return lax.dot_general(a, b, (((1,), (1,)), ((), ())), preferred_element_type=jnp.float32)


def matmul_exact(a, b):
    return jnp.dot(a, b, preferred_element_type=jnp.float32, precision=lax.Precision.HIGHEST)


def high_low(values):
    high = values.astype(jnp.bfloat16)
    return high, (values - high.astype(jnp.float32)).astype(jnp.bfloat16)


def matmul_split(left, right):
    high, low = high_low(right)
    return matmul(left, jnp.concatenate([high, low, high], 0))


def pitch(count):
    return count + 4 if count % 8 == 0 else count


class Sizes:
    def __init__(self, fine_state, legendre):
        self.n_wave, self.n_lev = lax.axis_size("wave"), lax.axis_size("lev")
        self.lev_dev, self.nodes, _, self.slots, self.fine_rows = fine_state.shape
        self.lats = legendre.shape[1]
        self.n_pair = self.n_lev // 2
        self.fine_width = self.fine_rows - 1
        self.coarse = self.fine_width // 2
        self.levels = self.n_lev * self.lev_dev
        self.own_levels = self.n_pair * self.lev_dev
        self.dev_rows = self.lev_dev * self.nodes * 2
        self.rows = self.levels * self.nodes * 2
        self.per_node = self.levels * 2
        self.head = self.slots * self.coarse
        self.rest = self.fine_rows - self.coarse
        self.used = self.slots * self.fine_rows
        self.state_rows = round_up(self.dev_rows, SUBLANES)
        self.groups = (self.lats + self.state_rows) // SUBLANES
        self.unit = LANES // self.groups
        self.block_rows = self.lats + SUBLANES + self.state_rows
        self.chips = self.n_wave * self.n_pair
        lead = self.chips // 2 - 1
        self.order = [lead] + [i for i in range(self.chips) if i != lead]
        self.position = [self.order.index(i) for i in range(self.chips)]
        self.fine_columns = self.n_wave * self.slots * 2
        self.coarse_columns = self.n_wave * self.slots
        self.row_pitch = pitch(self.rows)
        self.column_pitch = pitch(self.fine_columns)
        self.mode_pitch = pitch(2 * self.per_node)
        self.slot_pitch = pitch(self.coarse_columns)
        self.points = round_up(4 * (self.fine_width - 1) + 1, 32)
        self.coarse_points = round_up(4 * (self.coarse - 1) + 1, 32)


def parts(z):
    narrow = dict(
        wave=(z.points, 2 * z.fine_columns),
        coarse_wave=(z.coarse_points, 2 * z.coarse_columns),
        mix_to=(z.rows, 3 * z.rows),
        mix_from=(z.per_node, 3 * z.per_node),
        mix_back=(z.per_node, 3 * z.per_node),
        lift=(z.lev_dev * (z.nodes - 1) * 2, 3 * (z.nodes - 1) * z.per_node),
    )
    full = dict(
        member=(z.fine_columns, 2 * LANES),
        slot=(z.coarse_columns, LANES),
        keep=(z.n_wave, LANES),
        stiff=(z.n_wave * z.per_node, LANES),
        inverse=(z.n_wave * z.per_node, LANES),
    )

    def placed(shapes, unit):
        out, at = {}, 0
        for name, (count, columns) in shapes.items():
            out[name] = (at, count, columns)
            at += round_up(count, unit)
        return out, (at, max(columns for _, columns in shapes.values()))

    quads = dict(
        quad=(z.own_levels * 2 * z.fine_columns, z.points),
        coarse_quad=(z.own_levels * 2 * z.coarse_columns, z.coarse_points),
    )
    return [placed(shapes, 2 * SUBLANES) for shapes in (narrow, full, quads)]


class Table:
    def __init__(self, ref, place):
        self.ref, (self.at, self.count, self.columns) = ref, place

    def get(self, begin=0, count=None):
        begin = self.at + begin
        return self.ref[begin : begin + (count or self.count), : self.columns]

    def put(self, values, begin=0):
        begin = self.at + begin
        self.ref[begin : begin + values.shape[0], : self.columns] = values


def named(z, *refs):
    tables = {}
    for ref, (places, _) in zip(refs, parts(z)):
        tables |= {name: Table(ref, place) for name, place in places.items()}
    return tables


def copies_in(sources, targets, sems):
    copies = [
        pltpu.make_async_copy(source, target, sems.at[i])
        for i, (source, target) in enumerate(zip(sources, targets))
    ]
    for copy in copies:
        copy.start()
    return copies


def pack_kernel(z, state_hbm, leg_hbm, gauss_hbm, out_ref, state_ref, leg_ref, gauss_ref, sems, rows_s):
    bf, f32 = jnp.bfloat16, jnp.float32
    copies = copies_in((state_hbm, leg_hbm, gauss_hbm), (state_ref, leg_ref, gauss_ref), sems)
    for copy in copies:
        copy.wait()
    row = lax.broadcasted_iota(jnp.int32, (z.fine_rows, LANES), 0)
    lane = lax.broadcasted_iota(jnp.int32, (z.fine_rows, LANES), 1)
    for a in range(z.lev_dev):
        for b in range(z.nodes):
            n = (a * z.nodes + b) * 2
            for s in range(z.slots):
                rows_s[s, n : n + 2, :] = state_ref[a, b, s]
    if z.state_rows > z.dev_rows:
        for s in range(z.slots):
            rows_s[s, z.dev_rows :, :] = jnp.zeros((z.state_rows - z.dev_rows, z.fine_rows), f32)
    table = jnp.zeros((z.lats, LANES), f32)
    state = jnp.zeros((z.state_rows, LANES), f32)
    extra = jnp.zeros((SUBLANES, LANES), f32)
    for s in range(z.slots):
        target = jnp.where(row < z.coarse, s * z.coarse + row, z.head + s * z.rest + row - z.coarse)
        leg = leg_ref[s].astype(f32)
        spec = rows_s[s]
        place = (target == lane).astype(bf)
        table = table + matmul(leg.astype(bf), place)
        state = state + matmul(spec.astype(bf), place)
        if z.head + (s + 1) * z.rest > LANES:
            for q in range(z.groups):
                at = q * SUBLANES
                part = leg[at : at + SUBLANES] if at < z.lats else spec[at - z.lats : at - z.lats + SUBLANES]
                place = ((target >= LANES) & (target - LANES + q * z.unit == lane)).astype(bf)
                extra = extra + matmul(part.astype(bf), place)
    wide_row = lax.broadcasted_iota(jnp.int32, (SUBLANES, z.lats), 0)
    wide_lane = lax.broadcasted_iota(jnp.int32, (SUBLANES, z.lats), 1)
    out_lane = lax.broadcasted_iota(jnp.int32, (SUBLANES, LANES), 1)
    for q in range(z.lats // SUBLANES):
        chosen = jnp.where(wide_lane == wide_row + q * SUBLANES, gauss_ref[...], 0.0)
        column = jnp.sum(chosen, axis=1, keepdims=True)
        high = column.astype(bf).astype(f32)
        at = q * z.unit + z.used - LANES
        extra = extra + jnp.where(out_lane == at, high, 0.0)
        extra = extra + jnp.where(out_lane == at + 1, column - high, 0.0)
    block = jnp.concatenate([table, extra, state], 0).astype(bf)
    for i in range(z.chips):
        out_ref[i] = block


def mix_matrix(pick_left, matrix, pick_right, mask):
    bf, f32 = jnp.bfloat16, jnp.float32
    high, low = high_low(matrix)
    left = pick_left.astype(bf)
    halves = jnp.concatenate([matmul(left, high).astype(bf), matmul(left, low).astype(bf)], 1)
    return (matmul(halves, pick_right.astype(bf)) * mask.astype(f32)).astype(bf)


def tables_kernel(z, layout, rate_ref, fold_smem, *refs):
    inputs, outputs, scratch = refs[:9], refs[9:12], refs[12:]
    (scaled_s, sems), staged = scratch[:2], scratch[2:]
    copies = copies_in(inputs, staged, sems)
    fold_ref, coef_ref, basis_ref, spread_ref = staged[:4]
    sampled_ref, coarse_sampled_ref, from_ref, to_ref, picks_ref = staged[4:]
    out = named(z, *outputs)
    bf, f32 = jnp.bfloat16, jnp.float32
    lev = lax.axis_index("lev")
    core = lax.rem(lev, 2)
    waves, coarse = z.fine_width, z.coarse
    half = z.fine_columns

    wide = 2 * LANES
    lane = lax.broadcasted_iota(jnp.int32, (1, wide), 1)
    lane_slot = jnp.full((1, wide), -1, jnp.int32)
    lane_row = jnp.zeros((1, wide), jnp.int32)
    for s in range(z.slots):
        for begin, width, first in ((s * coarse, coarse, 0), (z.head + s * z.rest, z.rest, coarse)):
            inside = (lane >= begin) & (lane < begin + width)
            lane_slot = jnp.where(inside, s, lane_slot)
            lane_row = jnp.where(inside, lane - begin + first, lane_row)
    rate_row = lax.broadcasted_iota(jnp.int32, (z.per_node, LANES), 0)
    rates = jnp.zeros((z.per_node, LANES), f32)
    for q in range(z.levels):
        rates = jnp.where((rate_row >= 2 * q) & (rate_row < 2 * q + 2), rate_ref[q], rates)
    for w in range(z.n_wave):
        small = jnp.zeros((1, wide), jnp.int32)
        for s in range(z.slots):
            small = jnp.where(lane_slot == s, fold_smem[w * z.slots + s], small)
        first = lane_row < waves - small
        keep = (lane < z.head) & (lane_row < coarse - small)
        out["keep"].put(keep[:, :LANES].astype(f32), w)
        for s in range(z.slots):
            own = lane_slot == s
            at = (w * z.slots + s) * 2
            out["member"].put((own & first).astype(f32), at)
            out["member"].put((own & jnp.logical_not(first)).astype(f32), at + 1)
            out["slot"].put((own & keep)[:, :LANES].astype(f32), w * z.slots + s)
        degree = (small + lane_row)[:, :LANES].astype(f32)
        stiff = rates * (degree * (degree + 1.0) / (coarse * (coarse + 1.0)))
        out["stiff"].put(stiff, w * z.per_node)
        out["inverse"].put(1.0 / (1.0 + STEP_HALF * stiff), w * z.per_node)

    for copy in copies[:3]:
        copy.wait()

    def wave_column(count, per_slot):
        row = lax.broadcasted_iota(jnp.int32, (count, z.coarse_columns), 0)
        lane = lax.broadcasted_iota(jnp.int32, (count, z.coarse_columns), 1)
        inside = (row >= lane * per_slot) & (row < (lane + 1) * per_slot)
        small = jnp.sum(jnp.where(inside, fold_ref[...].astype(f32), 0.0), axis=1, keepdims=True)
        if per_slot == 1:
            return small
        first = lax.broadcasted_iota(jnp.int32, (count, 1), 0) & 1
        return jnp.where(first == 0, small, waves - 1 - small)

    def one_hot(count, per_slot, width):
        column = wave_column(count, per_slot)
        lane = lax.broadcasted_iota(jnp.int32, (count, 2 * width), 1).astype(f32)
        extra = width - coarse
        top = lane == jnp.where(column < coarse, column, column + coarse)
        bottom = lane == jnp.where(column < coarse, column + coarse, column + coarse + extra)
        return jnp.concatenate([top.astype(f32), bottom.astype(f32)], 0).astype(bf)

    hot = one_hot(half, 2, waves)
    coarse_hot = one_hot(z.coarse_columns, 1, coarse)
    short, long = 2 * coarse, 2 * (waves - coarse)
    levels = [(2 * x + core) * z.lev_dev + al for x in range(z.n_pair) for al in range(z.lev_dev)]
    period = basis_ref.shape[1]
    row = lax.broadcasted_iota(jnp.int32, (2 * waves, 1), 0)
    count = jnp.where(row < short, coarse, waves - coarse)
    wave = jnp.where(row < short, row, row - short)
    wave = jnp.where(wave < count, wave, wave - count) + jnp.where(row < short, 0, coarse)
    sign = (1 - 2 * (wave & 1)).astype(f32)
    chunk = LANES
    lines = [coef_ref[pl.ds(level, 1), :] for level in levels]
    for begin in range(0, period, chunk):
        span = slice(begin, begin + chunk)
        values = basis_ref[:, span].astype(f32)
        signed = values * sign
        for a, line in enumerate(lines):
            near = line[:, span] * values
            far = line[:, period + begin : period + begin + chunk] * signed
            for side, scaled in enumerate((near + far, near - far)):
                scaled_s[side, a * short : (a + 1) * short, span] = scaled[:short].astype(bf)
                at = z.own_levels * short + a * long
                scaled_s[side, at : at + long, span] = scaled[short:].astype(bf)
    for copy in copies[3:]:
        copy.wait()
    out["wave"].put(matmul_nt(sampled_ref[...], hot).astype(bf))
    out["coarse_wave"].put(matmul_nt(coarse_sampled_ref[...], coarse_hot).astype(bf))
    even = matmul(scaled_s[0], spread_ref[0])
    odd = matmul(scaled_s[1], spread_ref[1])
    total, delta = even + odd, even - odd
    middle, top = z.points // 2, z.own_levels * short
    quad = jnp.concatenate([total[:, :middle], delta[:, :middle]], 1).astype(bf)
    coarse_quad = jnp.concatenate([total[:top, middle:], delta[:top, middle:]], 1).astype(bf)
    for a in range(z.own_levels):
        at = z.own_levels * short + a * long
        pair = jnp.concatenate([quad[a * short : (a + 1) * short], quad[at : at + long]], 0)
        values = matmul(hot, pair).astype(bf)
        out["quad"].put(values, a * values.shape[0])
        values = matmul(coarse_hot, coarse_quad[a * short : (a + 1) * short]).astype(bf)
        out["coarse_quad"].put(values, a * values.shape[0])

    def pick(name, index=0):
        at, height, count, columns = layout[name]
        return picks_ref[pl.ds(pl.multiple_of(at + index * height, 2 * SUBLANES), count), :columns]

    def mix(left, matrix, right, mask):
        return mix_matrix(left, matrix[...], right, mask)

    out["mix_to"].put(mix(pick("to_left"), to_ref, pick("to_right", core), pick("to_mask")))
    out["mix_from"].put(mix(pick("from_left", core), from_ref, pick("from_right"), pick("from_mask")))
    out["mix_back"].put(mix(pick("back_left"), to_ref, pick("back_right", core), pick("from_mask")))
    out["lift"].put(mix(pick("lift_left", lev), from_ref, pick("lift_right"), pick("lift_mask")))


def sweep_kernel(
    z,
    own_ref,
    other_ref,
    state_ref,
    narrow_hbm,
    full_hbm,
    quads_hbm,
    other_quads_hbm,
    corrected_ref,
    tend_ref,
    leg_s,
    state_s,
    fourier_s,
    back_s,
    tend_s,
    coarse_s,
    coarse_back_s,
    change_s,
    narrow_ref,
    full_ref,
    quads_ref,
    other_quads_ref,
    sems,
    legendre_s,
    product_s,
    coarse_product_s,
):
    bf, f32 = jnp.bfloat16, jnp.float32
    slots, rows, lats, per_node = z.slots, z.rows, z.lats, z.per_node
    table = named(z, narrow_ref, full_ref)
    quads = [named(z, *[ref] * 3) for ref in (quads_ref, other_quads_ref)]
    masks = pl.ds(0, z.fine_columns)
    others = pl.ds(z.fine_columns, full_ref.shape[0] - z.fine_columns)
    copies = copies_in(
        (full_hbm.at[masks], narrow_hbm, full_hbm.at[others], quads_hbm, other_quads_hbm),
        (full_ref.at[masks], narrow_ref, full_ref.at[others], quads_ref, other_quads_ref),
        sems,
    )

    def quad(name, a, count):
        lev, inner = a // z.lev_dev, a % z.lev_dev
        return quads[lev % 2][name].get((lev // 2 * z.lev_dev + inner) * count, count)

    wide = 2 * LANES
    all_lats = z.n_lev * lats

    def member(w, j):
        return table["member"].get(w * slots * 2 + j, 1)

    def slot(w, s):
        return table["slot"].get(w * slots + s, 1)

    def keep(w):
        return table["keep"].get(w, 1)

    for w in range(z.n_wave):
        for x in range(z.n_pair):
            for o, ref in enumerate((own_ref, other_ref)):
                d = 2 * x + o
                block = ref[z.position[w * z.n_pair + x]].astype(f32)
                extra = block[lats : lats + SUBLANES]
                leg_s[w, d * lats : (d + 1) * lats, :LANES] = block[:lats]
                state_at = d * z.dev_rows
                begin = lats + SUBLANES
                state_s[w, state_at : state_at + z.dev_rows, :LANES] = block[begin : begin + z.dev_rows]
                for q in range(z.groups):
                    moved = extra if q == 0 else pltpu.roll(extra, LANES - q * z.unit, 1)
                    at = q * SUBLANES
                    if at < lats:
                        leg_s[w, d * lats + at : d * lats + at + SUBLANES, LANES:] = moved
                    else:
                        at = at - lats
                        count = min(SUBLANES, z.dev_rows - at)
                        state_s[w, state_at + at : state_at + at + count, LANES:] = moved[:count]
        if all_lats < leg_s.shape[1]:
            leg_s[w, all_lats:, :] = jnp.zeros((leg_s.shape[1] - all_lats, wide), f32)
        legendre_s[w] = leg_s[w].astype(bf)

    lane = lax.broadcasted_iota(jnp.int32, (2 * SUBLANES, wide), 1)
    picked = ((lane == z.used) | (lane == z.used + 1)).astype(bf)
    gauss = matmul_nt(picked, legendre_s[0])[:1]

    inner = 2 * sum(z.head + (s + 1) * z.rest <= LANES for s in range(slots))
    spans = [(0, inner, LANES), (inner, 2 * slots, wide)]
    copies[0].wait()
    for w in range(z.n_wave):
        state = state_s[w]
        for first, last, width in spans:
            left = [state[:, :width] * member(w, j)[:, :width] for j in range(first, last)]
            left = jnp.concatenate(left, 0).astype(bf)
            out = matmul_nt(left, legendre_s[w, :, :width])
            for j in range(first, last):
                at = (w * 2 * slots + j) * z.row_pitch
                fourier_s[at : at + rows, :] = out[(j - first) * rows : (j - first + 1) * rows]

    for copy in copies[1:]:
        copy.wait()
    both = 2 * z.fine_columns
    half = z.fine_columns
    for a in range(z.levels):
        pieces = []
        for b in range(z.nodes):
            at = (a * z.nodes + b) * 2
            piece = [fourier_s[pl.ds(at + c, half, stride=z.row_pitch), :] for c in range(2)]
            pieces.append(jnp.concatenate(piece, 0).astype(bf))
        grid = matmul(table["wave"].get(), jnp.concatenate(pieces, 1))
        product_s[a] = (grid * grid).astype(bf)
    for a in range(z.levels):
        back = matmul(quad("quad", a, both), product_s[a])
        for b in range(z.nodes):
            values = back[:, b * LANES : (b + 1) * LANES] * gauss
            for c in range(2):
                at = ((a * z.nodes + b) * 2 + c) * z.column_pitch
                back_s[at : at + half, :] = values[c * half : (c + 1) * half]

    stacked = []
    for w in range(z.n_wave):
        outs = []
        for first, last, width in spans:
            left = [
                back_s[pl.ds(w * 2 * slots + j, rows, stride=z.column_pitch), :].astype(bf)
                for j in range(first, last)
            ]
            out = matmul(jnp.concatenate(left, 0), legendre_s[w, :, :width])
            outs += [out[i * rows : (i + 1) * rows] for i in range(last - first)]
        total, beyond = outs[-1][:, :LANES], outs[-1][:, LANES:]
        for j in range(2 * slots - 1):
            chosen = member(w, j) > 0.5
            total = jnp.where(chosen[:, :LANES], outs[j][:, :LANES], total)
            if j >= inner:
                beyond = jnp.where(chosen[:, LANES:], outs[j][:, LANES:], beyond)
        tend_s[w, :rows, :LANES] = total
        tend_s[w, :rows, LANES:] = beyond
        stacked.append(state_s[w][:, :LANES] * keep(w))
        stacked.append(total * keep(w))

    modes = matmul_split(table["mix_to"].get(), jnp.concatenate(stacked, 1))
    evals, later, old_of, mid_of = [], [], [], []
    for w in range(z.n_wave):
        old, source = [], []
        stiff = table["stiff"].get(w * per_node, per_node)
        for b in range(z.nodes):
            part = modes[b * per_node : (b + 1) * per_node]
            old.append(part[:, 2 * w * LANES : (2 * w + 1) * LANES])
            source.append(part[:, (2 * w + 1) * LANES : (2 * w + 2) * LANES] - stiff * old[-1])
        inverse = table["inverse"].get(w * per_node, per_node)
        mid = sum(quad_weights[0][b] * source[b] for b in range(z.nodes))
        mid = (mid + old[0] + STEP_HALF * stiff * old[1]) * inverse
        end = sum(quad_weights[1][b] * source[b] for b in range(z.nodes))
        end = end + mid + STEP_HALF * stiff * old[2]
        evals.append(old[1])
        evals.append(mid)
        later.append((end, inverse))
        old_of.append(old)
        mid_of.append(mid)

    level_values = matmul_split(table["mix_from"].get(), jnp.concatenate(evals, 1))
    for w in range(z.n_wave):
        left = jnp.concatenate(
            [
                level_values[:, (2 * w + e) * LANES : (2 * w + e + 1) * LANES] * slot(w, s)
                for s in range(slots)
                for e in range(2)
            ],
            0,
        ).astype(bf)
        out = matmul_nt(left, legendre_s[w, :, :LANES])
        for s in range(slots):
            at = (w * slots + s) * z.mode_pitch
            coarse_s[at : at + 2 * per_node, :] = out[s * 2 * per_node : (s + 1) * 2 * per_node]

    both_c = 2 * z.coarse_columns
    for a in range(z.levels):
        pieces = []
        for e in range(2):
            at = e * per_node + a * 2
            piece = [
                coarse_s[pl.ds(at + c, z.coarse_columns, stride=z.mode_pitch), :] for c in range(2)
            ]
            pieces.append(jnp.concatenate(piece, 0).astype(bf))
        grid = matmul(table["coarse_wave"].get(), jnp.concatenate(pieces, 1))
        before, fresh = grid[:, :LANES], grid[:, LANES:]
        coarse_product_s[a] = (fresh * fresh - before * before).astype(bf)
    for a in range(z.levels):
        back = matmul(quad("coarse_quad", a, both_c), coarse_product_s[a])
        values = back * gauss
        for c in range(2):
            at = (a * 2 + c) * z.slot_pitch
            coarse_back_s[at : at + z.coarse_columns, :] = values[c * z.coarse_columns :][: z.coarse_columns]

    tends = []
    for w in range(z.n_wave):
        left = jnp.concatenate(
            [
                coarse_back_s[pl.ds(w * slots + s, per_node, stride=z.slot_pitch), :].astype(bf)
                for s in range(slots)
            ],
            0,
        )
        out = matmul(left, legendre_s[w, :, :LANES])
        total = None
        for s in range(slots):
            term = slot(w, s) * out[s * per_node : (s + 1) * per_node]
            total = term if total is None else total + term
        tends.append(total)
    coarse_modes = matmul_split(table["mix_back"].get(), jnp.concatenate(tends, 1))
    for w in range(z.n_wave):
        end, inverse = later[w]
        end = (end + STEP_HALF * coarse_modes[:, w * LANES : (w + 1) * LANES]) * inverse
        change_s[w, :per_node, :] = mid_of[w] - old_of[w][1]
        change_s[w, per_node:, :] = end - old_of[w][2]

    place = lax.axis_index("wave")
    begin = pl.multiple_of(lax.div(lax.axis_index("lev"), 2) * (2 * z.dev_rows), SUBLANES)
    mine = tend_s[place, pl.ds(begin, z.state_rows), :]
    raised = matmul_split(table["lift"].get(), change_s[place])
    lane = lax.broadcasted_iota(jnp.int32, (z.state_rows, wide), 1)
    for s in range(slots):
        low = mine if s == 0 else pltpu.roll(mine, wide - s * z.coarse, 1)
        high = pltpu.roll(mine, wide - (z.head + s * z.rest - z.coarse), 1)
        values = jnp.where(lane < z.coarse, low, high)
        for n in range(0, z.dev_rows, 2):
            tend_ref[n // (z.nodes * 2), n // 2 % z.nodes, s] = values[n : n + 2, : z.fine_rows]
        low = raised if s == 0 else pltpu.roll(raised, LANES - s * z.coarse, 1)
        low = jnp.where(lane[: low.shape[0], :LANES] < z.coarse, low, 0.0)
        for n in range(0, low.shape[0], 2):
            a, b = n // (2 * (z.nodes - 1)), n // 2 % (z.nodes - 1)
            corrected_ref[a, b, s] = state_ref[a, b + 1, s] + low[n : n + 2, : z.fine_rows]


def mix_constants(z):
    level, node, part = np.arange(z.levels), np.arange(z.nodes), np.arange(2)

    def pick(index):
        return (np.asarray(index)[:, None] == level[None, :]).astype(np.float32)

    def grid(*axes):
        return [m.reshape(-1) for m in np.meshgrid(*axes, indexing="ij")]

    def ordered(index, core):
        lev, inner = index // z.lev_dev, index % z.lev_dev
        return (lev ^ core) * z.lev_dev + inner

    def thrice(matrix):
        return np.concatenate([matrix] * 3, -1)

    def halves(matrix):
        zero = np.zeros_like(matrix)
        return np.concatenate(
            [np.concatenate([matrix, matrix, zero], 1), np.concatenate([zero, zero, matrix], 1)]
        )

    rb, rq, rc = grid(node, level, part)
    ca, cb, cc = grid(level, node, part)
    sa, sc = grid(level, part)
    to_mask = (rb[:, None] == cb[None]) & (rc[:, None] == cc[None])
    same_part = sc[:, None] == sc[None]
    la, lb, lc = grid(np.arange(z.lev_dev), np.arange(z.nodes - 1), part)
    kb, kq, kc = grid(np.arange(z.nodes - 1), level, part)
    lift_mask = (lb[:, None] == kb[None]) & (lc[:, None] == kc[None])
    by_core = range(2)
    constants = dict(
        to_left=[pick(rq)],
        to_right=[halves(pick(ordered(ca, k)).T) for k in by_core],
        to_mask=[thrice(to_mask)],
        from_left=[pick(ordered(sa, k)) for k in by_core],
        from_right=[halves(pick(sa).T)],
        from_mask=[thrice(same_part)],
        back_left=[pick(sa)],
        back_right=[halves(pick(ordered(sa, k)).T) for k in by_core],
        lift_left=[pick(k * z.lev_dev + la) for k in range(z.n_lev)],
        lift_right=[halves(pick(kq).T)],
        lift_mask=[thrice(lift_mask)],
    )
    wide = max(m[0].shape[1] for m in constants.values())
    layout, rows, at = {}, [], 0
    for name, members in constants.items():
        count, columns = members[0].shape
        height = round_up(count, 2 * SUBLANES)
        layout[name] = (at, height, count, columns)
        at += height * len(members)
        rows += [np.pad(m, ((0, height - count), (0, wide - columns))) for m in members]
    return layout, jnp.asarray(np.concatenate(rows), jnp.bfloat16)


def replicated_plan(
    fine_state, fold_pairs, legendre, gauss_weights, grid_coef, modes_from, modes_to, mode_rates
):
    z = Sizes(fine_state, legendre)
    bf, f32 = jnp.bfloat16, jnp.float32
    longitudes = grid_coef.shape[1]
    vmem = pl.BlockSpec(memory_space=pltpu.VMEM)
    smem = pl.BlockSpec(memory_space=pltpu.SMEM)
    hbm = pl.BlockSpec(memory_space=pltpu.HBM)
    shape = jax.ShapeDtypeStruct
    stored = jnp.swapaxes(fine_state, 2, 3)
    block = pl.pallas_call(
        functools.partial(pack_kernel, z),
        out_shape=shape((z.chips, z.block_rows, LANES), bf),
        in_specs=[hbm] * 3,
        out_specs=vmem,
        scratch_shapes=[
            pltpu.VMEM(stored.shape, f32),
            pltpu.VMEM(legendre.shape, bf),
            pltpu.VMEM((1, z.lats), f32),
            pltpu.SemaphoreType.DMA((3,)),
            pltpu.VMEM((z.slots, z.state_rows, z.fine_rows), f32),
        ],
        name="pack",
    )(stored, legendre, gauss_weights[None])
    groups = [[2 * i + c for i in z.order] for c in range(2)]
    own = lax.all_to_all(
        block, ("wave", "lev"), 0, 0, tiled=True, axis_index_groups=groups
    )
    fine_amp, coarse_amp = z.fine_width**-0.5, z.coarse**-0.5
    order = np.arange(2 * z.fine_width).reshape(2, -1)
    order = np.concatenate([order[:, : z.coarse].reshape(-1), order[:, z.coarse :].reshape(-1)])
    basis = wave_rows(z.fine_width, longitudes, fine_amp)[order]
    spread = interpolation(z.points, longitudes, 2 * (z.fine_width - 1))
    spread *= 2.0 * z.fine_width / longitudes
    coarse_spread = interpolation(z.coarse_points, longitudes, 2 * (z.coarse - 1))
    coarse_spread *= 2.0 * z.coarse / (longitudes // 2) * (coarse_amp / fine_amp)
    coarse_spread[1::2] = 0.0
    spread = np.stack(
        [
            np.concatenate([folded(spread, side), folded(coarse_spread, side)], 1)
            for side in (0.5, -0.5)
        ]
    )
    sampled = wave_rows(z.fine_width, z.points, fine_amp)[order].T
    coarse_sampled = wave_rows(z.coarse, z.coarse_points, coarse_amp).T
    basis = basis[:, : longitudes // 2]
    constants = [jnp.asarray(c, bf) for c in (basis, spread, sampled, coarse_sampled)]
    layout, picks = mix_constants(z)
    staged = [fold_pairs[None], grid_coef, *constants, modes_from, modes_to, picks]
    wide = 2 * LANES
    narrow_shape, full_shape, quads_shape = [entry[1] for entry in parts(z)]
    narrow, full, quads = pl.pallas_call(
        functools.partial(tables_kernel, z, layout),
        out_shape=(shape(narrow_shape, bf), shape(full_shape, f32), shape(quads_shape, bf)),
        in_specs=[smem, smem] + [hbm] * len(staged),
        out_specs=(vmem,) * 3,
        scratch_shapes=[
            pltpu.VMEM((2, z.own_levels * 2 * z.fine_width, longitudes // 2), bf),
            pltpu.SemaphoreType.DMA((len(staged),)),
        ]
        + [pltpu.VMEM(array.shape, array.dtype) for array in staged],
        cost_estimate=pl.CostEstimate(flops=10**9, bytes_accessed=4 * 10**6, transcendentals=0),
        name="tables",
    )(mode_rates, fold_pairs, *staged)

    partners = [(i, i ^ 1) for i in range(2 * z.chips)]
    other_quads = lax.ppermute(quads, ("wave", "lev"), partners)
    own, narrow = lax.optimization_barrier((own, narrow))
    other = lax.ppermute(own, ("wave", "lev"), partners)

    lat_rows = round_up(z.n_lev * z.lats, LANES)
    corrected, fine_tend = pl.pallas_call(
        functools.partial(sweep_kernel, z),
        out_shape=(
            shape((z.lev_dev, z.nodes - 1, z.slots, 2, z.fine_rows), f32),
            shape(stored.shape, f32),
        ),
        in_specs=[vmem] * 3 + [hbm] * 4,
        out_specs=(vmem, vmem),
        scratch_shapes=[
            pltpu.VMEM((z.n_wave, lat_rows, wide), f32),
            pltpu.VMEM((z.n_wave, z.rows, wide), f32),
            pltpu.VMEM((z.row_pitch * z.fine_columns, lat_rows), f32),
            pltpu.VMEM((z.rows * z.column_pitch, lat_rows), f32),
            pltpu.VMEM((z.n_wave, z.rows + SUBLANES, wide), f32),
            pltpu.VMEM((z.mode_pitch * z.coarse_columns, lat_rows), f32),
            pltpu.VMEM((z.per_node * z.slot_pitch, lat_rows), f32),
            pltpu.VMEM((z.n_wave, (z.nodes - 1) * z.per_node, LANES), f32),
            pltpu.VMEM(narrow_shape, bf),
            pltpu.VMEM(full_shape, f32),
            pltpu.VMEM(quads_shape, bf),
            pltpu.VMEM(quads_shape, bf),
            pltpu.SemaphoreType.DMA((5,)),
            pltpu.VMEM((z.n_wave, lat_rows, wide), bf),
            pltpu.VMEM((z.levels, z.points, z.nodes * LANES), bf),
            pltpu.VMEM((z.levels, z.coarse_points, LANES), bf),
        ],
        compiler_params=pltpu.CompilerParams(vmem_limit_bytes=VMEM_BYTES),
        name="sweep",
    )(own, other, stored, narrow, full, quads, other_quads)
    return (jnp.swapaxes(corrected, 2, 3), jnp.swapaxes(fine_tend, 2, 3))


def fits_replicated(fine_state, legendre):
    n_wave, n_lev = lax.axis_size("wave"), lax.axis_size("lev")
    if n_lev % 2 or fine_state.shape[1] != len(quad_weights[0]):
        return False
    z = Sizes(fine_state, legendre)
    gathered = 32 * n_wave * n_lev * (legendre.size + fine_state.size)
    return (
        z.head <= LANES
        and z.used > LANES
        and z.used + 2 - LANES <= z.unit
        and z.lats % SUBLANES == 0
        and z.head + z.rest <= LANES
        and n_lev * z.lats <= LANES
        and gathered <= REPLICATED_BYTES
    )


def per_device(fine_state, fold_pairs, legendre, *rest):
    plan = replicated_plan if fits_replicated(fine_state, legendre) else split_plan
    return plan(fine_state, fold_pairs, legendre, *rest)


def solution(mesh):
    placed = (
        P("lev", None, None, "wave", None),
        P(),
        P("wave", "lev", None),
        P("lev"),
        P(),
        P(),
        P(),
        P(),
    )
    return jax.shard_map(
        per_device,
        mesh=mesh,
        in_specs=placed,
        out_specs=(P("lev", None, None, "wave", None), P("lev", None, None, "wave", None)),
        check_vma=False,
    )
```

```python
import functools
import math

import jax
import jax.numpy as jnp
import numpy as np
from jax import lax
from jax.experimental import pallas as pl
from jax.experimental.pallas import tpu as pltpu
from jax.sharding import PartitionSpec as P

STEP_HALF = 0.5
quad_weights = ((5.0 / 24.0, 1.0 / 3.0, -1.0 / 24.0), (-1.0 / 24.0, 1.0 / 3.0, 5.0 / 24.0))
HIGHEST = lax.Precision.HIGHEST


def fourier_table(waves, points, amplitude):
    steps = jnp.arange(points, dtype=jnp.int32)
    turns = waves[:, :, None] * steps[None, None, :] % points
    angles = turns.astype(jnp.float32) * (2.0 * math.pi / points)
    return jnp.stack([jnp.cos(angles) * amplitude, -jnp.sin(angles) * amplitude]).astype(
        jnp.bfloat16
    )


def fine_rows(small_wave, fine_width):
    row_ids = jnp.arange(fine_width + 1, dtype=jnp.int32)[None, :]
    return row_ids < fine_width - small_wave[:, None]


def coarse_rows(small_wave, coarse):
    row_ids = jnp.arange(coarse, dtype=jnp.int32)[None, :]
    coarse_keep = row_ids < coarse - small_wave[:, None]
    degree = (small_wave[:, None] + row_ids).astype(jnp.float32)
    return (coarse_keep, degree)


def legendre_inverse(spectral, legendre_table, row_mask):
    split_spec = spectral[:, :, :, :, None, :] * row_mask[None, None, None]
    return jnp.einsum(
        "abcpmr,plr->abcpml", split_spec, legendre_table, preferred_element_type=jnp.float32
    ).astype(jnp.bfloat16)


def legendre_forward(returned, legendre_table, row_mask):
    members = jnp.einsum(
        "abcpml,plr->abcpmr", returned, legendre_table, preferred_element_type=jnp.float32
    )
    return jnp.sum(members * row_mask.astype(jnp.float32)[None, None, None], axis=4)


def grid_step(fourier, wave_table, coef, weights, factor):
    grid_field = jnp.einsum(
        "abcpmz,cpmk->abzk", fourier, wave_table, preferred_element_type=jnp.float32
    )
    product = (coef[:, None, None, :] * grid_field * grid_field).astype(jnp.bfloat16)
    returned = jnp.einsum(
        "abzk,cpmk->abcpmz", product, wave_table, preferred_element_type=jnp.float32
    )
    return (returned * (weights * factor)).astype(jnp.bfloat16)


def mix(matrix, values):
    return jnp.einsum("ql,lbcpr->qbcpr", matrix, values, precision=HIGHEST)


def split_plan(
    fine_state, fold_pairs, legendre, gauss_weights, grid_coef, modes_from, modes_to, mode_rates
):
    n_wave = lax.axis_size("wave")
    wave_idx = lax.axis_index("wave")
    lev_idx = lax.axis_index("lev")
    lev_dev = fine_state.shape[0]
    pairs_dev = fine_state.shape[3]
    fine_width = fine_state.shape[4] - 1
    coarse = fine_width // 2
    longitudes = grid_coef.shape[1]
    band_size = legendre.shape[1] // n_wave
    small_wave = lax.dynamic_slice_in_dim(fold_pairs, wave_idx * pairs_dev, pairs_dev)
    first_member = fine_rows(small_wave, fine_width)
    member_mask = jnp.stack([first_member, jnp.logical_not(first_member)], 1).astype(jnp.bfloat16)
    coarse_keep, degree = coarse_rows(small_wave, coarse)
    keep_mask = coarse_keep[:, None, :].astype(jnp.bfloat16)
    keep_float = coarse_keep.astype(jnp.float32)
    fine_table = fourier_table(
        jnp.stack([fold_pairs, fine_width - 1 - fold_pairs], 1), longitudes, fine_width ** (-0.5)
    )
    coarse_table = fourier_table(fold_pairs[:, None], longitudes // 2, coarse ** (-0.5))
    coarse_leg = legendre[:, :, :coarse]
    coarse_coef = grid_coef[:, ::2]
    band_gauss = lax.dynamic_slice_in_dim(gauss_weights, wave_idx * band_size, band_size)
    local_to = lax.dynamic_slice_in_dim(modes_to, lev_idx * lev_dev, lev_dev, 1)
    local_from = lax.dynamic_slice_in_dim(modes_from, lev_idx * lev_dev, lev_dev, 1)
    mode_decay = lax.dynamic_slice_in_dim(mode_rates, lev_idx * lev_dev, lev_dev)

    def project(partial_sum):
        return mix(modes_to, partial_sum)

    def coarse_start(modes):
        gathered = lax.all_gather(modes, "lev", axis=0, tiled=True)
        levels = (mix(modes_from, gathered) * keep_float).astype(jnp.bfloat16)
        return legendre_inverse(levels, coarse_leg, keep_mask)

    def coarse_grid_step(fourier):
        return grid_step(
            fourier, coarse_table, coarse_coef, band_gauss, 2.0 * coarse / (longitudes // 2)
        )

    def coarse_finish(returned):
        partial_sum = legendre_forward(returned, coarse_leg, keep_mask)
        return lax.psum_scatter(
            project(partial_sum).astype(jnp.bfloat16), "lev", scatter_dimension=0, tiled=True
        ).astype(jnp.float32)

    def coarse_eval(modes):
        fourier = lax.all_to_all(
            coarse_start(modes), "wave", split_axis=5, concat_axis=3, tiled=True
        )
        returned = lax.all_to_all(
            coarse_grid_step(fourier), "wave", split_axis=3, concat_axis=5, tiled=True
        )
        return coarse_finish(returned)

    restricted = fine_state[..., :coarse] * keep_float
    fine_spec = lax.all_gather(fine_state.astype(jnp.bfloat16), "lev", axis=0, tiled=True)
    fine_fourier = legendre_inverse(fine_spec, legendre, member_mask)
    fine_fourier = lax.all_to_all(fine_fourier, "wave", split_axis=5, concat_axis=3, tiled=True)
    fine_back = lax.all_to_all(
        grid_step(fine_fourier, fine_table, grid_coef, band_gauss, 2.0 * fine_width / longitudes),
        "wave",
        split_axis=3,
        concat_axis=5,
        tiled=True,
    )
    fine_tend = lax.psum_scatter(
        legendre_forward(fine_back, legendre, member_mask).astype(jnp.bfloat16),
        "lev",
        scatter_dimension=0,
        tiled=True,
    ).astype(jnp.float32)
    restricted_tend = fine_tend[..., :coarse] * keep_float
    stacked = jnp.concatenate([restricted, restricted_tend], 1)
    both_modes = lax.psum_scatter(
        mix(local_to, stacked).astype(jnp.bfloat16), "lev", scatter_dimension=0, tiled=True
    ).astype(jnp.float32)
    nodes = fine_state.shape[1]
    old_state = both_modes[:, :nodes]
    old_tend = both_modes[:, nodes:]
    old_coarse = coarse_eval(old_state[:, 1:2])
    stiffness = (
        mode_decay[:, None, None, None]
        * (degree * (degree + 1.0) / (coarse * (coarse + 1.0)))[None, None]
    )
    source = old_tend - stiffness[:, None] * old_state
    integral_mid = (
        quad_weights[0][0] * source[:, 0]
        + quad_weights[0][1] * source[:, 1]
        + quad_weights[0][2] * source[:, 2]
    )
    integral_end = (
        quad_weights[1][0] * source[:, 0]
        + quad_weights[1][1] * source[:, 1]
        + quad_weights[1][2] * source[:, 2]
    )
    divisor = 1.0 + STEP_HALF * stiffness
    next_mid = (old_state[:, 0] + STEP_HALF * stiffness * old_state[:, 1] + integral_mid) / divisor
    coarse_fresh = coarse_eval(next_mid[:, None])
    next_end = (
        next_mid
        + STEP_HALF * (coarse_fresh[:, 0] - old_coarse[:, 0])
        + STEP_HALF * stiffness * old_state[:, 2]
        + integral_end
    ) / divisor
    change = jnp.stack([next_mid - old_state[:, 1], next_end - old_state[:, 2]], 1)
    lifted = lax.psum_scatter(
        mix(local_from, change).astype(jnp.bfloat16), "lev", scatter_dimension=0, tiled=True
    ).astype(jnp.float32)
    corrected = fine_state[:, 1:] + jnp.pad(
        lifted, ((0, 0), (0, 0), (0, 0), (0, 0), (0, fine_width + 1 - coarse))
    )
    return (corrected, fine_tend)


LANES = 128
SUBLANES = 8
REPLICATED_BYTES = 16 * 2**20
VMEM_BYTES = 56 * 10**6


def round_up(value, unit):
    return -(-value // unit) * unit


def interpolation(points, targets, degree):
    offset = (
        2.0 * np.pi * (np.arange(targets)[:, None] / targets - np.arange(points)[None, :] / points)
    )
    order = np.arange(1, degree + 1)
    return (1.0 + 2.0 * np.cos(offset[:, :, None] * order).sum(-1)) / points


def wave_rows(waves, points, amplitude):
    turns = np.arange(waves)[:, None] * np.arange(points)[None, :] % points
    angles = turns * (2.0 * np.pi / points)
    return np.concatenate([np.cos(angles), -np.sin(angles)]) * amplitude


def folded(table, side):
    near = table[: table.shape[0] // 2]
    middle = table.shape[1] // 2
    return 0.5 * near[:, :middle] + side * near[:, middle:]


def matmul(a, b):
    return jnp.dot(a, b, preferred_element_type=jnp.float32)


def matmul_nt(a, b):
    return lax.dot_general(a, b, (((1,), (1,)), ((), ())), preferred_element_type=jnp.float32)


def matmul_exact(a, b):
    return jnp.dot(a, b, preferred_element_type=jnp.float32, precision=lax.Precision.HIGHEST)


def high_low(values):
    high = values.astype(jnp.bfloat16)
    return high, (values - high.astype(jnp.float32)).astype(jnp.bfloat16)


def matmul_split(left, right):
    high, low = high_low(right)
    return matmul(left, jnp.concatenate([high, low, high], 0))


def pitch(count):
    return count + 4 if count % 8 == 0 else count


class Sizes:
    def __init__(self, fine_state, legendre):
        self.n_wave, self.n_lev = lax.axis_size("wave"), lax.axis_size("lev")
        self.lev_dev, self.nodes, _, self.slots, self.fine_rows = fine_state.shape
        self.lats = legendre.shape[1]
        self.n_pair = self.n_lev // 2
        self.fine_width = self.fine_rows - 1
        self.coarse = self.fine_width // 2
        self.levels = self.n_lev * self.lev_dev
        self.own_levels = self.n_pair * self.lev_dev
        self.dev_rows = self.lev_dev * self.nodes * 2
        self.rows = self.levels * self.nodes * 2
        self.per_node = self.levels * 2
        self.head = self.slots * self.coarse
        self.rest = self.fine_rows - self.coarse
        self.used = self.slots * self.fine_rows
        self.state_rows = round_up(self.dev_rows, SUBLANES)
        self.groups = (self.lats + self.state_rows) // SUBLANES
        self.unit = LANES // self.groups
        self.block_rows = self.lats + SUBLANES + self.state_rows
        self.chips = self.n_wave * self.n_pair
        lead = self.chips // 2 - 1
        self.order = [lead] + [i for i in range(self.chips) if i != lead]
        self.position = [self.order.index(i) for i in range(self.chips)]
        self.fine_columns = self.n_wave * self.slots * 2
        self.coarse_columns = self.n_wave * self.slots
        self.row_pitch = pitch(self.rows)
        self.column_pitch = pitch(self.fine_columns)
        self.mode_pitch = pitch(2 * self.per_node)
        self.slot_pitch = round_up(self.per_node, SUBLANES) + SUBLANES
        self.points = round_up(4 * (self.fine_width - 1) + 1, 32)
        self.coarse_points = round_up(4 * (self.coarse - 1) + 1, 32)


def parts(z):
    narrow = dict(
        wave=(z.points, 2 * z.fine_columns),
        coarse_wave=(z.coarse_points, 2 * z.coarse_columns),
        mix_to=(z.rows, 3 * z.rows),
        mix_from=(z.per_node, 3 * z.per_node),
        mix_back=(z.per_node, 3 * z.per_node),
        lift=(z.lev_dev * (z.nodes - 1) * 2, 3 * (z.nodes - 1) * z.per_node),
    )
    full = dict(
        member=(z.fine_columns, 2 * LANES),
        slot=(z.coarse_columns, LANES),
        keep=(z.n_wave, LANES),
        stiff=(z.n_wave * z.per_node, 2 * LANES),
    )

    def placed(shapes, unit):
        out, at = {}, 0
        for name, (count, columns) in shapes.items():
            out[name] = (at, count, columns)
            at += round_up(count, unit)
        return out, (at, max(columns for _, columns in shapes.values()))

    quads = dict(
        quad=(z.own_levels * 2 * z.fine_columns, z.points),
        coarse_quad=(z.own_levels * 2 * z.coarse_columns, z.coarse_points),
    )
    return [placed(shapes, 2 * SUBLANES) for shapes in (narrow, full, quads)]


class Table:
    def __init__(self, ref, place):
        self.ref, (self.at, self.count, self.columns) = ref, place

    def get(self, begin=0, count=None):
        begin = self.at + begin
        return self.ref[begin : begin + (count or self.count), : self.columns]

    def rows(self, block, count):
        begin = pl.multiple_of(self.at + block * count, SUBLANES)
        return self.ref[pl.ds(begin, count), : self.columns]

    def put(self, values, begin=0):
        begin = self.at + begin
        self.ref[begin : begin + values.shape[0], : self.columns] = values


def named(z, *refs):
    tables = {}
    for ref, (places, _) in zip(refs, parts(z)):
        tables |= {name: Table(ref, place) for name, place in places.items()}
    return tables


def copies_in(sources, targets, sems):
    copies = [
        pltpu.make_async_copy(source, target, sems.at[i])
        for i, (source, target) in enumerate(zip(sources, targets))
    ]
    for copy in copies:
        copy.start()
    return copies


def pack_kernel(z, state_hbm, leg_hbm, gauss_hbm, out_ref, state_ref, leg_ref, gauss_ref, sems, rows_s):
    bf, f32 = jnp.bfloat16, jnp.float32
    copies = copies_in((state_hbm, leg_hbm, gauss_hbm), (state_ref, leg_ref, gauss_ref), sems)
    for copy in copies:
        copy.wait()
    row = lax.broadcasted_iota(jnp.int32, (z.fine_rows, LANES), 0)
    lane = lax.broadcasted_iota(jnp.int32, (z.fine_rows, LANES), 1)
    for a in range(z.lev_dev):
        for b in range(z.nodes):
            n = (a * z.nodes + b) * 2
            for s in range(z.slots):
                rows_s[s, n : n + 2, :] = state_ref[a, b, s]
    if z.state_rows > z.dev_rows:
        for s in range(z.slots):
            rows_s[s, z.dev_rows :, :] = jnp.zeros((z.state_rows - z.dev_rows, z.fine_rows), f32)
    table = jnp.zeros((z.lats, LANES), f32)
    state = jnp.zeros((z.state_rows, LANES), f32)
    extra = jnp.zeros((SUBLANES, LANES), f32)
    for s in range(z.slots):
        target = jnp.where(row < z.coarse, s * z.coarse + row, z.head + s * z.rest + row - z.coarse)
        leg = leg_ref[s].astype(f32)
        spec = rows_s[s]
        place = (target == lane).astype(bf)
        table = table + matmul(leg.astype(bf), place)
        state = state + matmul(spec.astype(bf), place)
        if z.head + (s + 1) * z.rest > LANES:
            for q in range(z.groups):
                at = q * SUBLANES
                part = leg[at : at + SUBLANES] if at < z.lats else spec[at - z.lats : at - z.lats + SUBLANES]
                place = ((target >= LANES) & (target - LANES + q * z.unit == lane)).astype(bf)
                extra = extra + matmul(part.astype(bf), place)
    wide_row = lax.broadcasted_iota(jnp.int32, (SUBLANES, z.lats), 0)
    wide_lane = lax.broadcasted_iota(jnp.int32, (SUBLANES, z.lats), 1)
    out_lane = lax.broadcasted_iota(jnp.int32, (SUBLANES, LANES), 1)
    for q in range(z.lats // SUBLANES):
        chosen = jnp.where(wide_lane == wide_row + q * SUBLANES, gauss_ref[...], 0.0)
        column = jnp.sum(chosen, axis=1, keepdims=True)
        high = column.astype(bf).astype(f32)
        at = q * z.unit + z.used - LANES
        extra = extra + jnp.where(out_lane == at, high, 0.0)
        extra = extra + jnp.where(out_lane == at + 1, column - high, 0.0)
    block = jnp.concatenate([table, extra, state], 0).astype(bf)
    for i in range(z.chips):
        out_ref[i] = block


def mix_matrix(pick_left, matrix, pick_right, mask):
    bf, f32 = jnp.bfloat16, jnp.float32
    high, low = high_low(matrix)
    left = pick_left.astype(bf)
    halves = jnp.concatenate([matmul(left, high).astype(bf), matmul(left, low).astype(bf)], 1)
    return (matmul(halves, pick_right.astype(bf)) * mask.astype(f32)).astype(bf)


def tables_kernel(z, layout, *refs):
    inputs, outputs, scratch = refs[:10], refs[10:13], refs[13:]
    (scaled_s, sems), staged = scratch[:2], scratch[2:]
    copies = copies_in(inputs, staged, sems)
    fold_ref, rate_ref, coef_ref, basis_ref, spread_ref = staged[:5]
    sampled_ref, coarse_sampled_ref, from_ref, to_ref, picks_ref = staged[5:]
    out = named(z, *outputs)
    bf, f32 = jnp.bfloat16, jnp.float32
    lev = lax.axis_index("lev")
    core = lax.rem(lev, 2)
    waves, coarse = z.fine_width, z.coarse
    half = z.fine_columns

    wide = 2 * LANES
    lane = lax.broadcasted_iota(jnp.int32, (1, wide), 1)
    lane_slot = jnp.full((1, wide), -1, jnp.int32)
    lane_row = jnp.zeros((1, wide), jnp.int32)
    for s in range(z.slots):
        for begin, width, first in ((s * coarse, coarse, 0), (z.head + s * z.rest, z.rest, coarse)):
            inside = (lane >= begin) & (lane < begin + width)
            lane_slot = jnp.where(inside, s, lane_slot)
            lane_row = jnp.where(inside, lane - begin + first, lane_row)
    copies[0].wait()
    copies[1].wait()
    wave_row = lax.broadcasted_iota(jnp.int32, (z.n_wave, z.coarse_columns), 0)
    fold_lane = lax.broadcasted_iota(jnp.int32, (z.n_wave, z.coarse_columns), 1)
    small = jnp.zeros((z.n_wave, wide), f32)
    for s in range(z.slots):
        chosen = jnp.where(fold_lane == wave_row * z.slots + s, fold_ref[...].astype(f32), 0.0)
        small = jnp.where(lane_slot == s, jnp.sum(chosen, axis=1, keepdims=True), small)
    lane_row = lane_row.astype(f32)
    first = lane_row < waves - small
    keep = (lane < z.head) & (lane_row < coarse - small)
    out["keep"].put(keep[:, :LANES].astype(f32))
    for s in range(z.slots):
        own = lane_slot == s
        at = 2 * s * z.n_wave
        out["member"].put((own & first).astype(f32), at)
        out["member"].put((own & jnp.logical_not(first)).astype(f32), at + z.n_wave)
        out["slot"].put((own & keep)[:, :LANES].astype(f32), s * z.n_wave)
    mode_row = lax.broadcasted_iota(jnp.int32, (z.per_node, z.levels), 0)
    rate_lane = lax.broadcasted_iota(jnp.int32, (z.per_node, z.levels), 1)
    chosen = jnp.where((mode_row >= 2 * rate_lane) & (mode_row < 2 * rate_lane + 2), rate_ref[...], 0.0)
    rates = jnp.sum(chosen, axis=1, keepdims=True)
    degree = (small + lane_row)[:, :LANES]
    degree = degree * (degree + 1.0) / (coarse * (coarse + 1.0))
    for w in range(z.n_wave):
        stiff = rates * degree[w : w + 1]
        both = jnp.concatenate([stiff, 1.0 / (1.0 + STEP_HALF * stiff)], 1)
        out["stiff"].put(both, w * z.per_node)

    for copy in copies[2:4]:
        copy.wait()

    def wave_column(count, per_slot):
        row = lax.broadcasted_iota(jnp.int32, (count, z.coarse_columns), 0)
        lane = lax.broadcasted_iota(jnp.int32, (count, z.coarse_columns), 1)
        inside = (row >= lane * per_slot) & (row < (lane + 1) * per_slot)
        small = jnp.sum(jnp.where(inside, fold_ref[...].astype(f32), 0.0), axis=1, keepdims=True)
        if per_slot == 1:
            return small
        first = lax.broadcasted_iota(jnp.int32, (count, 1), 0) & 1
        return jnp.where(first == 0, small, waves - 1 - small)

    def one_hot(count, per_slot, width):
        column = wave_column(count, per_slot)
        lane = lax.broadcasted_iota(jnp.int32, (count, 2 * width), 1).astype(f32)
        extra = width - coarse
        top = lane == jnp.where(column < coarse, column, column + coarse)
        bottom = lane == jnp.where(column < coarse, column + coarse, column + coarse + extra)
        return jnp.concatenate([top.astype(f32), bottom.astype(f32)], 0).astype(bf)

    hot = one_hot(half, 2, waves)
    coarse_hot = one_hot(z.coarse_columns, 1, coarse)
    short, long = 2 * coarse, 2 * (waves - coarse)
    levels = [(2 * x + core) * z.lev_dev + al for x in range(z.n_pair) for al in range(z.lev_dev)]
    period = basis_ref.shape[1]
    row = lax.broadcasted_iota(jnp.int32, (2 * waves, 1), 0)
    count = jnp.where(row < short, coarse, waves - coarse)
    wave = jnp.where(row < short, row, row - short)
    wave = jnp.where(wave < count, wave, wave - count) + jnp.where(row < short, 0, coarse)
    sign = (1 - 2 * (wave & 1)).astype(f32)
    chunk = LANES
    lines = [coef_ref[pl.ds(level, 1), :] for level in levels]
    for begin in range(0, period, chunk):
        span = slice(begin, begin + chunk)
        values = basis_ref[:, span].astype(f32)
        signed = values * sign
        for a, line in enumerate(lines):
            near = line[:, span] * values
            far = line[:, period + begin : period + begin + chunk] * signed
            for side, scaled in enumerate((near + far, near - far)):
                scaled_s[side, a * short : (a + 1) * short, span] = scaled[:short].astype(bf)
                at = z.own_levels * short + a * long
                scaled_s[side, at : at + long, span] = scaled[short:].astype(bf)
    for copy in copies[4:]:
        copy.wait()
    out["wave"].put(matmul_nt(sampled_ref[...], hot).astype(bf))
    out["coarse_wave"].put(matmul_nt(coarse_sampled_ref[...], coarse_hot).astype(bf))
    even = matmul(scaled_s[0], spread_ref[0])
    odd = matmul(scaled_s[1], spread_ref[1])
    total, delta = even + odd, even - odd
    middle, top = z.points // 2, z.own_levels * short
    quad = jnp.concatenate([total[:, :middle], delta[:, :middle]], 1).astype(bf)
    coarse_quad = jnp.concatenate([total[:top, middle:], delta[:top, middle:]], 1).astype(bf)
    for a in range(z.own_levels):
        at = z.own_levels * short + a * long
        pair = jnp.concatenate([quad[a * short : (a + 1) * short], quad[at : at + long]], 0)
        values = matmul(hot, pair).astype(bf)
        out["quad"].put(values, a * values.shape[0])
        values = matmul(coarse_hot, coarse_quad[a * short : (a + 1) * short]).astype(bf)
        out["coarse_quad"].put(values, a * values.shape[0])

    def pick(name, index=0):
        at, height, count, columns = layout[name]
        return picks_ref[pl.ds(pl.multiple_of(at + index * height, 2 * SUBLANES), count), :columns]

    def mix(left, matrix, right, mask):
        return mix_matrix(left, matrix[...], right, mask)

    out["mix_to"].put(mix(pick("to_left"), to_ref, pick("to_right", core), pick("to_mask")))
    out["mix_from"].put(mix(pick("from_left", core), from_ref, pick("from_right"), pick("from_mask")))
    out["mix_back"].put(mix(pick("back_left"), to_ref, pick("back_right", core), pick("from_mask")))
    out["lift"].put(mix(pick("lift_left", lev), from_ref, pick("lift_right"), pick("lift_mask")))


def sweep_kernel(
    z,
    own_ref,
    other_ref,
    state_ref,
    narrow_hbm,
    full_hbm,
    quads_hbm,
    other_quads_hbm,
    corrected_ref,
    tend_ref,
    leg_s,
    state_s,
    fourier_s,
    back_s,
    tend_s,
    coarse_s,
    coarse_back_s,
    modes_s,
    narrow_ref,
    full_ref,
    quads_ref,
    other_quads_ref,
    sems,
    legendre_s,
    product_s,
    coarse_product_s,
):
    bf, f32 = jnp.bfloat16, jnp.float32
    slots, rows, lats, per_node = z.slots, z.rows, z.lats, z.per_node
    table = named(z, narrow_ref, full_ref)
    quads = [named(z, *[ref] * 3) for ref in (quads_ref, other_quads_ref)]
    masks = pl.ds(0, z.fine_columns)
    others = pl.ds(z.fine_columns, full_ref.shape[0] - z.fine_columns)
    copies = copies_in(
        (full_hbm.at[masks], narrow_hbm, full_hbm.at[others], quads_hbm, other_quads_hbm),
        (full_ref.at[masks], narrow_ref, full_ref.at[others], quads_ref, other_quads_ref),
        sems,
    )

    def quad(name, a, count):
        lev, inner = a // z.lev_dev, a % z.lev_dev
        return quads[lev % 2][name].get((lev // 2 * z.lev_dev + inner) * count, count)

    wide = 2 * LANES
    all_lats = z.n_lev * lats

    def member(w, j):
        return table["member"].get(j * z.n_wave + w, 1)

    def slot(w, s):
        return table["slot"].get(s * z.n_wave + w, 1)

    def keep(w):
        return table["keep"].get(w, 1)

    for w in range(z.n_wave):
        for x in range(z.n_pair):
            for o, ref in enumerate((own_ref, other_ref)):
                d = 2 * x + o
                block = ref[z.position[w * z.n_pair + x]].astype(f32)
                extra = block[lats : lats + SUBLANES]
                leg_s[w, d * lats : (d + 1) * lats, :LANES] = block[:lats]
                state_at = d * z.dev_rows
                begin = lats + SUBLANES
                state_s[w, state_at : state_at + z.dev_rows, :LANES] = block[begin : begin + z.dev_rows]
                for q in range(z.groups):
                    moved = extra if q == 0 else pltpu.roll(extra, LANES - q * z.unit, 1)
                    at = q * SUBLANES
                    if at < lats:
                        leg_s[w, d * lats + at : d * lats + at + SUBLANES, LANES:] = moved
                    else:
                        at = at - lats
                        count = min(SUBLANES, z.dev_rows - at)
                        state_s[w, state_at + at : state_at + at + count, LANES:] = moved[:count]
        if all_lats < leg_s.shape[1]:
            leg_s[w, all_lats:, :] = jnp.zeros((leg_s.shape[1] - all_lats, wide), f32)
        legendre_s[w] = leg_s[w].astype(bf)

    lane = lax.broadcasted_iota(jnp.int32, (2 * SUBLANES, wide), 1)
    picked = ((lane == z.used) | (lane == z.used + 1)).astype(bf)
    gauss = matmul_nt(picked, legendre_s[0])[:1]

    inner = 2 * sum(z.head + (s + 1) * z.rest <= LANES for s in range(slots))
    spans = [(0, inner, LANES), (inner, 2 * slots, wide)]
    copies[0].wait()
    for w in range(z.n_wave):
        state = state_s[w]
        for first, last, width in spans:
            left = [state[:, :width] * member(w, j)[:, :width] for j in range(first, last)]
            left = jnp.concatenate(left, 0).astype(bf)
            out = matmul_nt(left, legendre_s[w, :, :width])
            for j in range(first, last):
                at = (w * 2 * slots + j) * z.row_pitch
                fourier_s[at : at + rows, :] = out[(j - first) * rows : (j - first + 1) * rows]

    for copy in copies[1:]:
        copy.wait()
    both = 2 * z.fine_columns
    half = z.fine_columns
    for a in range(z.levels):
        pieces = []
        for b in range(z.nodes):
            at = (a * z.nodes + b) * 2
            piece = [fourier_s[pl.ds(at + c, half, stride=z.row_pitch), :] for c in range(2)]
            pieces.append(jnp.concatenate(piece, 0).astype(bf))
        grid = matmul(table["wave"].get(), jnp.concatenate(pieces, 1))
        product_s[a] = (grid * grid).astype(bf)
    for a in range(z.levels):
        back = matmul(quad("quad", a, both), product_s[a])
        for b in range(z.nodes):
            values = back[:, b * LANES : (b + 1) * LANES] * gauss
            for c in range(2):
                at = ((a * z.nodes + b) * 2 + c) * z.column_pitch
                back_s[at : at + half, :] = values[c * half : (c + 1) * half]

    stacked = []
    for w in range(z.n_wave):
        outs = []
        for first, last, width in spans:
            left = [
                back_s[pl.ds(w * 2 * slots + j, rows, stride=z.column_pitch), :].astype(bf)
                for j in range(first, last)
            ]
            out = matmul(jnp.concatenate(left, 0), legendre_s[w, :, :width])
            outs += [out[i * rows : (i + 1) * rows] for i in range(last - first)]
        total, beyond = outs[-1][:, :LANES], outs[-1][:, LANES:]
        for j in range(2 * slots - 1):
            chosen = member(w, j) > 0.5
            total = jnp.where(chosen[:, :LANES], outs[j][:, :LANES], total)
            if j >= inner:
                beyond = jnp.where(chosen[:, LANES:], outs[j][:, LANES:], beyond)
        tend_s[w, :rows, :LANES] = total
        tend_s[w, :rows, LANES:] = beyond
        stacked.append(state_s[w][:, :LANES] * keep(w))
        stacked.append(total * keep(w))

    modes = matmul_split(table["mix_to"].get(), jnp.concatenate(stacked, 1))
    for w in range(z.n_wave):
        modes_s[w] = modes[:, 2 * w * LANES : 2 * (w + 1) * LANES]

    def advance(part, both_stiff):
        stiff, inverse = both_stiff[:, :LANES], both_stiff[:, LANES:]
        old, source = [], []
        for b in range(z.nodes):
            values = part[b * per_node : (b + 1) * per_node]
            old.append(values[:, :LANES])
            source.append(values[:, LANES:] - stiff * old[-1])
        mid = sum(quad_weights[0][b] * source[b] for b in range(z.nodes))
        mid = (mid + old[0] + STEP_HALF * stiff * old[1]) * inverse
        end = sum(quad_weights[1][b] * source[b] for b in range(z.nodes))
        return old, mid, end + mid + STEP_HALF * stiff * old[2], inverse

    evals = []
    for w in range(z.n_wave):
        part = modes[:, 2 * w * LANES : 2 * (w + 1) * LANES]
        old, mid, _, _ = advance(part, table["stiff"].get(w * per_node, per_node))
        evals += [old[1], mid]

    level_values = matmul_split(table["mix_from"].get(), jnp.concatenate(evals, 1))
    for w in range(z.n_wave):
        left = jnp.concatenate(
            [
                level_values[:, (2 * w + e) * LANES : (2 * w + e + 1) * LANES] * slot(w, s)
                for s in range(slots)
                for e in range(2)
            ],
            0,
        ).astype(bf)
        out = matmul_nt(left, legendre_s[w, :, :LANES])
        for s in range(slots):
            at = (w * slots + s) * z.mode_pitch
            coarse_s[at : at + 2 * per_node, :] = out[s * 2 * per_node : (s + 1) * 2 * per_node]

    both_c = 2 * z.coarse_columns
    for a in range(z.levels):
        pieces = []
        for e in range(2):
            at = e * per_node + a * 2
            piece = [
                coarse_s[pl.ds(at + c, z.coarse_columns, stride=z.mode_pitch), :] for c in range(2)
            ]
            pieces.append(jnp.concatenate(piece, 0).astype(bf))
        grid = matmul(table["coarse_wave"].get(), jnp.concatenate(pieces, 1))
        before, fresh = grid[:, :LANES], grid[:, LANES:]
        coarse_product_s[a] = (fresh * fresh - before * before).astype(bf)
    for a in range(z.levels):
        back = matmul(quad("coarse_quad", a, both_c), coarse_product_s[a])
        values = back * gauss
        for c in range(2):
            coarse_back_s[pl.ds(a * 2 + c, z.coarse_columns, stride=z.slot_pitch), :] = values[
                c * z.coarse_columns : (c + 1) * z.coarse_columns
            ]

    place = lax.axis_index("wave")
    begin = place * (slots * z.slot_pitch)
    left = jnp.concatenate(
        [
            coarse_back_s[pl.ds(pl.multiple_of(begin + s * z.slot_pitch, SUBLANES), per_node), :].astype(bf)
            for s in range(slots)
        ],
        0,
    )
    out = matmul(left, legendre_s[place][:, :LANES])
    wave_row = lax.broadcasted_iota(jnp.int32, (z.n_wave, LANES), 0)
    total = None
    for s in range(slots):
        block = table["slot"].get(s * z.n_wave, z.n_wave)
        mask = jnp.sum(jnp.where(wave_row == place, block, 0.0), axis=0, keepdims=True)
        term = mask * out[s * per_node : (s + 1) * per_node]
        total = term if total is None else total + term
    coarse_modes = matmul_split(table["mix_back"].get(), total)
    old, mid, end, inverse = advance(modes_s[place], table["stiff"].rows(place, per_node))
    end = (end + STEP_HALF * coarse_modes) * inverse
    change = jnp.concatenate([mid - old[1], end - old[2]], 0)
    begin = pl.multiple_of(lax.div(lax.axis_index("lev"), 2) * (2 * z.dev_rows), SUBLANES)
    mine = tend_s[place, pl.ds(begin, z.state_rows), :]
    raised = matmul_split(table["lift"].get(), change)
    lane = lax.broadcasted_iota(jnp.int32, (z.state_rows, wide), 1)
    for s in range(slots):
        low = mine if s == 0 else pltpu.roll(mine, wide - s * z.coarse, 1)
        high = pltpu.roll(mine, wide - (z.head + s * z.rest - z.coarse), 1)
        values = jnp.where(lane < z.coarse, low, high)
        for n in range(0, z.dev_rows, 2):
            tend_ref[n // (z.nodes * 2), n // 2 % z.nodes, s] = values[n : n + 2, : z.fine_rows]
        low = raised if s == 0 else pltpu.roll(raised, LANES - s * z.coarse, 1)
        low = jnp.where(lane[: low.shape[0], :LANES] < z.coarse, low, 0.0)
        for n in range(0, low.shape[0], 2):
            a, b = n // (2 * (z.nodes - 1)), n // 2 % (z.nodes - 1)
            corrected_ref[a, b, s] = state_ref[a, b + 1, s] + low[n : n + 2, : z.fine_rows]


def mix_constants(z):
    level, node, part = np.arange(z.levels), np.arange(z.nodes), np.arange(2)

    def pick(index):
        return (np.asarray(index)[:, None] == level[None, :]).astype(np.float32)

    def grid(*axes):
        return [m.reshape(-1) for m in np.meshgrid(*axes, indexing="ij")]

    def ordered(index, core):
        lev, inner = index // z.lev_dev, index % z.lev_dev
        return (lev ^ core) * z.lev_dev + inner

    def thrice(matrix):
        return np.concatenate([matrix] * 3, -1)

    def halves(matrix):
        zero = np.zeros_like(matrix)
        return np.concatenate(
            [np.concatenate([matrix, matrix, zero], 1), np.concatenate([zero, zero, matrix], 1)]
        )

    rb, rq, rc = grid(node, level, part)
    ca, cb, cc = grid(level, node, part)
    sa, sc = grid(level, part)
    to_mask = (rb[:, None] == cb[None]) & (rc[:, None] == cc[None])
    same_part = sc[:, None] == sc[None]
    la, lb, lc = grid(np.arange(z.lev_dev), np.arange(z.nodes - 1), part)
    kb, kq, kc = grid(np.arange(z.nodes - 1), level, part)
    lift_mask = (lb[:, None] == kb[None]) & (lc[:, None] == kc[None])
    by_core = range(2)
    constants = dict(
        to_left=[pick(rq)],
        to_right=[halves(pick(ordered(ca, k)).T) for k in by_core],
        to_mask=[thrice(to_mask)],
        from_left=[pick(ordered(sa, k)) for k in by_core],
        from_right=[halves(pick(sa).T)],
        from_mask=[thrice(same_part)],
        back_left=[pick(sa)],
        back_right=[halves(pick(ordered(sa, k)).T) for k in by_core],
        lift_left=[pick(k * z.lev_dev + la) for k in range(z.n_lev)],
        lift_right=[halves(pick(kq).T)],
        lift_mask=[thrice(lift_mask)],
    )
    wide = max(m[0].shape[1] for m in constants.values())
    layout, rows, at = {}, [], 0
    for name, members in constants.items():
        count, columns = members[0].shape
        height = round_up(count, 2 * SUBLANES)
        layout[name] = (at, height, count, columns)
        at += height * len(members)
        rows += [np.pad(m, ((0, height - count), (0, wide - columns))) for m in members]
    return layout, jnp.asarray(np.concatenate(rows), jnp.bfloat16)


def replicated_plan(
    fine_state, fold_pairs, legendre, gauss_weights, grid_coef, modes_from, modes_to, mode_rates
):
    z = Sizes(fine_state, legendre)
    bf, f32 = jnp.bfloat16, jnp.float32
    longitudes = grid_coef.shape[1]
    vmem = pl.BlockSpec(memory_space=pltpu.VMEM)
    hbm = pl.BlockSpec(memory_space=pltpu.HBM)
    shape = jax.ShapeDtypeStruct
    stored = jnp.swapaxes(fine_state, 2, 3)
    block = pl.pallas_call(
        functools.partial(pack_kernel, z),
        out_shape=shape((z.chips, z.block_rows, LANES), bf),
        in_specs=[hbm] * 3,
        out_specs=vmem,
        scratch_shapes=[
            pltpu.VMEM(stored.shape, f32),
            pltpu.VMEM(legendre.shape, bf),
            pltpu.VMEM((1, z.lats), f32),
            pltpu.SemaphoreType.DMA((3,)),
            pltpu.VMEM((z.slots, z.state_rows, z.fine_rows), f32),
        ],
        name="pack",
    )(stored, legendre, gauss_weights[None])
    groups = [[2 * i + c for i in z.order] for c in range(2)]
    own = lax.all_to_all(
        block, ("wave", "lev"), 0, 0, tiled=True, axis_index_groups=groups
    )
    fine_amp, coarse_amp = z.fine_width**-0.5, z.coarse**-0.5
    order = np.arange(2 * z.fine_width).reshape(2, -1)
    order = np.concatenate([order[:, : z.coarse].reshape(-1), order[:, z.coarse :].reshape(-1)])
    basis = wave_rows(z.fine_width, longitudes, fine_amp)[order]
    spread = interpolation(z.points, longitudes, 2 * (z.fine_width - 1))
    spread *= 2.0 * z.fine_width / longitudes
    coarse_spread = interpolation(z.coarse_points, longitudes, 2 * (z.coarse - 1))
    coarse_spread *= 2.0 * z.coarse / (longitudes // 2) * (coarse_amp / fine_amp)
    coarse_spread[1::2] = 0.0
    spread = np.stack(
        [
            np.concatenate([folded(spread, side), folded(coarse_spread, side)], 1)
            for side in (0.5, -0.5)
        ]
    )
    sampled = wave_rows(z.fine_width, z.points, fine_amp)[order].T
    coarse_sampled = wave_rows(z.coarse, z.coarse_points, coarse_amp).T
    basis = basis[:, : longitudes // 2]
    constants = [jnp.asarray(c, bf) for c in (basis, spread, sampled, coarse_sampled)]
    layout, picks = mix_constants(z)
    staged = [fold_pairs[None], mode_rates[None], grid_coef, *constants, modes_from, modes_to, picks]
    wide = 2 * LANES
    narrow_shape, full_shape, quads_shape = [entry[1] for entry in parts(z)]
    narrow, full, quads = pl.pallas_call(
        functools.partial(tables_kernel, z, layout),
        out_shape=(shape(narrow_shape, bf), shape(full_shape, f32), shape(quads_shape, bf)),
        in_specs=[hbm] * len(staged),
        out_specs=(vmem,) * 3,
        scratch_shapes=[
            pltpu.VMEM((2, z.own_levels * 2 * z.fine_width, longitudes // 2), bf),
            pltpu.SemaphoreType.DMA((len(staged),)),
        ]
        + [pltpu.VMEM(array.shape, array.dtype) for array in staged],
        cost_estimate=pl.CostEstimate(flops=10**9, bytes_accessed=4 * 10**6, transcendentals=0),
        name="tables",
    )(*staged)

    partners = [(i, i ^ 1) for i in range(2 * z.chips)]
    other_quads = lax.ppermute(quads, ("wave", "lev"), partners)
    own, narrow = lax.optimization_barrier((own, narrow))
    other = lax.ppermute(own, ("wave", "lev"), partners)

    lat_rows = round_up(z.n_lev * z.lats, LANES)
    corrected, fine_tend = pl.pallas_call(
        functools.partial(sweep_kernel, z),
        out_shape=(
            shape((z.lev_dev, z.nodes - 1, z.slots, 2, z.fine_rows), f32),
            shape(stored.shape, f32),
        ),
        in_specs=[vmem] * 3 + [hbm] * 4,
        out_specs=(vmem, vmem),
        scratch_shapes=[
            pltpu.VMEM((z.n_wave, lat_rows, wide), f32),
            pltpu.VMEM((z.n_wave, z.rows, wide), f32),
            pltpu.VMEM((z.row_pitch * z.fine_columns, lat_rows), f32),
            pltpu.VMEM((z.rows * z.column_pitch, lat_rows), f32),
            pltpu.VMEM((z.n_wave, z.rows + SUBLANES, wide), f32),
            pltpu.VMEM((z.mode_pitch * z.coarse_columns, lat_rows), f32),
            pltpu.VMEM((z.coarse_columns * z.slot_pitch, lat_rows), f32),
            pltpu.VMEM((z.n_wave, z.rows, 2 * LANES), f32),
            pltpu.VMEM(narrow_shape, bf),
            pltpu.VMEM(full_shape, f32),
            pltpu.VMEM(quads_shape, bf),
            pltpu.VMEM(quads_shape, bf),
            pltpu.SemaphoreType.DMA((5,)),
            pltpu.VMEM((z.n_wave, lat_rows, wide), bf),
            pltpu.VMEM((z.levels, z.points, z.nodes * LANES), bf),
            pltpu.VMEM((z.levels, z.coarse_points, LANES), bf),
        ],
        compiler_params=pltpu.CompilerParams(vmem_limit_bytes=VMEM_BYTES),
        name="sweep",
    )(own, other, stored, narrow, full, quads, other_quads)
    return (jnp.swapaxes(corrected, 2, 3), jnp.swapaxes(fine_tend, 2, 3))


def fits_replicated(fine_state, legendre):
    n_wave, n_lev = lax.axis_size("wave"), lax.axis_size("lev")
    if n_lev % 2 or fine_state.shape[1] != len(quad_weights[0]):
        return False
    z = Sizes(fine_state, legendre)
    gathered = 32 * n_wave * n_lev * (legendre.size + fine_state.size)
    return (
        z.head <= LANES
        and z.used > LANES
        and z.used + 2 - LANES <= z.unit
        and z.lats % SUBLANES == 0
        and z.head + z.rest <= LANES
        and n_lev * z.lats <= LANES
        and gathered <= REPLICATED_BYTES
    )


def per_device(fine_state, fold_pairs, legendre, *rest):
    plan = replicated_plan if fits_replicated(fine_state, legendre) else split_plan
    return plan(fine_state, fold_pairs, legendre, *rest)


def solution(mesh):
    placed = (
        P("lev", None, None, "wave", None),
        P(),
        P("wave", "lev", None),
        P("lev"),
        P(),
        P(),
        P(),
        P(),
    )
    return jax.shard_map(
        per_device,
        mesh=mesh,
        in_specs=placed,
        out_specs=(P("lev", None, None, "wave", None), P("lev", None, None, "wave", None)),
        check_vma=False,
    )
```

```python
import functools
import math

import jax
import jax.numpy as jnp
import numpy as np
from jax import lax
from jax.experimental import pallas as pl
from jax.experimental.pallas import tpu as pltpu
from jax.sharding import PartitionSpec as P

STEP_HALF = 0.5
quad_weights = ((5.0 / 24.0, 1.0 / 3.0, -1.0 / 24.0), (-1.0 / 24.0, 1.0 / 3.0, 5.0 / 24.0))
HIGHEST = lax.Precision.HIGHEST


def fourier_table(waves, points, amplitude):
    steps = jnp.arange(points, dtype=jnp.int32)
    turns = waves[:, :, None] * steps[None, None, :] % points
    angles = turns.astype(jnp.float32) * (2.0 * math.pi / points)
    return jnp.stack([jnp.cos(angles) * amplitude, -jnp.sin(angles) * amplitude]).astype(
        jnp.bfloat16
    )


def fine_rows(small_wave, fine_width):
    row_ids = jnp.arange(fine_width + 1, dtype=jnp.int32)[None, :]
    return row_ids < fine_width - small_wave[:, None]


def coarse_rows(small_wave, coarse):
    row_ids = jnp.arange(coarse, dtype=jnp.int32)[None, :]
    coarse_keep = row_ids < coarse - small_wave[:, None]
    degree = (small_wave[:, None] + row_ids).astype(jnp.float32)
    return (coarse_keep, degree)


def legendre_inverse(spectral, legendre_table, row_mask):
    split_spec = spectral[:, :, :, :, None, :] * row_mask[None, None, None]
    return jnp.einsum(
        "abcpmr,plr->abcpml", split_spec, legendre_table, preferred_element_type=jnp.float32
    ).astype(jnp.bfloat16)


def legendre_forward(returned, legendre_table, row_mask):
    members = jnp.einsum(
        "abcpml,plr->abcpmr", returned, legendre_table, preferred_element_type=jnp.float32
    )
    return jnp.sum(members * row_mask.astype(jnp.float32)[None, None, None], axis=4)


def grid_step(fourier, wave_table, coef, weights, factor):
    grid_field = jnp.einsum(
        "abcpmz,cpmk->abzk", fourier, wave_table, preferred_element_type=jnp.float32
    )
    product = (coef[:, None, None, :] * grid_field * grid_field).astype(jnp.bfloat16)
    returned = jnp.einsum(
        "abzk,cpmk->abcpmz", product, wave_table, preferred_element_type=jnp.float32
    )
    return (returned * (weights * factor)).astype(jnp.bfloat16)


def mix(matrix, values):
    return jnp.einsum("ql,lbcpr->qbcpr", matrix, values, precision=HIGHEST)


def split_plan(
    fine_state, fold_pairs, legendre, gauss_weights, grid_coef, modes_from, modes_to, mode_rates
):
    n_wave = lax.axis_size("wave")
    wave_idx = lax.axis_index("wave")
    lev_idx = lax.axis_index("lev")
    lev_dev = fine_state.shape[0]
    pairs_dev = fine_state.shape[3]
    fine_width = fine_state.shape[4] - 1
    coarse = fine_width // 2
    longitudes = grid_coef.shape[1]
    band_size = legendre.shape[1] // n_wave
    small_wave = lax.dynamic_slice_in_dim(fold_pairs, wave_idx * pairs_dev, pairs_dev)
    first_member = fine_rows(small_wave, fine_width)
    member_mask = jnp.stack([first_member, jnp.logical_not(first_member)], 1).astype(jnp.bfloat16)
    coarse_keep, degree = coarse_rows(small_wave, coarse)
    keep_mask = coarse_keep[:, None, :].astype(jnp.bfloat16)
    keep_float = coarse_keep.astype(jnp.float32)
    fine_table = fourier_table(
        jnp.stack([fold_pairs, fine_width - 1 - fold_pairs], 1), longitudes, fine_width ** (-0.5)
    )
    coarse_table = fourier_table(fold_pairs[:, None], longitudes // 2, coarse ** (-0.5))
    coarse_leg = legendre[:, :, :coarse]
    coarse_coef = grid_coef[:, ::2]
    band_gauss = lax.dynamic_slice_in_dim(gauss_weights, wave_idx * band_size, band_size)
    local_to = lax.dynamic_slice_in_dim(modes_to, lev_idx * lev_dev, lev_dev, 1)
    local_from = lax.dynamic_slice_in_dim(modes_from, lev_idx * lev_dev, lev_dev, 1)
    mode_decay = lax.dynamic_slice_in_dim(mode_rates, lev_idx * lev_dev, lev_dev)

    def project(partial_sum):
        return mix(modes_to, partial_sum)

    def coarse_start(modes):
        gathered = lax.all_gather(modes, "lev", axis=0, tiled=True)
        levels = (mix(modes_from, gathered) * keep_float).astype(jnp.bfloat16)
        return legendre_inverse(levels, coarse_leg, keep_mask)

    def coarse_grid_step(fourier):
        return grid_step(
            fourier, coarse_table, coarse_coef, band_gauss, 2.0 * coarse / (longitudes // 2)
        )

    def coarse_finish(returned):
        partial_sum = legendre_forward(returned, coarse_leg, keep_mask)
        return lax.psum_scatter(
            project(partial_sum).astype(jnp.bfloat16), "lev", scatter_dimension=0, tiled=True
        ).astype(jnp.float32)

    def coarse_eval(modes):
        fourier = lax.all_to_all(
            coarse_start(modes), "wave", split_axis=5, concat_axis=3, tiled=True
        )
        returned = lax.all_to_all(
            coarse_grid_step(fourier), "wave", split_axis=3, concat_axis=5, tiled=True
        )
        return coarse_finish(returned)

    restricted = fine_state[..., :coarse] * keep_float
    fine_spec = lax.all_gather(fine_state.astype(jnp.bfloat16), "lev", axis=0, tiled=True)
    fine_fourier = legendre_inverse(fine_spec, legendre, member_mask)
    fine_fourier = lax.all_to_all(fine_fourier, "wave", split_axis=5, concat_axis=3, tiled=True)
    fine_back = lax.all_to_all(
        grid_step(fine_fourier, fine_table, grid_coef, band_gauss, 2.0 * fine_width / longitudes),
        "wave",
        split_axis=3,
        concat_axis=5,
        tiled=True,
    )
    fine_tend = lax.psum_scatter(
        legendre_forward(fine_back, legendre, member_mask).astype(jnp.bfloat16),
        "lev",
        scatter_dimension=0,
        tiled=True,
    ).astype(jnp.float32)
    restricted_tend = fine_tend[..., :coarse] * keep_float
    stacked = jnp.concatenate([restricted, restricted_tend], 1)
    both_modes = lax.psum_scatter(
        mix(local_to, stacked).astype(jnp.bfloat16), "lev", scatter_dimension=0, tiled=True
    ).astype(jnp.float32)
    nodes = fine_state.shape[1]
    old_state = both_modes[:, :nodes]
    old_tend = both_modes[:, nodes:]
    old_coarse = coarse_eval(old_state[:, 1:2])
    stiffness = (
        mode_decay[:, None, None, None]
        * (degree * (degree + 1.0) / (coarse * (coarse + 1.0)))[None, None]
    )
    source = old_tend - stiffness[:, None] * old_state
    integral_mid = (
        quad_weights[0][0] * source[:, 0]
        + quad_weights[0][1] * source[:, 1]
        + quad_weights[0][2] * source[:, 2]
    )
    integral_end = (
        quad_weights[1][0] * source[:, 0]
        + quad_weights[1][1] * source[:, 1]
        + quad_weights[1][2] * source[:, 2]
    )
    divisor = 1.0 + STEP_HALF * stiffness
    next_mid = (old_state[:, 0] + STEP_HALF * stiffness * old_state[:, 1] + integral_mid) / divisor
    coarse_fresh = coarse_eval(next_mid[:, None])
    next_end = (
        next_mid
        + STEP_HALF * (coarse_fresh[:, 0] - old_coarse[:, 0])
        + STEP_HALF * stiffness * old_state[:, 2]
        + integral_end
    ) / divisor
    change = jnp.stack([next_mid - old_state[:, 1], next_end - old_state[:, 2]], 1)
    lifted = lax.psum_scatter(
        mix(local_from, change).astype(jnp.bfloat16), "lev", scatter_dimension=0, tiled=True
    ).astype(jnp.float32)
    corrected = fine_state[:, 1:] + jnp.pad(
        lifted, ((0, 0), (0, 0), (0, 0), (0, 0), (0, fine_width + 1 - coarse))
    )
    return (corrected, fine_tend)


LANES = 128
SUBLANES = 8
REPLICATED_BYTES = 16 * 2**20
VMEM_BYTES = 56 * 10**6


def round_up(value, unit):
    return -(-value // unit) * unit


def interpolation(points, targets, degree):
    offset = (
        2.0 * np.pi * (np.arange(targets)[:, None] / targets - np.arange(points)[None, :] / points)
    )
    order = np.arange(1, degree + 1)
    return (1.0 + 2.0 * np.cos(offset[:, :, None] * order).sum(-1)) / points


def wave_rows(waves, points, amplitude):
    turns = np.arange(waves)[:, None] * np.arange(points)[None, :] % points
    angles = turns * (2.0 * np.pi / points)
    return np.concatenate([np.cos(angles), -np.sin(angles)]) * amplitude


def folded(table, side):
    near = table[: table.shape[0] // 2]
    middle = table.shape[1] // 2
    return 0.5 * near[:, :middle] + side * near[:, middle:]


def matmul(a, b):
    return jnp.dot(a, b, preferred_element_type=jnp.float32)


def matmul_nt(a, b):
    return lax.dot_general(a, b, (((1,), (1,)), ((), ())), preferred_element_type=jnp.float32)


def matmul_exact(a, b):
    return jnp.dot(a, b, preferred_element_type=jnp.float32, precision=lax.Precision.HIGHEST)


def high_low(values):
    high = values.astype(jnp.bfloat16)
    return high, (values - high.astype(jnp.float32)).astype(jnp.bfloat16)


def matmul_split(left, right):
    high, low = high_low(right)
    return matmul(left, jnp.concatenate([high, low, high], 0))


def pitch(count):
    return count + 4 if count % 8 == 0 else count


class Sizes:
    def __init__(self, fine_state, legendre):
        self.n_wave, self.n_lev = lax.axis_size("wave"), lax.axis_size("lev")
        self.lev_dev, self.nodes, _, self.slots, self.fine_rows = fine_state.shape
        self.lats = legendre.shape[1]
        self.n_pair = self.n_lev // 2
        self.fine_width = self.fine_rows - 1
        self.coarse = self.fine_width // 2
        self.levels = self.n_lev * self.lev_dev
        self.own_levels = self.n_pair * self.lev_dev
        self.dev_rows = self.lev_dev * self.nodes * 2
        self.rows = self.levels * self.nodes * 2
        self.per_node = self.levels * 2
        self.head = self.slots * self.coarse
        self.rest = self.fine_rows - self.coarse
        self.used = self.slots * self.fine_rows
        self.state_rows = round_up(self.dev_rows, SUBLANES)
        self.groups = (self.lats + self.state_rows) // SUBLANES
        self.unit = LANES // self.groups
        self.block_rows = self.lats + SUBLANES + self.state_rows
        self.chips = self.n_wave * self.n_pair
        lead = self.chips // 2 - 1
        self.order = [lead] + [i for i in range(self.chips) if i != lead]
        self.position = [self.order.index(i) for i in range(self.chips)]
        self.fine_columns = self.n_wave * self.slots * 2
        self.coarse_columns = self.n_wave * self.slots
        self.row_pitch = pitch(self.rows)
        self.column_pitch = pitch(self.fine_columns)
        self.mode_pitch = pitch(2 * self.per_node)
        self.slot_pitch = round_up(self.per_node, SUBLANES) + SUBLANES
        self.points = round_up(4 * (self.fine_width - 1) + 1, 32)
        self.coarse_points = round_up(4 * (self.coarse - 1) + 1, 32)


def parts(z):
    narrow = dict(
        wave=(z.points, 2 * z.fine_columns),
        coarse_wave=(z.coarse_points, 2 * z.coarse_columns),
        mix_to=(z.rows, 3 * z.rows),
        mix_from=(z.per_node, 3 * z.per_node),
        mix_back=(z.per_node, 3 * z.per_node),
        lift=(z.lev_dev * (z.nodes - 1) * 2, 3 * (z.nodes - 1) * z.per_node),
    )
    full = dict(
        member=(z.fine_columns, 2 * LANES),
        slot=(z.coarse_columns, LANES),
        keep=(z.n_wave, LANES),
        stiff=(z.n_wave * z.per_node, 2 * LANES),
    )

    def placed(shapes, unit):
        out, at = {}, 0
        for name, (count, columns) in shapes.items():
            out[name] = (at, count, columns)
            at += round_up(count, unit)
        return out, (at, max(columns for _, columns in shapes.values()))

    quads = dict(
        quad=(z.own_levels * 2 * z.fine_columns, z.points),
        coarse_quad=(z.own_levels * 2 * z.coarse_columns, z.coarse_points),
    )
    return [placed(shapes, 2 * SUBLANES) for shapes in (narrow, full, quads)]


class Table:
    def __init__(self, ref, place):
        self.ref, (self.at, self.count, self.columns) = ref, place

    def get(self, begin=0, count=None):
        begin = self.at + begin
        return self.ref[begin : begin + (count or self.count), : self.columns]

    def rows(self, block, count):
        begin = pl.multiple_of(self.at + block * count, SUBLANES)
        return self.ref[pl.ds(begin, count), : self.columns]

    def put(self, values, begin=0):
        begin = self.at + begin
        self.ref[begin : begin + values.shape[0], : self.columns] = values


def named(z, *refs):
    tables = {}
    for ref, (places, _) in zip(refs, parts(z)):
        tables |= {name: Table(ref, place) for name, place in places.items()}
    return tables


def copies_in(sources, targets, sems):
    copies = [
        pltpu.make_async_copy(source, target, sems.at[i])
        for i, (source, target) in enumerate(zip(sources, targets))
    ]
    for copy in copies:
        copy.start()
    return copies


def pack_kernel(z, state_hbm, leg_hbm, gauss_hbm, out_ref, state_ref, leg_ref, gauss_ref, sems, rows_s):
    bf, f32 = jnp.bfloat16, jnp.float32
    copies = copies_in((state_hbm, leg_hbm, gauss_hbm), (state_ref, leg_ref, gauss_ref), sems)
    for copy in copies:
        copy.wait()
    row = lax.broadcasted_iota(jnp.int32, (z.fine_rows, LANES), 0)
    lane = lax.broadcasted_iota(jnp.int32, (z.fine_rows, LANES), 1)
    for a in range(z.lev_dev):
        for b in range(z.nodes):
            n = (a * z.nodes + b) * 2
            for s in range(z.slots):
                rows_s[s, n : n + 2, :] = state_ref[a, b, s]
    if z.state_rows > z.dev_rows:
        for s in range(z.slots):
            rows_s[s, z.dev_rows :, :] = jnp.zeros((z.state_rows - z.dev_rows, z.fine_rows), f32)
    table = jnp.zeros((z.lats, LANES), f32)
    state = jnp.zeros((z.state_rows, LANES), f32)
    extra = jnp.zeros((SUBLANES, LANES), f32)
    for s in range(z.slots):
        target = jnp.where(row < z.coarse, s * z.coarse + row, z.head + s * z.rest + row - z.coarse)
        leg = leg_ref[s].astype(f32)
        spec = rows_s[s]
        place = (target == lane).astype(bf)
        table = table + matmul(leg.astype(bf), place)
        state = state + matmul(spec.astype(bf), place)
        if z.head + (s + 1) * z.rest > LANES:
            for q in range(z.groups):
                at = q * SUBLANES
                part = leg[at : at + SUBLANES] if at < z.lats else spec[at - z.lats : at - z.lats + SUBLANES]
                place = ((target >= LANES) & (target - LANES + q * z.unit == lane)).astype(bf)
                extra = extra + matmul(part.astype(bf), place)
    wide_row = lax.broadcasted_iota(jnp.int32, (SUBLANES, z.lats), 0)
    wide_lane = lax.broadcasted_iota(jnp.int32, (SUBLANES, z.lats), 1)
    out_lane = lax.broadcasted_iota(jnp.int32, (SUBLANES, LANES), 1)
    for q in range(z.lats // SUBLANES):
        chosen = jnp.where(wide_lane == wide_row + q * SUBLANES, gauss_ref[...], 0.0)
        column = jnp.sum(chosen, axis=1, keepdims=True)
        high = column.astype(bf).astype(f32)
        at = q * z.unit + z.used - LANES
        extra = extra + jnp.where(out_lane == at, high, 0.0)
        extra = extra + jnp.where(out_lane == at + 1, column - high, 0.0)
    block = jnp.concatenate([table, extra, state], 0).astype(bf)
    for i in range(z.chips):
        out_ref[i] = block


def mix_matrix(pick_left, matrix, pick_right, mask):
    bf, f32 = jnp.bfloat16, jnp.float32
    high, low = high_low(matrix)
    left = pick_left.astype(bf)
    halves = jnp.concatenate([matmul(left, high).astype(bf), matmul(left, low).astype(bf)], 1)
    return (matmul(halves, pick_right.astype(bf)) * mask.astype(f32)).astype(bf)


def tables_kernel(z, layout, *refs):
    inputs, outputs, scratch = refs[:10], refs[10:13], refs[13:]
    (scaled_s, sems), staged = scratch[:2], scratch[2:]
    copies = copies_in(inputs, staged, sems)
    fold_ref, rate_ref, coef_ref, basis_ref, spread_ref = staged[:5]
    sampled_ref, coarse_sampled_ref, from_ref, to_ref, picks_ref = staged[5:]
    out = named(z, *outputs)
    bf, f32 = jnp.bfloat16, jnp.float32
    lev = lax.axis_index("lev")
    core = lax.rem(lev, 2)
    waves, coarse = z.fine_width, z.coarse
    half = z.fine_columns

    wide = 2 * LANES
    lane = lax.broadcasted_iota(jnp.int32, (1, wide), 1)
    lane_slot = jnp.full((1, wide), -1, jnp.int32)
    lane_row = jnp.zeros((1, wide), jnp.int32)
    for s in range(z.slots):
        for begin, width, first in ((s * coarse, coarse, 0), (z.head + s * z.rest, z.rest, coarse)):
            inside = (lane >= begin) & (lane < begin + width)
            lane_slot = jnp.where(inside, s, lane_slot)
            lane_row = jnp.where(inside, lane - begin + first, lane_row)
    copies[0].wait()
    copies[1].wait()
    wave_row = lax.broadcasted_iota(jnp.int32, (z.n_wave, z.coarse_columns), 0)
    fold_lane = lax.broadcasted_iota(jnp.int32, (z.n_wave, z.coarse_columns), 1)
    small = jnp.zeros((z.n_wave, wide), f32)
    for s in range(z.slots):
        chosen = jnp.where(fold_lane == wave_row * z.slots + s, fold_ref[...].astype(f32), 0.0)
        small = jnp.where(lane_slot == s, jnp.sum(chosen, axis=1, keepdims=True), small)
    lane_row = lane_row.astype(f32)
    first = lane_row < waves - small
    keep = (lane < z.head) & (lane_row < coarse - small)
    out["keep"].put(keep[:, :LANES].astype(f32))
    for s in range(z.slots):
        own = lane_slot == s
        at = 2 * s * z.n_wave
        out["member"].put((own & first).astype(f32), at)
        out["member"].put((own & jnp.logical_not(first)).astype(f32), at + z.n_wave)
        out["slot"].put((own & keep)[:, :LANES].astype(f32), s * z.n_wave)
    mode_row = lax.broadcasted_iota(jnp.int32, (z.per_node, z.levels), 0)
    rate_lane = lax.broadcasted_iota(jnp.int32, (z.per_node, z.levels), 1)
    chosen = jnp.where((mode_row >= 2 * rate_lane) & (mode_row < 2 * rate_lane + 2), rate_ref[...], 0.0)
    rates = jnp.sum(chosen, axis=1, keepdims=True)
    degree = (small + lane_row)[:, :LANES]
    degree = degree * (degree + 1.0) / (coarse * (coarse + 1.0))
    for w in range(z.n_wave):
        stiff = rates * degree[w : w + 1]
        both = jnp.concatenate([stiff, 1.0 / (1.0 + STEP_HALF * stiff)], 1)
        out["stiff"].put(both, w * z.per_node)

    for copy in copies[2:4]:
        copy.wait()

    def wave_column(count, per_slot):
        row = lax.broadcasted_iota(jnp.int32, (count, z.coarse_columns), 0)
        lane = lax.broadcasted_iota(jnp.int32, (count, z.coarse_columns), 1)
        inside = (row >= lane * per_slot) & (row < (lane + 1) * per_slot)
        small = jnp.sum(jnp.where(inside, fold_ref[...].astype(f32), 0.0), axis=1, keepdims=True)
        if per_slot == 1:
            return small
        first = lax.broadcasted_iota(jnp.int32, (count, 1), 0) & 1
        return jnp.where(first == 0, small, waves - 1 - small)

    def one_hot(count, per_slot, width):
        column = wave_column(count, per_slot)
        lane = lax.broadcasted_iota(jnp.int32, (count, 2 * width), 1).astype(f32)
        extra = width - coarse
        top = lane == jnp.where(column < coarse, column, column + coarse)
        bottom = lane == jnp.where(column < coarse, column + coarse, column + coarse + extra)
        return jnp.concatenate([top.astype(f32), bottom.astype(f32)], 0).astype(bf)

    hot = one_hot(half, 2, waves)
    coarse_hot = one_hot(z.coarse_columns, 1, coarse)
    short, long = 2 * coarse, 2 * (waves - coarse)
    levels = [(2 * x + core) * z.lev_dev + al for x in range(z.n_pair) for al in range(z.lev_dev)]
    period = basis_ref.shape[1]
    row = lax.broadcasted_iota(jnp.int32, (2 * waves, 1), 0)
    count = jnp.where(row < short, coarse, waves - coarse)
    wave = jnp.where(row < short, row, row - short)
    wave = jnp.where(wave < count, wave, wave - count) + jnp.where(row < short, 0, coarse)
    sign = (1 - 2 * (wave & 1)).astype(f32)
    chunk = LANES
    lines = [coef_ref[pl.ds(level, 1), :] for level in levels]
    for begin in range(0, period, chunk):
        span = slice(begin, begin + chunk)
        values = basis_ref[:, span].astype(f32)
        signed = values * sign
        for a, line in enumerate(lines):
            near = line[:, span] * values
            far = line[:, period + begin : period + begin + chunk] * signed
            for side, scaled in enumerate((near + far, near - far)):
                scaled_s[side, a * short : (a + 1) * short, span] = scaled[:short].astype(bf)
                at = z.own_levels * short + a * long
                scaled_s[side, at : at + long, span] = scaled[short:].astype(bf)
    for copy in copies[4:]:
        copy.wait()
    out["wave"].put(matmul_nt(sampled_ref[...], hot).astype(bf))
    out["coarse_wave"].put(matmul_nt(coarse_sampled_ref[...], coarse_hot).astype(bf))
    even = matmul(scaled_s[0], spread_ref[0])
    odd = matmul(scaled_s[1], spread_ref[1])
    total, delta = even + odd, even - odd
    middle, top = z.points // 2, z.own_levels * short
    quad = jnp.concatenate([total[:, :middle], delta[:, :middle]], 1).astype(bf)
    coarse_quad = jnp.concatenate([total[:top, middle:], delta[:top, middle:]], 1).astype(bf)
    for a in range(z.own_levels):
        at = z.own_levels * short + a * long
        pair = jnp.concatenate([quad[a * short : (a + 1) * short], quad[at : at + long]], 0)
        values = matmul(hot, pair).astype(bf)
        out["quad"].put(values, a * values.shape[0])
        values = matmul(coarse_hot, coarse_quad[a * short : (a + 1) * short]).astype(bf)
        out["coarse_quad"].put(values, a * values.shape[0])

    def pick(name, index=0):
        at, height, count, columns = layout[name]
        return picks_ref[pl.ds(pl.multiple_of(at + index * height, 2 * SUBLANES), count), :columns]

    def mix(left, matrix, right, mask):
        return mix_matrix(left, matrix[...], right, mask)

    out["mix_to"].put(mix(pick("to_left"), to_ref, pick("to_right", core), pick("to_mask")))
    out["mix_from"].put(mix(pick("from_left", core), from_ref, pick("from_right"), pick("from_mask")))
    out["mix_back"].put(mix(pick("back_left"), to_ref, pick("back_right", core), pick("from_mask")))
    out["lift"].put(mix(pick("lift_left", lev), from_ref, pick("lift_right"), pick("lift_mask")))


def sweep_kernel(
    z,
    own_ref,
    other_ref,
    state_ref,
    narrow_hbm,
    full_hbm,
    quads_hbm,
    other_quads_hbm,
    corrected_ref,
    tend_ref,
    leg_s,
    state_s,
    fourier_s,
    back_s,
    tend_s,
    coarse_s,
    coarse_back_s,
    modes_s,
    narrow_ref,
    full_ref,
    quads_ref,
    other_quads_ref,
    sems,
    legendre_s,
    product_s,
    coarse_product_s,
):
    bf, f32 = jnp.bfloat16, jnp.float32
    slots, rows, lats, per_node = z.slots, z.rows, z.lats, z.per_node
    table = named(z, narrow_ref, full_ref)
    quads = [named(z, *[ref] * 3) for ref in (quads_ref, other_quads_ref)]
    masks = pl.ds(0, z.fine_columns)
    others = pl.ds(z.fine_columns, full_ref.shape[0] - z.fine_columns)
    copies = copies_in(
        (full_hbm.at[masks], narrow_hbm, full_hbm.at[others], quads_hbm, other_quads_hbm),
        (full_ref.at[masks], narrow_ref, full_ref.at[others], quads_ref, other_quads_ref),
        sems,
    )

    def quad(name, a, count):
        lev, inner = a // z.lev_dev, a % z.lev_dev
        return quads[lev % 2][name].get((lev // 2 * z.lev_dev + inner) * count, count)

    wide = 2 * LANES
    all_lats = z.n_lev * lats

    def member(w, j):
        return table["member"].get(j * z.n_wave + w, 1)

    def slot(w, s):
        return table["slot"].get(s * z.n_wave + w, 1)

    def keep(w):
        return table["keep"].get(w, 1)

    for w in range(z.n_wave):
        for x in range(z.n_pair):
            for o, ref in enumerate((own_ref, other_ref)):
                d = 2 * x + o
                block = ref[z.position[w * z.n_pair + x]].astype(f32)
                extra = block[lats : lats + SUBLANES]
                leg_s[w, d * lats : (d + 1) * lats, :LANES] = block[:lats]
                state_at = d * z.dev_rows
                begin = lats + SUBLANES
                state_s[w, state_at : state_at + z.dev_rows, :LANES] = block[begin : begin + z.dev_rows]
                for q in range(z.groups):
                    moved = extra if q == 0 else pltpu.roll(extra, LANES - q * z.unit, 1)
                    at = q * SUBLANES
                    if at < lats:
                        leg_s[w, d * lats + at : d * lats + at + SUBLANES, LANES:] = moved
                    else:
                        at = at - lats
                        count = min(SUBLANES, z.dev_rows - at)
                        state_s[w, state_at + at : state_at + at + count, LANES:] = moved[:count]
        if all_lats < leg_s.shape[1]:
            leg_s[w, all_lats:, :] = jnp.zeros((leg_s.shape[1] - all_lats, wide), f32)
        legendre_s[w] = leg_s[w].astype(bf)

    lane = lax.broadcasted_iota(jnp.int32, (2 * SUBLANES, wide), 1)
    picked = ((lane == z.used) | (lane == z.used + 1)).astype(bf)
    gauss = matmul_nt(picked, legendre_s[0])[:1]

    inner = 2 * sum(z.head + (s + 1) * z.rest <= LANES for s in range(slots))
    spans = [(0, inner, LANES), (inner, 2 * slots, wide)]
    copies[0].wait()
    for w in range(z.n_wave):
        state = state_s[w]
        for first, last, width in spans:
            left = [state[:, :width] * member(w, j)[:, :width] for j in range(first, last)]
            left = jnp.concatenate(left, 0).astype(bf)
            out = matmul_nt(left, legendre_s[w, :, :width])
            for j in range(first, last):
                at = (w * 2 * slots + j) * z.row_pitch
                fourier_s[at : at + rows, :] = out[(j - first) * rows : (j - first + 1) * rows]

    for copy in copies[1:]:
        copy.wait()
    both = 2 * z.fine_columns
    half = z.fine_columns
    for a in range(z.levels):
        pieces = []
        for b in range(z.nodes):
            at = (a * z.nodes + b) * 2
            piece = [fourier_s[pl.ds(at + c, half, stride=z.row_pitch), :] for c in range(2)]
            pieces.append(jnp.concatenate(piece, 0).astype(bf))
        grid = matmul(table["wave"].get(), jnp.concatenate(pieces, 1))
        product_s[a] = (grid * grid).astype(bf)
    for a in range(z.levels):
        back = matmul(quad("quad", a, both), product_s[a])
        for b in range(z.nodes):
            values = back[:, b * LANES : (b + 1) * LANES] * gauss
            for c in range(2):
                at = ((a * z.nodes + b) * 2 + c) * z.column_pitch
                back_s[at : at + half, :] = values[c * half : (c + 1) * half]

    stacked = []
    for w in range(z.n_wave):
        outs = []
        for first, last, width in spans:
            left = [
                back_s[pl.ds(w * 2 * slots + j, rows, stride=z.column_pitch), :].astype(bf)
                for j in range(first, last)
            ]
            out = matmul(jnp.concatenate(left, 0), legendre_s[w, :, :width])
            outs += [out[i * rows : (i + 1) * rows] for i in range(last - first)]
        total, beyond = outs[-1][:, :LANES], outs[-1][:, LANES:]
        for j in range(2 * slots - 1):
            chosen = member(w, j) > 0.5
            total = jnp.where(chosen[:, :LANES], outs[j][:, :LANES], total)
            if j >= inner:
                beyond = jnp.where(chosen[:, LANES:], outs[j][:, LANES:], beyond)
        tend_s[w, :rows, :LANES] = total
        tend_s[w, :rows, LANES:] = beyond
        stacked.append(state_s[w][:, :LANES] * keep(w))
        stacked.append(total * keep(w))

    modes = matmul_split(table["mix_to"].get(), jnp.concatenate(stacked, 1))
    for w in range(z.n_wave):
        modes_s[w] = modes[:, 2 * w * LANES : 2 * (w + 1) * LANES]

    def advance(part, both_stiff):
        stiff, inverse = both_stiff[:, :LANES], both_stiff[:, LANES:]
        old, source = [], []
        for b in range(z.nodes):
            values = part[b * per_node : (b + 1) * per_node]
            old.append(values[:, :LANES])
            source.append(values[:, LANES:] - stiff * old[-1])
        mid = sum(quad_weights[0][b] * source[b] for b in range(z.nodes))
        mid = (mid + old[0] + STEP_HALF * stiff * old[1]) * inverse
        end = sum(quad_weights[1][b] * source[b] for b in range(z.nodes))
        return old, mid, end + mid + STEP_HALF * stiff * old[2], inverse

    evals = []
    for w in range(z.n_wave):
        part = modes[:, 2 * w * LANES : 2 * (w + 1) * LANES]
        old, mid, _, _ = advance(part, table["stiff"].get(w * per_node, per_node))
        evals += [old[1], mid]

    level_values = matmul_split(table["mix_from"].get(), jnp.concatenate(evals, 1))
    for w in range(z.n_wave):
        left = jnp.concatenate(
            [
                level_values[:, (2 * w + e) * LANES : (2 * w + e + 1) * LANES] * slot(w, s)
                for s in range(slots)
                for e in range(2)
            ],
            0,
        ).astype(bf)
        out = matmul_nt(left, legendre_s[w, :, :LANES])
        for s in range(slots):
            at = (w * slots + s) * z.mode_pitch
            coarse_s[at : at + 2 * per_node, :] = out[s * 2 * per_node : (s + 1) * 2 * per_node]

    both_c = 2 * z.coarse_columns
    for a in range(z.levels):
        pieces = []
        for e in range(2):
            at = e * per_node + a * 2
            piece = [
                coarse_s[pl.ds(at + c, z.coarse_columns, stride=z.mode_pitch), :] for c in range(2)
            ]
            pieces.append(jnp.concatenate(piece, 0).astype(bf))
        grid = matmul(table["coarse_wave"].get(), jnp.concatenate(pieces, 1))
        before, fresh = grid[:, :LANES], grid[:, LANES:]
        coarse_product_s[a] = (fresh * fresh - before * before).astype(bf)
    for a in range(z.levels):
        back = matmul(quad("coarse_quad", a, both_c), coarse_product_s[a])
        values = back * gauss
        for c in range(2):
            coarse_back_s[pl.ds(a * 2 + c, z.coarse_columns, stride=z.slot_pitch), :] = values[
                c * z.coarse_columns : (c + 1) * z.coarse_columns
            ]

    place = lax.axis_index("wave")
    begin = place * (slots * z.slot_pitch)
    left = jnp.concatenate(
        [
            coarse_back_s[pl.ds(pl.multiple_of(begin + s * z.slot_pitch, SUBLANES), per_node), :].astype(bf)
            for s in range(slots)
        ],
        0,
    )
    out = matmul(left, legendre_s[place][:, :LANES])
    wave_row = lax.broadcasted_iota(jnp.int32, (z.n_wave, LANES), 0)
    total = None
    for s in range(slots):
        block = table["slot"].get(s * z.n_wave, z.n_wave)
        mask = jnp.sum(jnp.where(wave_row == place, block, 0.0), axis=0, keepdims=True)
        term = mask * out[s * per_node : (s + 1) * per_node]
        total = term if total is None else total + term
    coarse_modes = matmul_split(table["mix_back"].get(), total)
    old, mid, end, inverse = advance(modes_s[place], table["stiff"].rows(place, per_node))
    end = (end + STEP_HALF * coarse_modes) * inverse
    change = jnp.concatenate([mid - old[1], end - old[2]], 0)
    begin = pl.multiple_of(lax.div(lax.axis_index("lev"), 2) * (2 * z.dev_rows), SUBLANES)
    mine = tend_s[place, pl.ds(begin, z.state_rows), :]
    raised = matmul_split(table["lift"].get(), change)
    lane = lax.broadcasted_iota(jnp.int32, (z.state_rows, wide), 1)
    for s in range(slots):
        low = mine if s == 0 else pltpu.roll(mine, wide - s * z.coarse, 1)
        high = pltpu.roll(mine, wide - (z.head + s * z.rest - z.coarse), 1)
        values = jnp.where(lane < z.coarse, low, high)
        for n in range(0, z.dev_rows, 2):
            tend_ref[n // (z.nodes * 2), n // 2 % z.nodes, s] = values[n : n + 2, : z.fine_rows]
        low = raised if s == 0 else pltpu.roll(raised, LANES - s * z.coarse, 1)
        low = jnp.where(lane[: low.shape[0], :LANES] < z.coarse, low, 0.0)
        for n in range(0, low.shape[0], 2):
            a, b = n // (2 * (z.nodes - 1)), n // 2 % (z.nodes - 1)
            corrected_ref[a, b, s] = state_ref[a, b + 1, s] + low[n : n + 2, : z.fine_rows]


def mix_constants(z):
    level, node, part = np.arange(z.levels), np.arange(z.nodes), np.arange(2)

    def pick(index):
        return (np.asarray(index)[:, None] == level[None, :]).astype(np.float32)

    def grid(*axes):
        return [m.reshape(-1) for m in np.meshgrid(*axes, indexing="ij")]

    def ordered(index, core):
        lev, inner = index // z.lev_dev, index % z.lev_dev
        return (lev ^ core) * z.lev_dev + inner

    def thrice(matrix):
        return np.concatenate([matrix] * 3, -1)

    def halves(matrix):
        zero = np.zeros_like(matrix)
        return np.concatenate(
            [np.concatenate([matrix, matrix, zero], 1), np.concatenate([zero, zero, matrix], 1)]
        )

    rb, rq, rc = grid(node, level, part)
    ca, cb, cc = grid(level, node, part)
    sa, sc = grid(level, part)
    to_mask = (rb[:, None] == cb[None]) & (rc[:, None] == cc[None])
    same_part = sc[:, None] == sc[None]
    la, lb, lc = grid(np.arange(z.lev_dev), np.arange(z.nodes - 1), part)
    kb, kq, kc = grid(np.arange(z.nodes - 1), level, part)
    lift_mask = (lb[:, None] == kb[None]) & (lc[:, None] == kc[None])
    by_core = range(2)
    constants = dict(
        to_left=[pick(rq)],
        to_right=[halves(pick(ordered(ca, k)).T) for k in by_core],
        to_mask=[thrice(to_mask)],
        from_left=[pick(ordered(sa, k)) for k in by_core],
        from_right=[halves(pick(sa).T)],
        from_mask=[thrice(same_part)],
        back_left=[pick(sa)],
        back_right=[halves(pick(ordered(sa, k)).T) for k in by_core],
        lift_left=[pick(k * z.lev_dev + la) for k in range(z.n_lev)],
        lift_right=[halves(pick(kq).T)],
        lift_mask=[thrice(lift_mask)],
    )
    wide = max(m[0].shape[1] for m in constants.values())
    layout, rows, at = {}, [], 0
    for name, members in constants.items():
        count, columns = members[0].shape
        height = round_up(count, 2 * SUBLANES)
        layout[name] = (at, height, count, columns)
        at += height * len(members)
        rows += [np.pad(m, ((0, height - count), (0, wide - columns))) for m in members]
    return layout, jnp.asarray(np.concatenate(rows), jnp.bfloat16)


def replicated_plan(
    fine_state, fold_pairs, legendre, gauss_weights, grid_coef, modes_from, modes_to, mode_rates
):
    z = Sizes(fine_state, legendre)
    bf, f32 = jnp.bfloat16, jnp.float32
    longitudes = grid_coef.shape[1]
    vmem = pl.BlockSpec(memory_space=pltpu.VMEM)
    hbm = pl.BlockSpec(memory_space=pltpu.HBM)
    shape = jax.ShapeDtypeStruct
    stored = jnp.swapaxes(fine_state, 2, 3)
    block = pl.pallas_call(
        functools.partial(pack_kernel, z),
        out_shape=shape((z.chips, z.block_rows, LANES), bf),
        in_specs=[hbm] * 3,
        out_specs=vmem,
        scratch_shapes=[
            pltpu.VMEM(stored.shape, f32),
            pltpu.VMEM(legendre.shape, bf),
            pltpu.VMEM((1, z.lats), f32),
            pltpu.SemaphoreType.DMA((3,)),
            pltpu.VMEM((z.slots, z.state_rows, z.fine_rows), f32),
        ],
        name="pack",
    )(stored, legendre, gauss_weights[None])
    groups = [[2 * i + c for i in z.order] for c in range(2)]
    own = lax.all_to_all(
        block, ("wave", "lev"), 0, 0, tiled=True, axis_index_groups=groups
    )
    fine_amp, coarse_amp = z.fine_width**-0.5, z.coarse**-0.5
    order = np.arange(2 * z.fine_width).reshape(2, -1)
    order = np.concatenate([order[:, : z.coarse].reshape(-1), order[:, z.coarse :].reshape(-1)])
    basis = wave_rows(z.fine_width, longitudes, fine_amp)[order]
    spread = interpolation(z.points, longitudes, 2 * (z.fine_width - 1))
    spread *= 2.0 * z.fine_width / longitudes
    coarse_spread = interpolation(z.coarse_points, longitudes, 2 * (z.coarse - 1))
    coarse_spread *= 2.0 * z.coarse / (longitudes // 2) * (coarse_amp / fine_amp)
    coarse_spread[1::2] = 0.0
    spread = np.stack(
        [
            np.concatenate([folded(spread, side), folded(coarse_spread, side)], 1)
            for side in (0.5, -0.5)
        ]
    )
    sampled = wave_rows(z.fine_width, z.points, fine_amp)[order].T
    coarse_sampled = wave_rows(z.coarse, z.coarse_points, coarse_amp).T
    basis = basis[:, : longitudes // 2]
    constants = [jnp.asarray(c, bf) for c in (basis, spread, sampled, coarse_sampled)]
    layout, picks = mix_constants(z)
    staged = [fold_pairs[None], mode_rates[None], grid_coef, *constants, modes_from, modes_to, picks]
    wide = 2 * LANES
    narrow_shape, full_shape, quads_shape = [entry[1] for entry in parts(z)]
    narrow, full, quads = pl.pallas_call(
        functools.partial(tables_kernel, z, layout),
        out_shape=(shape(narrow_shape, bf), shape(full_shape, f32), shape(quads_shape, bf)),
        in_specs=[hbm] * len(staged),
        out_specs=(vmem,) * 3,
        scratch_shapes=[
            pltpu.VMEM((2, z.own_levels * 2 * z.fine_width, longitudes // 2), bf),
            pltpu.SemaphoreType.DMA((len(staged),)),
        ]
        + [pltpu.VMEM(array.shape, array.dtype) for array in staged],
        cost_estimate=pl.CostEstimate(flops=10**9, bytes_accessed=4 * 10**6, transcendentals=0),
        name="tables",
    )(*staged)

    partners = [(i, i ^ 1) for i in range(2 * z.chips)]
    other_quads = lax.ppermute(quads, ("wave", "lev"), partners)
    own, narrow = lax.optimization_barrier((own, narrow))
    other = lax.ppermute(own, ("wave", "lev"), partners)

    lat_rows = round_up(z.n_lev * z.lats, LANES)
    corrected, fine_tend = pl.pallas_call(
        functools.partial(sweep_kernel, z),
        out_shape=(
            shape((z.lev_dev, z.nodes - 1, z.slots, 2, z.fine_rows), f32),
            shape(stored.shape, f32),
        ),
        in_specs=[vmem] * 3 + [hbm] * 4,
        out_specs=(vmem, vmem),
        scratch_shapes=[
            pltpu.VMEM((z.n_wave, lat_rows, wide), f32),
            pltpu.VMEM((z.n_wave, z.rows, wide), f32),
            pltpu.VMEM((z.row_pitch * (z.fine_columns + 1), lat_rows), f32),
            pltpu.VMEM(((z.rows + 1) * z.column_pitch, lat_rows), f32),
            pltpu.VMEM((z.n_wave, z.rows + SUBLANES, wide), f32),
            pltpu.VMEM((z.mode_pitch * (z.coarse_columns + 1), lat_rows), f32),
            pltpu.VMEM(((z.coarse_columns + 1) * z.slot_pitch, lat_rows), f32),
            pltpu.VMEM((z.n_wave, z.rows, 2 * LANES), f32),
            pltpu.VMEM(narrow_shape, bf),
            pltpu.VMEM(full_shape, f32),
            pltpu.VMEM(quads_shape, bf),
            pltpu.VMEM(quads_shape, bf),
            pltpu.SemaphoreType.DMA((5,)),
            pltpu.VMEM((z.n_wave, lat_rows, wide), bf),
            pltpu.VMEM((z.levels, z.points, z.nodes * LANES), bf),
            pltpu.VMEM((z.levels, z.coarse_points, LANES), bf),
        ],
        compiler_params=pltpu.CompilerParams(vmem_limit_bytes=VMEM_BYTES),
        name="sweep",
    )(own, other, stored, narrow, full, quads, other_quads)
    return (jnp.swapaxes(corrected, 2, 3), jnp.swapaxes(fine_tend, 2, 3))


def fits_replicated(fine_state, legendre):
    n_wave, n_lev = lax.axis_size("wave"), lax.axis_size("lev")
    if n_lev % 2 or fine_state.shape[1] != len(quad_weights[0]):
        return False
    z = Sizes(fine_state, legendre)
    gathered = 32 * n_wave * n_lev * (legendre.size + fine_state.size)
    return (
        z.head <= LANES
        and z.used > LANES
        and z.used + 2 - LANES <= z.unit
        and z.lats % SUBLANES == 0
        and z.head + z.rest <= LANES
        and n_lev * z.lats <= LANES
        and gathered <= REPLICATED_BYTES
    )


def per_device(fine_state, fold_pairs, legendre, *rest):
    plan = replicated_plan if fits_replicated(fine_state, legendre) else split_plan
    return plan(fine_state, fold_pairs, legendre, *rest)


def solution(mesh):
    placed = (
        P("lev", None, None, "wave", None),
        P(),
        P("wave", "lev", None),
        P("lev"),
        P(),
        P(),
        P(),
        P(),
    )
    return jax.shard_map(
        per_device,
        mesh=mesh,
        in_specs=placed,
        out_specs=(P("lev", None, None, "wave", None), P("lev", None, None, "wave", None)),
        check_vma=False,
    )
```
